32 devices in a mesh: row: 4 (over z), col: 4 (over x, core), dp: 2 (over y).
Axes of the slice: x: 2, y: 2, z: 4, core: 2. Of those that a mesh axis runs over, the one named last changes fastest.
Arguments:
- block_input: bfloat16 [4, 2, 2048, 1024], P(None, 'dp', 'row', 'col'), may hold values from -6 to 6
- segments: int32 [4, 2, 2048], P(None, 'dp', 'row'), may hold values from 0 to 11, never falling along the last dimension, each value on 1 to 1024 neighbouring positions
- decay_rate: float32 [8], P('col'), may hold values from 0 to 1, as said below
- w_query: bfloat16 [1024, 1024], P('row', 'col'), may hold values from -0.1875 to 0.1875
- w_key: bfloat16 [1024, 1024], P('row', 'col'), may hold values from -0.1875 to 0.1875
- w_value: bfloat16 [1024, 1024], P('row', 'col'), may hold values from -0.1875 to 0.1875
- w_output_gate: bfloat16 [1024, 1024], P('row', 'col'), may hold values from -0.1875 to 0.1875
- w_out: bfloat16 [1024, 1024], P('col', 'row'), may hold values from -0.375 to 0.375
- w_gate: bfloat16 [1024, 2816], P('row', 'col'), may hold values from -0.1875 to 0.1875
- w_up: bfloat16 [1024, 2816], P('row', 'col'), may hold values from -0.1875 to 0.1875
- w_down: bfloat16 [2816, 1024], P('col', 'row'), may hold values from -0.109375 to 0.109375
- out_grad: bfloat16 [4, 2, 2048, 1024], P(None, 'dp', 'row', 'col'), may hold values from -6 to 6
Outputs:
- block_output: bfloat16 [4, 2, 2048, 1024], P(None, 'dp', 'row', 'col')
- input_grad: bfloat16 [4, 2, 2048, 1024], P(None, 'dp', 'row', 'col')
- grad_query: float32 [1024, 1024], P(('row', 'dp'), 'col')
- grad_key: float32 [1024, 1024], P(('row', 'dp'), 'col')
- grad_value: float32 [1024, 1024], P(('row', 'dp'), 'col')
- grad_output_gate: float32 [1024, 1024], P(('row', 'dp'), 'col')
- grad_out: float32 [1024, 1024], P('col', ('row', 'dp'))
- grad_gate: float32 [1024, 2816], P(('row', 'dp'), 'col')
- grad_up: float32 [1024, 2816], P(('row', 'dp'), 'col')
- grad_down: float32 [2816, 1024], P('col', ('row', 'dp'))
The draws below stay inside these ranges and needn't reach their ends.
Inputs may be any that keep to these rules, and one draw needn't show every extreme that they name: `segments`: along each sequence the document numbers never fall; a document spans 1 to 1024 tokens, and in every sequence one spans exactly 1024. A head's state is multiplied by exp(-decay_rate[h]) at every token.
All inputs are finite; a program needn't handle non-finite values.
Results may differ from the reference program's by a relative error of at most 0.012.
Values may be sent and summed in bfloat16 or wider, within the bound.
No kernel may reach another device: no remote copies, remote signals or barrier semaphores. Data moves between devices by JAX's collectives and lax.ppermute only.
A program may use at most 192 MiB of HBM per device.

```python
import math
import jax
import jax.numpy as jnp
import numpy as np
from jax import lax

D = 1024
H = 8
HEAD = 128
FF = 2816
TOK_DEV = 512
MICRO = 4
DOCS = 12
LEN = 2048
SEQS = 2


def draw_decay_rate(key, part):
    key_list = jax.random.split(key, 4)
    order_rank = jax.random.permutation(key_list[0], H)
    fast_count = jax.random.randint(key_list[1], (), 2, H // 2 + 2)
    fast_heads = order_rank < fast_count
    fast_rate = jnp.exp(jax.random.uniform(key_list[2], (H,), jnp.float32, math.log(1.0 / 50.0), math.log(1.0 / 30.0)))
    slow_rate = jnp.exp(jax.random.uniform(key_list[3], (H,), jnp.float32, math.log(0.25 / LEN), math.log(2.0 / LEN)))
    return jnp.where(fast_heads, fast_rate, slow_rate).astype(jnp.float32)


def levels(key, dims, cuts, least, high):
    def one(position, shards_of):
        steps = jax.random.uniform(jax.random.fold_in(jax.random.fold_in(key, 6), position), (shards_of,), jnp.float32, least / len(cuts), high / len(cuts))
        return jnp.repeat(jnp.exp(steps), dims[position] // shards_of).reshape((-1,) + (1,) * (len(dims) - position - 1))

    loudness = one(*cuts[0])
    for cut in cuts[1:]:
        loudness = loudness * one(*cut)
    return loudness


def length_profile(amount, total, reach, skew):
    portions = [(1 << 20) // math.isqrt(standing ** skew) + 1 for standing in range(2, amount + 1)]
    spare, counts = total - reach - (amount - 1), [1] * (amount - 1)
    while spare > 0:
        candidates = [i for i in range(amount - 1) if counts[i] < reach]
        mass, remaining = sum([portions[i] for i in candidates]), spare
        for i in candidates:
            addition = min(reach - counts[i], max(1, remaining * portions[i] // mass), spare)
            counts[i] = counts[i] + addition
            spare = spare - addition
    return np.array([reach] + counts)


def uneven_parts(own_key, amount, total, most, slope):
    if amount == 2:
        one = jax.random.randint(own_key, (), max(1, total - most), min(most, total - 1) + 1)
        return jnp.stack([one, total - one])
    lengths = jnp.asarray(length_profile(amount, total, most, slope), jnp.int32)
    pairs = (amount - 1) // 2
    source_of, receiver = lengths[1:1 + 2 * pairs:2], lengths[2:2 + 2 * pairs:2]
    margin = jnp.minimum(source_of - 1, most - receiver)
    shifted = jax.random.randint(jax.random.fold_in(own_key, 1), (pairs,), 0, 1 << 20) % (margin + 1)
    lengths = lengths.at[1:1 + 2 * pairs:2].set(source_of - shifted).at[2:2 + 2 * pairs:2].set(receiver + shifted)
    return lengths[jax.random.permutation(jax.random.fold_in(own_key, 2), amount)]


def gaussian(rng, shape, deviation, reach, cuts=(), held_as=jnp.bfloat16):
    gain = levels(rng, shape, cuts, -0.22, 0.18) if cuts else 1.0
    values = jax.random.normal(rng, shape, jnp.float32) * deviation * gain
    return jnp.minimum(jnp.maximum(values, -reach), reach).astype(held_as)


def setup_inputs(seed: int = 0) -> dict:
    arg_keys = jax.random.split(jax.random.key(seed), 13)
    return {
        "block_input": gaussian(arg_keys[0], (MICRO, SEQS, LEN, D), 1.0, 6.0, ((1, 2), (2, 4), (3, 4))),
        "segments": jax.vmap(lambda own: jnp.searchsorted(jnp.cumsum(uneven_parts(own, DOCS, LEN, LEN // 2, 2)), jnp.arange(LEN), side="right"))(jax.random.split(arg_keys[1], MICRO * SEQS)).reshape((MICRO, SEQS, LEN)).astype(jnp.int32),
        "decay_rate": draw_decay_rate(jax.random.fold_in(arg_keys[12], 71), 0),
        "w_query": gaussian(arg_keys[3], (D, D), D ** -0.5, 0.1875, ((0, 4), (1, 4))),
        "w_key": gaussian(arg_keys[4], (D, D), D ** -0.5, 0.1875, ((0, 4), (1, 4))),
        "w_value": gaussian(arg_keys[5], (D, D), D ** -0.5, 0.1875, ((0, 4), (1, 4))),
        "w_output_gate": gaussian(arg_keys[6], (D, D), D ** -0.5, 0.1875, ((0, 4), (1, 4))),
        "w_out": gaussian(arg_keys[7], (D, D), (D // 4) ** -0.5, 0.375, ((0, 4), (1, 4))),
        "w_gate": gaussian(arg_keys[8], (D, FF), D ** -0.5, 0.1875, ((0, 4), (1, 4))),
        "w_up": gaussian(arg_keys[9], (D, FF), D ** -0.5, 0.1875, ((0, 4), (1, 4))),
        "w_down": gaussian(arg_keys[10], (FF, D), FF ** -0.5, 0.109375, ((0, 4), (1, 4))),
        "out_grad": gaussian(arg_keys[11], (MICRO, SEQS, LEN, D), 1.0, 6.0, ((1, 2), (2, 4), (3, 4))),
    }


@jax.custom_vjp
def low(v):
    return lax.optimization_barrier(v.astype(jnp.bfloat16)).astype(jnp.float32)

@jax.custom_vjp
def low_back(v):
    return v

def low_keep(v):
    return (low(v), None)

def low_pass(kept, grad):
    return (grad,)

def back_keep(v):
    return (v, None)

def back_low(kept, grad):
    return (low(grad),)
low.defvjp(low_keep, low_pass)
low_back.defvjp(back_keep, back_low)
norm_eps = 1e-06
highest = lax.Precision.HIGHEST

def rms_normalize(values):
    return values * lax.rsqrt(lax.optimization_barrier(jnp.mean(values * values, axis=-1, keepdims=True)) + norm_eps)

def matmul_high(left_side, right_side):
    return jnp.dot(left_side, right_side, precision=highest, preferred_element_type=jnp.float32)

def decay_attention(query_seq, key_seq, value_seq, segment_seq, head_rate):
    block_count = LEN // TOK_DEV
    places = jnp.arange(TOK_DEV).astype(jnp.float32)
    offsets = places[:, None] - places[None, :]

    def one_block(carry_in, block_items):
        state_in, prev_segment = carry_in
        query_block, key_block, value_block, segment_block = block_items
        visible = (offsets >= 0.0) & (segment_block[:, None] == segment_block[None, :])
        decay_mask = jnp.where(visible[None], jnp.exp(-head_rate[:, None, None] * jnp.maximum(offsets, 0.0)[None]), 0.0)
        scores = low_back(jnp.einsum('the,she->hts', query_block, key_block, precision=highest))
        mix_weights = low(scores * decay_mask)
        inner_part = jnp.einsum('hts,she->the', mix_weights, value_block, precision=highest)
        entry_scale = (segment_block == prev_segment).astype(jnp.float32)[:, None] * jnp.exp(-head_rate[None, :] * (places[:, None] + 1.0))
        carried = entry_scale[:, :, None] * jnp.einsum('the,hef->thf', query_block, state_in, precision=highest)
        last_segment = segment_block[TOK_DEV - 1]
        own_weight = (segment_block == last_segment).astype(jnp.float32)[:, None] * jnp.exp(-head_rate[None, :] * (TOK_DEV - 1.0 - places)[:, None])
        local_state = jnp.einsum('she,shf->hef', key_block * own_weight[:, :, None], value_block, precision=highest)
        linked = ((segment_block[0] == last_segment) & (prev_segment == last_segment)).astype(jnp.float32)
        state_out = local_state + (linked * jnp.exp(-head_rate * TOK_DEV))[:, None, None] * state_in
        return ((state_out, last_segment), inner_part + carried)
    blocks = (query_seq.reshape(block_count, TOK_DEV, H, HEAD), key_seq.reshape(block_count, TOK_DEV, H, HEAD), value_seq.reshape(block_count, TOK_DEV, H, HEAD), segment_seq.reshape(block_count, TOK_DEV))
    start = (jnp.zeros((H, HEAD, HEAD), jnp.float32), jnp.int32(-1))
    final_carry, mixed_out = lax.scan(jax.checkpoint(one_block), start, blocks)
    return mixed_out.reshape(LEN, H, HEAD)

def layer_forward(rows_in, weight_set, segment_seq, head_rate):
    query_weight, key_weight, value_weight, open_weight, out_weight, gate_weight, up_weight, down_weight = weight_set
    normed_in = low(rms_normalize(rows_in))
    query_seq = low(jax.nn.silu(low_back(matmul_high(normed_in, query_weight)))).reshape(LEN, H, HEAD)
    key_seq = low(jax.nn.silu(low_back(matmul_high(normed_in, key_weight)))).reshape(LEN, H, HEAD)
    value_seq = low(low_back(matmul_high(normed_in, value_weight))).reshape(LEN, H, HEAD)
    gate_open = jax.nn.sigmoid(low_back(matmul_high(normed_in, open_weight)))
    mixed_rows = low_back(decay_attention(query_seq, key_seq, value_seq, segment_seq, head_rate).reshape(LEN, D))
    attended = low(rms_normalize(mixed_rows) * gate_open)
    residual = rows_in + low_back(matmul_high(attended, out_weight))
    normed_mid = low(rms_normalize(residual))
    product = low(low_back(matmul_high(normed_mid, gate_weight)) * low_back(matmul_high(normed_mid, up_weight)))
    return residual + low_back(matmul_high(product, down_weight))

def reference(block_input, segments, decay_rate, w_query, w_key, w_value, w_output_gate, w_out, w_gate, w_up, w_down, out_grad):
    weights_f32 = tuple((weight_arr.astype(jnp.float32) for weight_arr in (w_query, w_key, w_value, w_output_gate, w_out, w_gate, w_up, w_down)))
    sequence_count = MICRO * SEQS
    inputs_f32 = block_input.astype(jnp.float32).reshape(sequence_count, LEN, D)
    cotangents = out_grad.astype(jnp.float32).reshape(sequence_count, LEN, D)
    segment_rows = segments.reshape(sequence_count, LEN)
    zeros_init = tuple((jnp.zeros_like(weight_arr) for weight_arr in weights_f32))

    def per_sequence(running, seq_items):
        seq_rows, seq_cotangent, seq_segment = seq_items

        def forward_rows(rows_in, *weight_list):
            return layer_forward(rows_in, weight_list, seq_segment, decay_rate)
        seq_out, pull_back = jax.vjp(forward_rows, seq_rows, *weights_f32)
        gradients = pull_back(seq_cotangent)
        new_running = tuple((acc_sum + gradient for acc_sum, gradient in zip(running, gradients[1:])))
        return (new_running, (seq_out.astype(jnp.bfloat16), gradients[0].astype(jnp.bfloat16)))
    totals, (outs_seq, grads_seq) = lax.scan(per_sequence, zeros_init, (inputs_f32, cotangents, segment_rows))
    return (outs_seq.reshape(block_input.shape), grads_seq.reshape(block_input.shape), totals[0], totals[1], totals[2], totals[3], totals[4], totals[5], totals[6], totals[7])
```

```python
import jax
import jax.numpy as jnp
from jax import lax
from jax.sharding import PartitionSpec as P

HEAD = 128
EPS = 1e-06
F32 = jnp.float32
BF16 = jnp.bfloat16


def swap(value, bits):
    count = lax.axis_size("col")
    return lax.ppermute(value, "col", [(i, i ^ bits) for i in range(count)])


def pair(value):
    return swap(value, 1)


def side(value):
    return swap(value, 2)


def shift(value, axis, by):
    count = lax.axis_size(axis)
    return lax.ppermute(value, axis, [(i, (i + by) % count) for i in range(count)])


def turned(value, dim, axis):
    count = lax.axis_size(axis)
    place = lax.axis_index(axis)
    back = jnp.flip(value, dim)
    both = jnp.concatenate([back, back], dim)
    return lax.dynamic_slice_in_dim(both, count - 1 - place, count, dim)


def reorder(rows):
    nz, ny = lax.axis_size("row"), lax.axis_size("dp")
    tokens, width = rows.shape
    split = rows.reshape(tokens, nz, ny, width // (nz * ny))
    return turned(turned(split, 1, "row"), 2, "dp").reshape(tokens, width)


def tokens_in(parts):
    col = lax.axis_index("col")
    got = [
        (lambda mine: mine if bits == 0 else swap(mine, bits))(
            lax.dynamic_index_in_dim(parts, col ^ bits, 0, False)
        )
        for bits in range(4)
    ]
    stack = jnp.stack(got)
    rows = [lax.dynamic_index_in_dim(stack, col ^ block, 0, False) for block in range(4)]
    return reorder(jnp.concatenate(rows, 1))


def tokens_out(rows):
    col = lax.axis_index("col")
    tokens, width = rows.shape
    blocks = reorder(rows).reshape(tokens, 4, width // 4)
    got = []
    for bits in range(4):
        mine = lax.dynamic_index_in_dim(blocks, col ^ bits, 1, False)
        got.append(mine if bits == 0 else swap(mine, bits))
    stack = jnp.stack(got)
    return jnp.stack(
        [lax.dynamic_index_in_dim(stack, col ^ micro, 0, False) for micro in range(4)]
    )


AXES = {"z": "row", "y": "dp"}


def gather_weight(shard, route):
    nz, ny = lax.axis_size("row"), lax.axis_size("dp")
    rows, width = shard.shape
    split = shard.reshape(ny, rows // ny, width)
    if "y" in route:
        value = lax.dynamic_index_in_dim(split, lax.axis_index("dp"), 0, False)
        dims = []
    else:
        value = turned(split, 0, "dp")
        dims = ["y"]
    values = [value]
    for step in route:
        if step == "x":
            values = [values[0], side(values[0])]
        else:
            axis = AXES[step]
            count = lax.axis_size(axis)
            values = [
                jnp.stack([v] + [shift(v, axis, k) for k in range(1, count)]) for v in values
            ]
            dims = [step] + dims
    if dims[0] == "y":
        values = [jnp.swapaxes(v, 0, 1) for v in values]
    return [v.reshape(nz * rows, width) for v in values]


def reduce_grad(own, other, route):
    nz, ny = lax.axis_size("row"), lax.axis_size("dp")
    depth, width = own.shape
    values = [v.reshape(nz, ny, depth // (nz * ny), width) for v in (own, other)]
    dims = ["z", "y"]
    for place, step in enumerate(route):
        last = place == len(route) - 1
        if step == "x":
            totals = [values[0].astype(F32) + side(values[1]).astype(F32)]
        else:
            axis = AXES[step]
            dim = dims.index(step)
            dims = dims[:dim] + dims[dim + 1 :]
            totals = []
            for v in values:
                pieces = [lax.index_in_dim(v, k, dim, False) for k in range(v.shape[dim])]
                total = pieces[0].astype(F32)
                for k in range(1, len(pieces)):
                    total = total + shift(pieces[k], axis, -k).astype(F32)
                totals.append(total)
        values = totals if last else [v.astype(BF16) for v in totals]
    return values[0]


def other_first(value):
    return jnp.flip(pair(value), 0)


def dot(left, right, form):
    return jnp.einsum(form, left, right, preferred_element_type=F32)


def silu_slope(pre):
    logistic = jax.nn.sigmoid(pre)
    return logistic * (1.0 + pre * (1.0 - logistic))


def chain(local, factor, reverse):
    count = lax.axis_size("row")
    entry = jnp.zeros_like(local)
    for hop in range(count - 1):
        out = (local + factor[:, :, None, None] * entry).astype(BF16)
        edge = (count - 1 - hop, count - 2 - hop) if reverse else (hop, hop + 1)
        entry = entry + lax.ppermute(out, "row", [edge]).astype(F32)
    return entry


def on_device(
    block_input,
    segments,
    decay_rate,
    w_query,
    w_key,
    w_value,
    w_output_gate,
    w_out,
    w_gate,
    w_up,
    w_down,
    out_grad,
):
    nz = lax.axis_size("row")
    col = lax.axis_index("col")
    place = lax.axis_index("row")
    tokens = block_input.shape[2]
    model = block_input.shape[3] * lax.axis_size("col")
    head_cols = w_query.shape[1]
    hidden = w_gate.shape[1]

    attn_a = gather_weight(jnp.concatenate([w_query, w_key], 1), "zxy")
    attn_b = gather_weight(jnp.concatenate([w_value, w_output_gate], 1), "zyx")
    out_w = gather_weight(w_out.T, "xz")
    gate_w = gather_weight(w_gate, "zxy")
    up_w = gather_weight(w_up, "zyx")
    down_w = gather_weight(w_down.T, "zxy")

    x_own = tokens_in(block_input[:, 0])
    g_own = tokens_in(out_grad[:, 0])
    rates = jnp.concatenate([decay_rate, side(decay_rate)])
    seg_all = segments[:, 0].astype(F32)
    seg = jnp.stack(
        [
            lax.dynamic_index_in_dim(seg_all, col, 0, False),
            lax.dynamic_index_in_dim(seg_all, col ^ 1, 0, False),
        ]
    )
    last = seg[:, tokens - 1]
    entry_seg = jnp.where(
        place == 0,
        -1.0,
        lax.ppermute(last, "row", [(i, i + 1) for i in range(nz - 1)]),
    )
    g_pair = jnp.stack([g_own, pair(g_own)]).reshape(2 * tokens, model)

    heads = rates.shape[0]
    places = jnp.arange(tokens).astype(F32)
    gaps = places[:, None] - places[None, :]
    visible = (gaps >= 0.0) & (seg[:, :, None] == seg[:, None, :])
    decay = jnp.where(
        visible[:, None],
        jnp.exp(-rates[:, None, None] * jnp.maximum(gaps, 0.0))[None],
        0.0,
    )
    own_weight = (seg == last[:, None]).astype(F32)[:, None, :] * jnp.exp(
        -rates[:, None] * (tokens - 1.0 - places)
    )
    entry_scale = (seg == entry_seg[:, None]).astype(F32)[:, None, :] * jnp.exp(
        -rates[:, None] * (places + 1.0)
    )
    linked = ((seg[:, 0] == last) & (entry_seg == last)).astype(F32)
    factor = linked[:, None] * jnp.exp(-rates * tokens)[None]

    x_wide = x_own.astype(F32)
    r1 = lax.rsqrt(jnp.mean(x_wide * x_wide, 1, keepdims=True) + EPS)
    a_own = (x_wide * r1).astype(BF16)
    a_pair = jnp.concatenate([a_own, pair(a_own)], 0)
    za = [dot(a_pair, w, "td,dc->tc") for w in attn_a]
    zb = [dot(a_pair, w, "td,dc->tc") for w in attn_b]
    zq = jnp.concatenate([z[:, :head_cols] for z in za], 1)
    zk = jnp.concatenate([z[:, head_cols:] for z in za], 1)
    zv = jnp.concatenate([z[:, :head_cols] for z in zb], 1)
    zu = jnp.concatenate([z[:, head_cols:] for z in zb], 1)

    def by_head(rows):
        return rows.reshape(2, tokens, heads, HEAD).transpose(0, 2, 1, 3)

    def by_row(value):
        return value.transpose(0, 2, 1, 3).reshape(2 * tokens, heads * HEAD)

    q = by_head(jax.nn.silu(zq).astype(BF16))
    k = by_head(jax.nn.silu(zk).astype(BF16))
    v = by_head(zv.astype(BF16))
    gate = jax.nn.sigmoid(zu)
    k_state = (k.astype(F32) * own_weight[..., None]).astype(BF16)
    local = dot(k_state, v, "bhse,bhsf->bhef")
    entry = chain(local, factor, False).astype(BF16)
    scores = dot(q, k, "bhte,bhse->bhts")
    mix = (scores * decay).astype(BF16)
    o = dot(mix, v, "bhts,bhsf->bhtf") + entry_scale[..., None] * dot(
        q, entry, "bhte,bhef->bhtf"
    )
    o = by_row(o)
    squares = jnp.sum(o * o, 1).reshape(2, tokens)
    squares = (squares + other_first(squares)).reshape(2 * tokens, 1)
    r2 = lax.rsqrt(squares / model + EPS)
    normed = o * r2
    y = (normed * gate).astype(BF16)
    y_x = [y[:, : y.shape[1] // 2], y[:, y.shape[1] // 2 :]]

    def back_sum(parts):
        total = parts.reshape(2, tokens, model)
        return total[0] + pair(total[1].astype(BF16)).astype(F32)

    h_part = dot(y_x[0], out_w[0], "tc,dc->td") + dot(y_x[1], out_w[1], "tc,dc->td")
    hres = x_wide + back_sum(h_part)
    r3 = lax.rsqrt(jnp.mean(hres * hres, 1, keepdims=True) + EPS)
    b_own = (hres * r3).astype(BF16)
    b_pair = jnp.concatenate([b_own, pair(b_own)], 0)
    z1 = [dot(b_pair, w, "td,df->tf") for w in gate_w]
    z2 = [dot(b_pair, w, "td,df->tf") for w in up_w]
    m = [(p * s).astype(BF16) for p, s in zip(z1, z2)]
    out_part = dot(m[0], down_w[0], "tf,df->td") + dot(m[1], down_w[1], "tf,df->td")
    block_out = tokens_out((hres + back_sum(out_part)).astype(BF16))

    grad_down = [dot(g_pair, p, "td,tf->df").astype(BF16) for p in m]
    dm = [dot(g_pair, w, "td,df->tf") for w in down_w]
    dz1 = [(d * s).astype(BF16) for d, s in zip(dm, z2)]
    dz2 = [(d * p).astype(BF16) for d, p in zip(dm, z1)]
    grad_gate = [dot(b_pair, d, "td,tf->df").astype(BF16) for d in dz1]
    grad_up = [dot(b_pair, d, "td,tf->df").astype(BF16) for d in dz2]
    db_part = (
        dot(dz1[0], gate_w[0], "tf,df->td")
        + dot(dz1[1], gate_w[1], "tf,df->td")
        + dot(dz2[0], up_w[0], "tf,df->td")
        + dot(dz2[1], up_w[1], "tf,df->td")
    )
    db = back_sum(db_part)
    dh = (
        g_own.astype(F32)
        + r3 * db
        - hres * (r3**3 * jnp.mean(db * hres, 1, keepdims=True))
    )
    dhr_own = dh.astype(BF16)
    dhr = jnp.concatenate([dhr_own, pair(dhr_own)], 0)

    grad_out = [dot(dhr, p, "td,tc->dc").astype(BF16) for p in y_x]
    dy = jnp.concatenate([dot(dhr, w, "td,dc->tc") for w in out_w], 1)
    dn = dy * gate
    dzu = (dy * normed * gate * (1.0 - gate)).astype(BF16)
    dots = jnp.sum(dn * o, 1).reshape(2, tokens)
    dots = (dots + other_first(dots)).reshape(2 * tokens, 1)
    do = by_head((r2 * dn - o * (r2**3 * dots / model)).astype(BF16))
    do_scaled = (do.astype(F32) * entry_scale[..., None]).astype(BF16)
    d_entry = dot(q, do_scaled, "bhte,bhtf->bhef")
    d_local = chain(d_entry, factor, True).astype(BF16)
    ds = (dot(do, v, "bhtf,bhsf->bhts") * decay).astype(BF16)
    dq = dot(ds, k, "bhts,bhse->bhte") + dot(do_scaled, entry, "bhtf,bhef->bhte")
    dk = dot(ds, q, "bhts,bhte->bhse") + own_weight[..., None] * dot(
        v, d_local, "bhsf,bhef->bhse"
    )
    dv = dot(mix, do, "bhts,bhtf->bhsf") + dot(k_state, d_local, "bhse,bhef->bhsf")
    dzq = (by_row(dq) * silu_slope(zq)).astype(BF16)
    dzk = (by_row(dk) * silu_slope(zk)).astype(BF16)
    dzv = by_row(dv).astype(BF16)

    def halves(value):
        return value[:, :head_cols], value[:, head_cols:]

    dza = [jnp.concatenate(p, 1) for p in zip(halves(dzq), halves(dzk))]
    dzb = [jnp.concatenate(p, 1) for p in zip(halves(dzv), halves(dzu))]
    grad_a = [dot(a_pair, d, "td,tc->dc").astype(BF16) for d in dza]
    grad_b = [dot(a_pair, d, "td,tc->dc").astype(BF16) for d in dzb]
    da_part = (
        dot(dza[0], attn_a[0], "tc,dc->td")
        + dot(dza[1], attn_a[1], "tc,dc->td")
        + dot(dzb[0], attn_b[0], "tc,dc->td")
        + dot(dzb[1], attn_b[1], "tc,dc->td")
    )
    da = back_sum(da_part)
    input_grad = tokens_out(
        (
            dh + r1 * da - x_wide * (r1**3 * jnp.mean(da * x_wide, 1, keepdims=True))
        ).astype(BF16)
    )

    total_down = reduce_grad(*grad_down, "xyz")
    total_gate = reduce_grad(*grad_gate, "yxz")
    total_up = reduce_grad(*grad_up, "xzy")
    total_out = reduce_grad(*grad_out, "yzx")
    total_a = reduce_grad(*grad_a, "xyz")
    total_b = reduce_grad(*grad_b, "yxz")
    return (
        block_out[:, None],
        input_grad[:, None],
        total_a[:, :head_cols],
        total_a[:, head_cols:],
        total_b[:, :head_cols],
        total_b[:, head_cols:],
        total_out.T,
        total_gate,
        total_up,
        total_down.T,
    )


def solution(mesh):
    placed = (
        P(None, "dp", "row", "col"),
        P(None, "dp", "row"),
        P("col"),
        P("row", "col"),
        P("row", "col"),
        P("row", "col"),
        P("row", "col"),
        P("col", "row"),
        P("row", "col"),
        P("row", "col"),
        P("col", "row"),
        P(None, "dp", "row", "col"),
    )
    return jax.shard_map(
        on_device,
        mesh=mesh,
        in_specs=placed,
        out_specs=(
            P(None, "dp", "row", "col"),
            P(None, "dp", "row", "col"),
            P(("row", "dp"), "col"),
            P(("row", "dp"), "col"),
            P(("row", "dp"), "col"),
            P(("row", "dp"), "col"),
            P("col", ("row", "dp")),
            P(("row", "dp"), "col"),
            P(("row", "dp"), "col"),
            P("col", ("row", "dp")),
        ),
        check_vma=False,
    )
```

```python
import functools

import jax
import jax.numpy as jnp
from jax import lax
from jax.experimental import pallas as pl
from jax.experimental.pallas import tpu as pltpu
from jax.sharding import PartitionSpec as P

HEAD = 128
TILE = 256
EPS = 1e-06
F32 = jnp.float32
BF16 = jnp.bfloat16


def swap(value, axis, bits):
    count = lax.axis_size(axis)
    return lax.ppermute(value, axis, [(i, i ^ bits) for i in range(count)])


def pair(value):
    return swap(value, "col", 1)


def side(value):
    return swap(value, "col", 2)


def bits_of(axis):
    return [1 << b for b in range(lax.axis_size(axis).bit_length() - 1)]


def xor_turn(value, dim, place, count):
    bit = 1
    while bit < count:
        shape = value.shape
        split = value.reshape(shape[:dim] + (count // (2 * bit), 2, bit) + shape[dim + 1 :])
        flipped = jnp.flip(split, dim + 1)
        value = jnp.where((place & bit) != 0, flipped, split).reshape(shape)
        bit *= 2
    return value


def to_order(rows):
    nz, ny = lax.axis_size("row"), lax.axis_size("dp")
    tokens, width = rows.shape
    split = rows.reshape(tokens, nz, ny, width // (nz * ny))
    split = xor_turn(split, 1, lax.axis_index("row"), nz)
    split = xor_turn(split, 2, lax.axis_index("dp"), ny)
    return split.transpose(0, 2, 1, 3).reshape(tokens, width)


def from_order(rows):
    nz, ny = lax.axis_size("row"), lax.axis_size("dp")
    tokens, width = rows.shape
    split = rows.reshape(tokens, ny, nz, width // (nz * ny)).transpose(0, 2, 1, 3)
    split = xor_turn(split, 1, lax.axis_index("row"), nz)
    split = xor_turn(split, 2, lax.axis_index("dp"), ny)
    return split.reshape(tokens, width)


def small_slice():
    return lax.axis_size("row") == 4 and lax.axis_size("dp") == 2


def place_bits():
    turn = lax.axis_index("col") ^ lax.axis_index("row")
    return jnp.stack([turn & 1, turn >> 1, lax.axis_index("dp"), 0]).astype(jnp.int32)


def pick4(parts, low, high):
    first = [jnp.where(low, parts[k ^ 1], parts[k]) for k in range(4)]
    return [jnp.where(high, first[k ^ 2], first[k]) for k in range(4)]


def assemble_kernel(norm, bits, *refs):
    parts = [r[...].astype(F32) for r in refs[:4]]
    blocks = pick4(parts, bits[0] != 0, bits[1] != 0)
    odd = bits[2] != 0
    halves = [[], []]
    for b in blocks:
        low, high = b[:, :HEAD], b[:, HEAD:]
        halves[0].append(jnp.where(odd, high, low))
        halves[1].append(jnp.where(odd, low, high))
    rows = jnp.concatenate(halves[0] + halves[1], 1)
    refs[4][...] = rows.astype(BF16)
    if norm:
        scale = lax.rsqrt(jnp.mean(rows * rows, 1, keepdims=True) + EPS)
        refs[5][...] = (rows * scale).astype(BF16)
        refs[6][...] = scale


def assemble(parts, norm):
    tokens, width = parts[0].shape
    model = 4 * width
    if not small_slice():
        col = lax.axis_index("col")
        blocks = pick4(parts, (col & 1) != 0, (col & 2) != 0)
        rows = to_order(jnp.concatenate(blocks, 1))
        if not norm:
            return rows
        wide = rows.astype(F32)
        scale = lax.rsqrt(jnp.mean(wide * wide, 1, keepdims=True) + EPS)
        return rows, (wide * scale).astype(BF16), scale
    step = 128
    row = lambda n: pl.BlockSpec((step, n), lambda i: (i, 0))
    shape = [jax.ShapeDtypeStruct((tokens, model), BF16)]
    specs = [row(model)]
    if norm:
        shape += [shape[0], jax.ShapeDtypeStruct((tokens, 1), F32)]
        specs += [row(model), row(1)]
    out = pl.pallas_call(
        functools.partial(assemble_kernel, norm),
        grid=(tokens // step,),
        in_specs=[pl.BlockSpec(memory_space=pltpu.SMEM)] + [row(width)] * 4,
        out_specs=specs,
        out_shape=shape,
        name="assemble",
    )(place_bits(), *parts)
    return out if norm else out[0]


def divide_kernel(bits, rows_ref, *refs):
    rows = rows_ref[...].astype(F32)
    odd = bits[2] != 0
    blocks = []
    for k in range(4):
        low = rows[:, k * HEAD : (k + 1) * HEAD]
        high = rows[:, (4 + k) * HEAD : (5 + k) * HEAD]
        blocks.append(
            jnp.concatenate([jnp.where(odd, high, low), jnp.where(odd, low, high)], 1)
        )
    for ref, block in zip(refs, pick4(blocks, bits[0] != 0, bits[1] != 0)):
        ref[...] = block.astype(BF16)


def divide(rows):
    tokens, model = rows.shape
    width = model // 4
    if not small_slice():
        col = lax.axis_index("col")
        whole = from_order(rows)
        blocks = [whole[:, k * width : (k + 1) * width] for k in range(4)]
        return pick4(blocks, (col & 1) != 0, (col & 2) != 0)
    step = 128
    row = lambda n: pl.BlockSpec((step, n), lambda i: (i, 0))
    return pl.pallas_call(
        divide_kernel,
        grid=(tokens // step,),
        in_specs=[pl.BlockSpec(memory_space=pltpu.SMEM), row(model)],
        out_specs=[row(width)] * 4,
        out_shape=[jax.ShapeDtypeStruct((tokens, width), BF16)] * 4,
        name="divide",
    )(place_bits(), rows)


def tokens_in(parts, norm):
    col = lax.axis_index("col")
    got = []
    for bits in range(4):
        mine = lax.dynamic_index_in_dim(parts, col ^ bits, 0, False)
        got.append(mine if bits == 0 else swap(mine, "col", bits))
    return assemble(got, norm)


def tokens_out(rows):
    col = lax.axis_index("col")
    parts = divide(rows)
    got = [parts[0]] + [swap(parts[bits], "col", bits) for bits in range(1, 4)]
    return jnp.stack(pick4(got, (col & 1) != 0, (col & 2) != 0))


def gather_weight(shard, order):
    ny = lax.axis_size("dp")
    rows, width = shard.shape
    part = rows // ny
    start = lax.axis_index("dp") * part
    value = lax.dynamic_slice_in_dim(shard, start, part, 0)
    for bit in bits_of("row"):
        value = jnp.concatenate([value, swap(value, "row", bit)], 0)
    if order == "yx":
        for bit in bits_of("dp"):
            value = jnp.concatenate([value, swap(value, "dp", bit)], 0)
        return [value, side(value)]
    values = [value, side(value)]
    for bit in bits_of("dp"):
        values = [jnp.concatenate([v, swap(v, "dp", bit)], 0) for v in values]
    return values


def fold(value, axis):
    for bit in reversed(bits_of(axis)):
        half = value.shape[0] // 2
        got = swap(value[half:].astype(BF16), axis, bit)
        value = value[:half].astype(F32) + got.astype(F32)
    return value


def reduce_grad(own, other, order):
    if order == "xy":
        value = own.astype(F32) + side(other).astype(F32)
        value = fold(value, "dp")
    else:
        own, other = fold(own, "dp"), fold(other, "dp")
        value = own + side(other.astype(BF16)).astype(F32)
    return fold(value, "row")


def dot(left, right, form):
    return jnp.einsum(form, left, right, preferred_element_type=F32)


def nn(a, b):
    return jnp.dot(a, b, preferred_element_type=F32)


def nt(a, b):
    return lax.dot_general(a, b, (((1,), (1,)), ((), ())), preferred_element_type=F32)


def tn(a, b):
    return lax.dot_general(a, b, (((0,), (0,)), ((), ())), preferred_element_type=F32)


def silu_slope(pre):
    logistic = jax.nn.sigmoid(pre)
    return logistic * (1.0 + pre * (1.0 - logistic))


def tile_decay(rate, seg_col, seg_row, at, width):
    rows = seg_col.shape[0]
    shape = (rows, width)
    gap = lax.broadcasted_iota(jnp.int32, shape, 0) + at - lax.broadcasted_iota(jnp.int32, shape, 1)
    visible = (gap >= 0) & (seg_col == seg_row)
    return jnp.where(visible, jnp.exp(-rate * jnp.maximum(gap, 0).astype(F32)), 0.0)


def column(tokens):
    return lax.broadcasted_iota(jnp.int32, (tokens, 1), 0).astype(F32)


def own_weight(rate, seg_col, last):
    tokens = seg_col.shape[0]
    return jnp.where(seg_col == last, jnp.exp(-rate * (tokens - 1.0 - column(tokens))), 0.0)


def entry_weight(rate, seg_col, entry_seg):
    tokens = seg_col.shape[0]
    return jnp.where(seg_col == entry_seg, jnp.exp(-rate * (column(tokens) + 1.0)), 0.0)


def first_kernel(rates, marks, seg_c, seg_r, zq, zk, zv, q_out, k_out, v_out, o_out, state):
    block, head = pl.program_id(0), pl.program_id(1)
    rate = rates[head]
    pre_q, pre_k = zq[...], zk[...]
    q = (pre_q * jax.nn.sigmoid(pre_q)).astype(BF16)
    k_wide = pre_k * jax.nn.sigmoid(pre_k)
    k = k_wide.astype(BF16)
    v = zv[...].astype(BF16)
    q_out[...], k_out[...], v_out[...] = q, k, v
    seg = seg_c[0]
    weight = own_weight(rate, seg, marks[block, 0])
    state[0, 0] = tn((k.astype(F32) * weight).astype(BF16), v)
    tokens = q.shape[0]
    for at in range(0, tokens, TILE):
        width = at + TILE
        decay = tile_decay(rate, seg[at:width], seg_r[0, :, :width], at, width)
        mix = (nt(q[at:width], k[:width]) * decay).astype(BF16)
        o_out[at:width, :] = nn(mix, v[:width])


def carry_kernel(rates, marks, seg_c, o_in, q, entry, o_out, squares):
    block, head = pl.program_id(0), pl.program_id(1)
    weight = entry_weight(rates[head], seg_c[0], marks[block, 1])
    o = o_in[...] + weight * nn(q[...], entry[0, 0])
    o_out[...] = o

    @pl.when(head == 0)
    def _():
        squares[...] = jnp.zeros_like(squares)

    squares[...] += jnp.sum(o * o, 1, keepdims=True)


def entry_grad_kernel(rates, marks, seg_c, q, do, grad):
    block, head = pl.program_id(0), pl.program_id(1)
    weight = entry_weight(rates[head], seg_c[0], marks[block, 1])
    grad[0, 0] = tn(q[...], (do[...].astype(F32) * weight).astype(BF16))


def inner_grad_kernel(
    rates, marks, seg_c, seg_r, q_ref, k_ref, v_ref, do_ref, entry, zq, dzq, dk, dv
):
    block, head = pl.program_id(0), pl.program_id(1)
    rate = rates[head]
    seg = seg_c[0]
    weight = entry_weight(rate, seg, marks[block, 1])
    tokens = seg.shape[0]
    for at in range(0, tokens, TILE):
        width = at + TILE
        q, do = q_ref[at:width, :], do_ref[at:width, :]
        k, v = k_ref[:width, :], v_ref[:width, :]
        decay = tile_decay(rate, seg[at:width], seg_r[0, :, :width], at, width)
        mix = (nt(q, k) * decay).astype(BF16)
        ds = (nt(do, v) * decay).astype(BF16)
        scaled = (do.astype(F32) * weight[at:width]).astype(BF16)
        dq = nn(ds, k) + nt(scaled, entry[0, 0])
        dzq[at:width, :] = (dq * silu_slope(zq[at:width, :])).astype(BF16)
        dk_new, dv_new = tn(ds, q), tn(mix, do)
        if at:
            dk[:at, :] += dk_new[:at]
            dv[:at, :] += dv_new[:at]
        dk[at:width, :] = dk_new[at:]
        dv[at:width, :] = dv_new[at:]


def last_grad_kernel(rates, marks, seg_c, k, v, d_state, zk, dk, dv, dzk, dzv):
    block, head = pl.program_id(0), pl.program_id(1)
    weight = own_weight(rates[head], seg_c[0], marks[block, 0])
    state = d_state[0, 0]
    dk_all = dk[...] + weight * nt(v[...], state)
    dzk[...] = (dk_all * silu_slope(zk[...])).astype(BF16)
    scaled = (k[...].astype(F32) * weight).astype(BF16)
    dzv[...] = (dv[...] + nn(scaled, state)).astype(BF16)


def head_call(kernel, tokens, heads, kinds_in, kinds_out, args, flops, name):
    specs = {
        "s": pl.BlockSpec(memory_space=pltpu.SMEM),
        "c": pl.BlockSpec((1, tokens, 1), lambda b, h: (b, 0, 0)),
        "r": pl.BlockSpec((1, 1, tokens), lambda b, h: (b, 0, 0)),
        "t": pl.BlockSpec((tokens, HEAD), lambda b, h: (b, h)),
        "p": pl.BlockSpec((1, 1, HEAD, HEAD), lambda b, h: (b, h, 0, 0)),
        "n": pl.BlockSpec((tokens, 1), lambda b, h: (b, 0)),
    }
    shapes = {
        "T": jax.ShapeDtypeStruct((2 * tokens, heads * HEAD), F32),
        "t": jax.ShapeDtypeStruct((2 * tokens, heads * HEAD), BF16),
        "p": jax.ShapeDtypeStruct((2, heads, HEAD, HEAD), F32),
        "n": jax.ShapeDtypeStruct((2 * tokens, 1), F32),
    }
    return pl.pallas_call(
        kernel,
        grid=(2, heads),
        in_specs=[specs[k.lower()] for k in kinds_in],
        out_specs=[specs[k.lower()] for k in kinds_out],
        out_shape=[shapes[k] for k in kinds_out],
        cost_estimate=pl.CostEstimate(flops=flops, bytes_accessed=8 << 20, transcendentals=0),
        name=name,
    )(*args)


def chain(local, factor, reverse):
    count = lax.axis_size("row")
    entry = jnp.zeros(local.shape, BF16)
    for hop in range(count - 1):
        out = (local + factor[:, :, None, None] * entry.astype(F32)).astype(BF16)
        edge = (count - 1 - hop, count - 2 - hop) if reverse else (hop, hop + 1)
        entry = entry + lax.ppermute(out, "row", [edge])
    return entry


def other_first(value):
    return jnp.flip(pair(value), 0)


def on_device(
    block_input,
    segments,
    decay_rate,
    w_query,
    w_key,
    w_value,
    w_output_gate,
    w_out,
    w_gate,
    w_up,
    w_down,
    out_grad,
):
    nz = lax.axis_size("row")
    col = lax.axis_index("col")
    place = lax.axis_index("row")
    tokens = block_input.shape[2]
    model = block_input.shape[3] * lax.axis_size("col")
    wide = w_query.shape[1]

    parts = gather_weight(jnp.concatenate([w_query, w_key], 1), "xy")
    wq = jnp.concatenate([w[:, :wide] for w in parts], 1)
    wk = jnp.concatenate([w[:, wide:] for w in parts], 1)
    parts = gather_weight(jnp.concatenate([w_value, w_output_gate], 1), "yx")
    wv = jnp.concatenate([w[:, :wide] for w in parts], 1)
    wu = jnp.concatenate([w[:, wide:] for w in parts], 1)
    wo = jnp.concatenate(gather_weight(w_out.T, "xy"), 1)
    down_w = gather_weight(w_down.T, "xy")
    gate_w = gather_weight(w_gate, "yx")
    up_w = gather_weight(w_up, "xy")

    x_own, a_own, r1 = tokens_in(block_input[:, 0], True)
    g_own = tokens_in(out_grad[:, 0], False)
    rates = jnp.concatenate([decay_rate, side(decay_rate)])
    heads = rates.shape[0]
    seg_all = segments[:, 0].astype(F32)
    seg = jnp.stack(
        [
            lax.dynamic_index_in_dim(seg_all, col, 0, False),
            lax.dynamic_index_in_dim(seg_all, col ^ 1, 0, False),
        ]
    )
    last = seg[:, tokens - 1]
    before = lax.ppermute(last, "row", [(i, i + 1) for i in range(nz - 1)])
    entry_seg = jnp.where(place == 0, -1.0, before)
    linked = ((seg[:, 0] == last) & (entry_seg == last)).astype(F32)
    factor = linked[:, None] * jnp.exp(-rates * tokens)[None]
    marks = jnp.stack([last, entry_seg], 1)
    seg_c, seg_r = seg[:, :, None], seg[:, None, :]
    heads_of = functools.partial(head_call, tokens=tokens, heads=heads)
    unit = 2 * heads * 2 * tokens * tokens * HEAD

    def both(own):
        return jnp.concatenate([own, pair(own)], 0)

    def back_sum(lefts, rights, form):
        def total(rows):
            out = dot(lefts[0][rows], rights[0], form)
            for left, right in zip(lefts[1:], rights[1:]):
                out = out + dot(left[rows], right, form)
            return out

        sent = pair(total(slice(tokens, None)).astype(BF16))
        return total(slice(0, tokens)) + sent.astype(F32)

    a = both(a_own)
    g = both(g_own)
    zq, zk, zv, zu = [dot(a, w, "td,dc->tc") for w in (wq, wk, wv, wu)]
    q, k, v, o_inner, local = heads_of(
        first_kernel,
        kinds_in="sscrTTT",
        kinds_out="tttTp",
        args=(rates, marks, seg_c, seg_r, zq, zk, zv),
        flops=unit,
        name="mixer_first",
    )
    entry = chain(local, factor, False)
    o, squares = heads_of(
        carry_kernel,
        kinds_in="sscTtp",
        kinds_out="Tn",
        args=(rates, marks, seg_c, o_inner, q, entry),
        flops=unit // 8,
        name="mixer_carry",
    )
    gate = jax.nn.sigmoid(zu)
    squares = squares.reshape(2, tokens)
    squares = (squares + other_first(squares)).reshape(2 * tokens, 1)
    r2 = lax.rsqrt(squares / model + EPS)
    y = (o * r2 * gate).astype(BF16)
    hres = x_own.astype(F32) + back_sum((y,), (wo,), "tc,dc->td")
    r3 = lax.rsqrt(jnp.mean(hres * hres, 1, keepdims=True) + EPS)
    b = both((hres * r3).astype(BF16))
    z1 = [dot(b, w, "td,df->tf") for w in gate_w]
    z2 = [dot(b, w, "td,df->tf") for w in up_w]
    m = [(p * s).astype(BF16) for p, s in zip(z1, z2)]
    block_out = tokens_out((hres + back_sum(m, down_w, "tf,df->td")).astype(BF16))

    grad_down = [dot(g, p, "td,tf->df").astype(BF16) for p in m]
    dm = [dot(g, w, "td,df->tf") for w in down_w]
    dz1 = [(d * s).astype(BF16) for d, s in zip(dm, z2)]
    dz2 = [(d * p).astype(BF16) for d, p in zip(dm, z1)]
    grad_gate = [dot(b, d, "td,tf->df").astype(BF16) for d in dz1]
    grad_up = [dot(b, d, "td,tf->df").astype(BF16) for d in dz2]
    db = back_sum(dz1 + dz2, gate_w + up_w, "tf,df->td")
    dh = (
        g_own.astype(F32)
        + r3 * db
        - hres * (r3**3 * jnp.mean(db * hres, 1, keepdims=True))
    )
    dhr = both(dh.astype(BF16))

    grad_out = dot(dhr, y, "td,tc->dc").astype(BF16)
    dy = dot(dhr, wo, "td,dc->tc")
    dn = dy * gate
    dzu = (dy * o * r2 * gate * (1.0 - gate)).astype(BF16)
    dots = jnp.sum(dn * o, 1).reshape(2, tokens)
    dots = (dots + other_first(dots)).reshape(2 * tokens, 1)
    do = (r2 * dn - o * (r2**3 * dots / model)).astype(BF16)
    (d_entry,) = heads_of(
        entry_grad_kernel,
        kinds_in="ssctt",
        kinds_out="p",
        args=(rates, marks, seg_c, q, do),
        flops=unit // 8,
        name="mixer_entry_grad",
    )
    d_local = chain(d_entry, factor, True)
    dzq, dk, dv = heads_of(
        inner_grad_kernel,
        kinds_in="sscrttttpT",
        kinds_out="tTT",
        args=(rates, marks, seg_c, seg_r, q, k, v, do, entry, zq),
        flops=5 * unit // 2,
        name="mixer_inner_grad",
    )
    dzk, dzv = heads_of(
        last_grad_kernel,
        kinds_in="sscttpTTT",
        kinds_out="tt",
        args=(rates, marks, seg_c, k, v, d_local, zk, dk, dv),
        flops=unit // 4,
        name="mixer_last_grad",
    )
    grads = [dot(a, d, "td,tc->dc").astype(BF16) for d in (dzq, dzk, dzv, dzu)]
    da = back_sum((dzq, dzk, dzv, dzu), (wq, wk, wv, wu), "tc,dc->td")
    x_wide = x_own.astype(F32)
    input_grad = tokens_out(
        (
            dh + r1 * da - x_wide * (r1**3 * jnp.mean(da * x_wide, 1, keepdims=True))
        ).astype(BF16)
    )

    def halves(*mats):
        return [
            jnp.concatenate([g[:, at : at + wide] for g in mats], 1) for at in (0, wide)
        ]

    total_down = reduce_grad(*grad_down, "xy")
    total_gate = reduce_grad(*grad_gate, "yx")
    total_up = reduce_grad(*grad_up, "xy")
    total_ou = reduce_grad(*halves(grad_out, grads[3]), "yx")
    total_qk = reduce_grad(*halves(grads[0], grads[1]), "xy")
    total_v = reduce_grad(*halves(grads[2]), "yx")
    return (
        block_out[:, None],
        input_grad[:, None],
        total_qk[:, :wide],
        total_qk[:, wide:],
        total_v,
        total_ou[:, wide:],
        total_ou[:, :wide].T,
        total_gate,
        total_up,
        total_down.T,
    )


def solution(mesh):
    placed = (
        P(None, "dp", "row", "col"),
        P(None, "dp", "row"),
        P("col"),
        P("row", "col"),
        P("row", "col"),
        P("row", "col"),
        P("row", "col"),
        P("col", "row"),
        P("row", "col"),
        P("row", "col"),
        P("col", "row"),
        P(None, "dp", "row", "col"),
    )
    return jax.shard_map(
        on_device,
        mesh=mesh,
        in_specs=placed,
        out_specs=(
            P(None, "dp", "row", "col"),
            P(None, "dp", "row", "col"),
            P(("row", "dp"), "col"),
            P(("row", "dp"), "col"),
            P(("row", "dp"), "col"),
            P(("row", "dp"), "col"),
            P("col", ("row", "dp")),
            P(("row", "dp"), "col"),
            P(("row", "dp"), "col"),
            P("col", ("row", "dp")),
        ),
        check_vma=False,
    )
```

```python
import functools

import jax
import jax.numpy as jnp
from jax import lax
from jax.experimental import pallas as pl
from jax.experimental.pallas import tpu as pltpu
from jax.sharding import PartitionSpec as P

HEAD = 128
TILE = 256
EPS = 1e-06
F32 = jnp.float32
BF16 = jnp.bfloat16


COL = ("cx", "cc")
CHIPS = ("cx", "row", "dp")


def swap(value, axis, bits):
    count = lax.axis_size(axis)
    return lax.ppermute(value, axis, [(i, i ^ bits) for i in range(count)])


def pair(value):
    return swap(value, COL, 1)


def side(value):
    return swap(value, COL, 2)


def bits_of(axis):
    return [1 << b for b in range(lax.axis_size(axis).bit_length() - 1)]


def xor_turn(value, dim, place, count):
    bit = 1
    while bit < count:
        shape = value.shape
        split = value.reshape(shape[:dim] + (count // (2 * bit), 2, bit) + shape[dim + 1 :])
        flipped = jnp.flip(split, dim + 1)
        value = jnp.where((place & bit) != 0, flipped, split).reshape(shape)
        bit *= 2
    return value


def to_order(rows):
    nz, ny = lax.axis_size("row"), lax.axis_size("dp")
    tokens, width = rows.shape
    split = rows.reshape(tokens, nz, ny, width // (nz * ny))
    split = xor_turn(split, 1, lax.axis_index("row"), nz)
    split = xor_turn(split, 2, lax.axis_index("dp"), ny)
    return split.transpose(0, 2, 1, 3).reshape(tokens, width)


def from_order(rows):
    nz, ny = lax.axis_size("row"), lax.axis_size("dp")
    tokens, width = rows.shape
    split = rows.reshape(tokens, ny, nz, width // (nz * ny)).transpose(0, 2, 1, 3)
    split = xor_turn(split, 1, lax.axis_index("row"), nz)
    split = xor_turn(split, 2, lax.axis_index("dp"), ny)
    return split.reshape(tokens, width)


def small_slice():
    return lax.axis_size("row") == 4 and lax.axis_size("dp") == 2


def place_bits():
    turn = lax.axis_index(COL) ^ lax.axis_index("row")
    return jnp.stack([turn & 1, turn >> 1, lax.axis_index("dp"), 0]).astype(jnp.int32)


def pick4(parts, low, high):
    first = [jnp.where(low, parts[k ^ 1], parts[k]) for k in range(4)]
    return [jnp.where(high, first[k ^ 2], first[k]) for k in range(4)]


def assemble_kernel(norm, bits, *refs):
    parts = [r[...].astype(F32) for r in refs[:4]]
    blocks = pick4(parts, bits[0] != 0, bits[1] != 0)
    odd = bits[2] != 0
    halves = [[], []]
    for b in blocks:
        low, high = b[:, :HEAD], b[:, HEAD:]
        halves[0].append(jnp.where(odd, high, low))
        halves[1].append(jnp.where(odd, low, high))
    rows = jnp.concatenate(halves[0] + halves[1], 1)
    refs[4][...] = rows.astype(BF16)
    if norm:
        scale = lax.rsqrt(jnp.mean(rows * rows, 1, keepdims=True) + EPS)
        refs[5][...] = (rows * scale).astype(BF16)
        refs[6][...] = scale


def assemble(parts, norm):
    tokens, width = parts[0].shape
    model = 4 * width
    if not small_slice():
        col = lax.axis_index(COL)
        blocks = pick4(parts, (col & 1) != 0, (col & 2) != 0)
        rows = to_order(jnp.concatenate(blocks, 1))
        if not norm:
            return rows
        wide = rows.astype(F32)
        scale = lax.rsqrt(jnp.mean(wide * wide, 1, keepdims=True) + EPS)
        return rows, (wide * scale).astype(BF16), scale
    step = 128
    row = lambda n: pl.BlockSpec((step, n), lambda i: (i, 0))
    shape = [jax.ShapeDtypeStruct((tokens, model), BF16)]
    specs = [row(model)]
    if norm:
        shape += [shape[0], jax.ShapeDtypeStruct((tokens, 1), F32)]
        specs += [row(model), row(1)]
    out = pl.pallas_call(
        functools.partial(assemble_kernel, norm),
        grid=(tokens // step,),
        in_specs=[pl.BlockSpec(memory_space=pltpu.SMEM)] + [row(width)] * 4,
        out_specs=specs,
        out_shape=shape,
        name="assemble",
    )(place_bits(), *parts)
    return out if norm else out[0]


def divide_kernel(bits, rows_ref, *refs):
    rows = rows_ref[...].astype(F32)
    odd = bits[2] != 0
    blocks = []
    for k in range(4):
        low = rows[:, k * HEAD : (k + 1) * HEAD]
        high = rows[:, (4 + k) * HEAD : (5 + k) * HEAD]
        blocks.append(
            jnp.concatenate([jnp.where(odd, high, low), jnp.where(odd, low, high)], 1)
        )
    for ref, block in zip(refs, pick4(blocks, bits[0] != 0, bits[1] != 0)):
        ref[...] = block.astype(BF16)


def divide(rows):
    tokens, model = rows.shape
    width = model // 4
    if not small_slice():
        col = lax.axis_index(COL)
        whole = from_order(rows)
        blocks = [whole[:, k * width : (k + 1) * width] for k in range(4)]
        return pick4(blocks, (col & 1) != 0, (col & 2) != 0)
    step = 128
    row = lambda n: pl.BlockSpec((step, n), lambda i: (i, 0))
    return pl.pallas_call(
        divide_kernel,
        grid=(tokens // step,),
        in_specs=[pl.BlockSpec(memory_space=pltpu.SMEM), row(model)],
        out_specs=[row(width)] * 4,
        out_shape=[jax.ShapeDtypeStruct((tokens, width), BF16)] * 4,
        name="divide",
    )(place_bits(), rows)


def tokens_in(parts, norm):
    col = lax.axis_index(COL)
    got = []
    for bits in range(4):
        mine = lax.dynamic_index_in_dim(parts, col ^ bits, 0, False)
        got.append(mine if bits == 0 else swap(mine, COL, bits))
    return assemble(got, norm)


def tokens_out(rows):
    col = lax.axis_index(COL)
    parts = divide(rows)
    got = [parts[0]] + [swap(parts[bits], COL, bits) for bits in range(1, 4)]
    return jnp.stack(pick4(got, (col & 1) != 0, (col & 2) != 0))


def gather_weight(shard, order):
    ny = lax.axis_size("dp")
    rows, width = shard.shape
    part = rows // ny
    start = lax.axis_index("dp") * part
    value = lax.dynamic_slice_in_dim(shard, start, part, 0)
    for bit in bits_of("row"):
        value = jnp.concatenate([value, swap(value, "row", bit)], 0)
    if order == "yx":
        for bit in bits_of("dp"):
            value = jnp.concatenate([value, swap(value, "dp", bit)], 0)
        return [value, side(value)]
    values = [value, side(value)]
    for bit in bits_of("dp"):
        values = [jnp.concatenate([v, swap(v, "dp", bit)], 0) for v in values]
    return values


def fold(value, axis):
    for bit in reversed(bits_of(axis)):
        half = value.shape[0] // 2
        got = swap(value[half:].astype(BF16), axis, bit)
        value = value[:half].astype(F32) + got.astype(F32)
    return value


def reduce_grad(own, other, order):
    if order == "xy":
        value = own.astype(F32) + side(other).astype(F32)
        value = fold(value, "dp")
    else:
        own, other = fold(own, "dp"), fold(other, "dp")
        value = own + side(other.astype(BF16)).astype(F32)
    return fold(value, "row")


def dot(left, right, form):
    return jnp.einsum(form, left, right, preferred_element_type=F32)


def nn(a, b):
    return jnp.dot(a, b, preferred_element_type=F32)


def nt(a, b):
    return lax.dot_general(a, b, (((1,), (1,)), ((), ())), preferred_element_type=F32)


def tn(a, b):
    return lax.dot_general(a, b, (((0,), (0,)), ((), ())), preferred_element_type=F32)


def silu_slope(pre):
    logistic = jax.nn.sigmoid(pre)
    return logistic * (1.0 + pre * (1.0 - logistic))


def tile_decay(rate, seg_col, seg_row, at, width):
    rows = seg_col.shape[0]
    shape = (rows, width)
    gap = lax.broadcasted_iota(jnp.int32, shape, 0) + at - lax.broadcasted_iota(jnp.int32, shape, 1)
    visible = (gap >= 0) & (seg_col == seg_row)
    return jnp.where(visible, jnp.exp(-rate * jnp.maximum(gap, 0).astype(F32)), 0.0)


def column(tokens):
    return lax.broadcasted_iota(jnp.int32, (tokens, 1), 0).astype(F32)


def own_weight(rate, seg_col, last):
    tokens = seg_col.shape[0]
    return jnp.where(seg_col == last, jnp.exp(-rate * (tokens - 1.0 - column(tokens))), 0.0)


def entry_weight(rate, seg_col, entry_seg):
    tokens = seg_col.shape[0]
    return jnp.where(seg_col == entry_seg, jnp.exp(-rate * (column(tokens) + 1.0)), 0.0)


def first_kernel(rates, marks, seg_c, seg_r, zq, zk, zv, q_out, k_out, v_out, o_out, state):
    block, head = pl.program_id(0), pl.program_id(1)
    rate = rates[head]
    pre_q, pre_k = zq[...], zk[...]
    q = (pre_q * jax.nn.sigmoid(pre_q)).astype(BF16)
    k_wide = pre_k * jax.nn.sigmoid(pre_k)
    k = k_wide.astype(BF16)
    v = zv[...].astype(BF16)
    q_out[...], k_out[...], v_out[...] = q, k, v
    seg = seg_c[0]
    weight = own_weight(rate, seg, marks[block, 0])
    state[0, 0] = tn((k.astype(F32) * weight).astype(BF16), v)
    tokens = q.shape[0]
    for at in range(0, tokens, TILE):
        width = at + TILE
        decay = tile_decay(rate, seg[at:width], seg_r[0, :, :width], at, width)
        mix = (nt(q[at:width], k[:width]) * decay).astype(BF16)
        o_out[at:width, :] = nn(mix, v[:width])


def carry_kernel(rates, marks, seg_c, o_in, q, entry, o_out, squares):
    block, head = pl.program_id(0), pl.program_id(1)
    weight = entry_weight(rates[head], seg_c[0], marks[block, 1])
    o = o_in[...] + weight * nn(q[...], entry[0, 0])
    o_out[...] = o

    @pl.when(head == 0)
    def _():
        squares[...] = jnp.zeros_like(squares)

    squares[...] += jnp.sum(o * o, 1, keepdims=True)


def entry_grad_kernel(rates, marks, seg_c, q, do, grad):
    block, head = pl.program_id(0), pl.program_id(1)
    weight = entry_weight(rates[head], seg_c[0], marks[block, 1])
    grad[0, 0] = tn(q[...], (do[...].astype(F32) * weight).astype(BF16))


def inner_grad_kernel(
    rates, marks, seg_c, seg_r, q_ref, k_ref, v_ref, do_ref, entry, zq, dzq, dk, dv
):
    block, head = pl.program_id(0), pl.program_id(1)
    rate = rates[head]
    seg = seg_c[0]
    weight = entry_weight(rate, seg, marks[block, 1])
    tokens = seg.shape[0]
    for at in range(0, tokens, TILE):
        width = at + TILE
        q, do = q_ref[at:width, :], do_ref[at:width, :]
        k, v = k_ref[:width, :], v_ref[:width, :]
        decay = tile_decay(rate, seg[at:width], seg_r[0, :, :width], at, width)
        mix = (nt(q, k) * decay).astype(BF16)
        ds = (nt(do, v) * decay).astype(BF16)
        scaled = (do.astype(F32) * weight[at:width]).astype(BF16)
        dq = nn(ds, k) + nt(scaled, entry[0, 0])
        dzq[at:width, :] = (dq * silu_slope(zq[at:width, :])).astype(BF16)
        dk_new, dv_new = tn(ds, q), tn(mix, do)
        if at:
            dk[:at, :] += dk_new[:at]
            dv[:at, :] += dv_new[:at]
        dk[at:width, :] = dk_new[at:]
        dv[at:width, :] = dv_new[at:]


def last_grad_kernel(rates, marks, seg_c, k, v, d_state, zk, dk, dv, dzk, dzv):
    block, head = pl.program_id(0), pl.program_id(1)
    weight = own_weight(rates[head], seg_c[0], marks[block, 0])
    state = d_state[0, 0]
    dk_all = dk[...] + weight * nt(v[...], state)
    dzk[...] = (dk_all * silu_slope(zk[...])).astype(BF16)
    scaled = (k[...].astype(F32) * weight).astype(BF16)
    dzv[...] = (dv[...] + nn(scaled, state)).astype(BF16)


def head_call(kernel, tokens, heads, kinds_in, kinds_out, args, flops, name):
    specs = {
        "s": pl.BlockSpec(memory_space=pltpu.SMEM),
        "c": pl.BlockSpec((1, tokens, 1), lambda b, h: (b, 0, 0)),
        "r": pl.BlockSpec((1, 1, tokens), lambda b, h: (b, 0, 0)),
        "t": pl.BlockSpec((tokens, HEAD), lambda b, h: (b, h)),
        "p": pl.BlockSpec((1, 1, HEAD, HEAD), lambda b, h: (b, h, 0, 0)),
        "n": pl.BlockSpec((tokens, 1), lambda b, h: (b, 0)),
    }
    shapes = {
        "T": jax.ShapeDtypeStruct((2 * tokens, heads * HEAD), F32),
        "t": jax.ShapeDtypeStruct((2 * tokens, heads * HEAD), BF16),
        "p": jax.ShapeDtypeStruct((2, heads, HEAD, HEAD), F32),
        "n": jax.ShapeDtypeStruct((2 * tokens, 1), F32),
    }
    return pl.pallas_call(
        kernel,
        grid=(2, heads),
        in_specs=[specs[k.lower()] for k in kinds_in],
        out_specs=[specs[k.lower()] for k in kinds_out],
        out_shape=[shapes[k] for k in kinds_out],
        cost_estimate=pl.CostEstimate(flops=flops, bytes_accessed=8 << 20, transcendentals=0),
        name=name,
    )(*args)


def chain(local, factor, reverse):
    count = lax.axis_size("row")
    entry = jnp.zeros(local.shape, BF16)
    for hop in range(count - 1):
        out = (local + factor[:, :, None, None] * entry.astype(F32)).astype(BF16)
        edge = (count - 1 - hop, count - 2 - hop) if reverse else (hop, hop + 1)
        entry = entry + lax.ppermute(out, "row", [edge])
    return entry


def other_first(value):
    return jnp.flip(pair(value), 0)


def ff_gather(w_gate, w_up, w_down):
    nx, nz, ny = [lax.axis_size(a) for a in CHIPS]
    rows = jnp.concatenate([w_gate.T, w_up.T, w_down], 0)
    part = rows.shape[1] // ny
    shard = lax.dynamic_slice_in_dim(rows, lax.axis_index("dp") * part, part, 1)
    blocks = lax.all_gather(shard, CHIPS, axis=0, tiled=True)
    hidden = rows.shape[0]
    z, y = lax.axis_index("row"), lax.axis_index("dp")
    if small_slice():
        blocks = blocks.reshape(nx, nz * ny, hidden, part)
        kz, ky = jnp.arange(nz * ny) % nz, jnp.arange(nz * ny) // nz
        tables = jnp.stack([(z ^ kz) * ny + (y ^ ky), (y ^ ky) * nz + (z ^ kz)])
        return blocks, tables.astype(jnp.int32)
    blocks = blocks.reshape(nx, nz, ny, hidden, part)
    blocks = xor_turn(xor_turn(blocks, 1, z, nz), 2, y, ny).transpose(0, 2, 1, 3, 4)
    blocks = blocks.reshape(nx, -1, HEAD // part, hidden, part).transpose(0, 1, 3, 2, 4)
    blocks = blocks.reshape(nx, -1, hidden, HEAD)
    same = jnp.arange(blocks.shape[1], dtype=jnp.int32)
    return blocks, jnp.stack([same, same])


def ff_scatter_xy(grads):
    nx, nz, ny = [lax.axis_size(a) for a in CHIPS]
    hidden = grads.shape[2]
    part = grads.shape[1] * HEAD // (nz * ny)
    if not small_slice():
        z, y = lax.axis_index("row"), lax.axis_index("dp")
        grads = grads.reshape(nx, -1, hidden, HEAD // part, part).transpose(0, 1, 3, 2, 4)
        grads = grads.reshape(nx, ny, nz, hidden, part)
        grads = xor_turn(xor_turn(grads, 1, y, ny), 2, z, nz)
    grads = grads.reshape(-1, part)
    return lax.psum_scatter(grads, ("cx", "dp"), scatter_dimension=0, tiled=True)


def ff_kernel(tables, b_ref, g_ref, w_ref, out, out_send, db, db_send, grads, *scratch):
    m_all, d1_all, d2_all, out_acc, db_acc = scratch
    step = pl.program_id(0)
    blocks, hidden = w_ref.shape[1], w_ref.shape[2] // 3
    tokens = out.shape[0]

    def weight(i):
        at = slice(i * hidden, (i + 1) * hidden)
        return jnp.concatenate([w_ref[0, tables[0, p], at, :] for p in range(blocks)], 1)

    gate_w, up_w, down_w = weight(0), weight(1), weight(2)
    for half in range(2):
        rows = slice(half * tokens, (half + 1) * tokens)
        b, g = b_ref[rows, :], g_ref[rows, :]
        z1, z2, dm = nt(b, gate_w), nt(b, up_w), nt(g, down_w)
        m, d1, d2 = (z1 * z2).astype(BF16), (dm * z2).astype(BF16), (dm * z1).astype(BF16)
        m_all[rows, :], d1_all[rows, :], d2_all[rows, :] = m, d1, d2
        sums = nn(m, down_w), nn(d1, gate_w) + nn(d2, up_w)
        kept = (out_acc, db_acc) if half else (out, db)

        @pl.when(step == 0)
        def _():
            for ref, value in zip(kept, sums):
                ref[...] = value

        @pl.when(step != 0)
        def _():
            sent = (out_send, db_send) if half else kept
            for to, ref, value in zip(sent, kept, sums):
                to[...] = (ref[...] + value).astype(to.dtype)

    for i, (left, right) in enumerate(((d1_all, b_ref), (d2_all, b_ref), (m_all, g_ref))):
        grad = tn(left[...], right[...]).astype(BF16)
        at = slice(i * hidden, (i + 1) * hidden)
        for p in range(blocks):
            grads[0, tables[1, p], at, :] = grad[:, p * HEAD : (p + 1) * HEAD]


def feed_forward(b, g, weights, tables):
    rows, model = b.shape
    tokens = rows // 2
    nx, blocks, hidden, width = weights.shape
    once = pl.Buffered(1)
    fixed = lambda n: pl.BlockSpec((n, model), lambda x: (0, 0), pipeline_mode=once)
    turn = pl.BlockSpec((1, blocks, hidden, width), lambda x: (x, 0, 0, 0))
    wide = jax.ShapeDtypeStruct((tokens, model), F32)
    narrow = jax.ShapeDtypeStruct((tokens, model), BF16)
    product = pltpu.VMEM((rows, hidden // 3), BF16)
    total = pltpu.VMEM((tokens, model), F32)
    return pl.pallas_call(
        ff_kernel,
        grid=(nx,),
        in_specs=[pl.BlockSpec(memory_space=pltpu.SMEM), fixed(rows), fixed(rows), turn],
        out_specs=[fixed(tokens)] * 4 + [turn],
        out_shape=[wide, narrow, wide, narrow, jax.ShapeDtypeStruct(weights.shape, BF16)],
        scratch_shapes=[product] * 3 + [total] * 2,
        compiler_params=pltpu.CompilerParams(vmem_limit_bytes=60 << 20),
        cost_estimate=pl.CostEstimate(
            flops=6 * nx * rows * model * hidden, bytes_accessed=36 << 20, transcendentals=0
        ),
        name="feed_forward",
    )(tables, b, g, weights)


def on_device(
    block_input,
    segments,
    decay_rate,
    w_query,
    w_key,
    w_value,
    w_output_gate,
    w_out,
    w_gate,
    w_up,
    w_down,
    out_grad,
):
    nz = lax.axis_size("row")
    col = lax.axis_index(COL)
    place = lax.axis_index("row")
    tokens = block_input.shape[2]
    model = block_input.shape[3] * lax.axis_size(COL)
    wide = w_query.shape[1]

    parts = gather_weight(jnp.concatenate([w_query, w_key], 1), "xy")
    wq = jnp.concatenate([w[:, :wide] for w in parts], 1)
    wk = jnp.concatenate([w[:, wide:] for w in parts], 1)
    parts = gather_weight(jnp.concatenate([w_value, w_output_gate], 1), "yx")
    wv = jnp.concatenate([w[:, :wide] for w in parts], 1)
    wu = jnp.concatenate([w[:, wide:] for w in parts], 1)
    wo = jnp.concatenate(gather_weight(w_out.T, "xy"), 1)
    ff_weights, tables = ff_gather(w_gate, w_up, w_down)

    x_own, a_own, r1 = tokens_in(block_input[:, 0], True)
    g_own = tokens_in(out_grad[:, 0], False)
    rates = jnp.concatenate([decay_rate, side(decay_rate)])
    heads = rates.shape[0]
    seg_all = segments[:, 0].astype(F32)
    seg = jnp.stack(
        [
            lax.dynamic_index_in_dim(seg_all, col, 0, False),
            lax.dynamic_index_in_dim(seg_all, col ^ 1, 0, False),
        ]
    )
    last = seg[:, tokens - 1]
    before = lax.ppermute(last, "row", [(i, i + 1) for i in range(nz - 1)])
    entry_seg = jnp.where(place == 0, -1.0, before)
    linked = ((seg[:, 0] == last) & (entry_seg == last)).astype(F32)
    factor = linked[:, None] * jnp.exp(-rates * tokens)[None]
    marks = jnp.stack([last, entry_seg], 1)
    seg_c, seg_r = seg[:, :, None], seg[:, None, :]
    heads_of = functools.partial(head_call, tokens=tokens, heads=heads)
    unit = 2 * heads * 2 * tokens * tokens * HEAD

    def both(own):
        return jnp.concatenate([own, pair(own)], 0)

    def back_sum(lefts, rights, form):
        def total(rows):
            out = dot(lefts[0][rows], rights[0], form)
            for left, right in zip(lefts[1:], rights[1:]):
                out = out + dot(left[rows], right, form)
            return out

        sent = pair(total(slice(tokens, None)).astype(BF16))
        return total(slice(0, tokens)) + sent.astype(F32)

    a = both(a_own)
    g = both(g_own)
    zq, zk, zv, zu = [dot(a, w, "td,dc->tc") for w in (wq, wk, wv, wu)]
    q, k, v, o_inner, local = heads_of(
        first_kernel,
        kinds_in="sscrTTT",
        kinds_out="tttTp",
        args=(rates, marks, seg_c, seg_r, zq, zk, zv),
        flops=unit,
        name="mixer_first",
    )
    entry = chain(local, factor, False)
    o, squares = heads_of(
        carry_kernel,
        kinds_in="sscTtp",
        kinds_out="Tn",
        args=(rates, marks, seg_c, o_inner, q, entry),
        flops=unit // 8,
        name="mixer_carry",
    )
    gate = jax.nn.sigmoid(zu)
    squares = squares.reshape(2, tokens)
    squares = (squares + other_first(squares)).reshape(2 * tokens, 1)
    r2 = lax.rsqrt(squares / model + EPS)
    y = (o * r2 * gate).astype(BF16)
    hres = x_own.astype(F32) + back_sum((y,), (wo,), "tc,dc->td")
    r3 = lax.rsqrt(jnp.mean(hres * hres, 1, keepdims=True) + EPS)
    b = both((hres * r3).astype(BF16))
    out, out_send, db, db_send, ff_grads = feed_forward(b, g, ff_weights, tables)
    db = db + pair(db_send).astype(F32)
    block_out = tokens_out((hres + out + pair(out_send).astype(F32)).astype(BF16))

    ff_part = ff_scatter_xy(ff_grads)
    dh = (
        g_own.astype(F32)
        + r3 * db
        - hres * (r3**3 * jnp.mean(db * hres, 1, keepdims=True))
    )
    dhr = both(dh.astype(BF16))

    grad_out = dot(dhr, y, "td,tc->dc").astype(BF16)
    dy = dot(dhr, wo, "td,dc->tc")
    dn = dy * gate
    dzu = (dy * o * r2 * gate * (1.0 - gate)).astype(BF16)
    dots = jnp.sum(dn * o, 1).reshape(2, tokens)
    dots = (dots + other_first(dots)).reshape(2 * tokens, 1)
    do = (r2 * dn - o * (r2**3 * dots / model)).astype(BF16)
    (d_entry,) = heads_of(
        entry_grad_kernel,
        kinds_in="ssctt",
        kinds_out="p",
        args=(rates, marks, seg_c, q, do),
        flops=unit // 8,
        name="mixer_entry_grad",
    )
    d_local = chain(d_entry, factor, True)
    dzq, dk, dv = heads_of(
        inner_grad_kernel,
        kinds_in="sscrttttpT",
        kinds_out="tTT",
        args=(rates, marks, seg_c, seg_r, q, k, v, do, entry, zq),
        flops=5 * unit // 2,
        name="mixer_inner_grad",
    )
    dzk, dzv = heads_of(
        last_grad_kernel,
        kinds_in="sscttpTTT",
        kinds_out="tt",
        args=(rates, marks, seg_c, k, v, d_local, zk, dk, dv),
        flops=unit // 4,
        name="mixer_last_grad",
    )
    grads = [dot(a, d, "td,tc->dc").astype(BF16) for d in (dzq, dzk, dzv, dzu)]
    da = back_sum((dzq, dzk, dzv, dzu), (wq, wk, wv, wu), "tc,dc->td")
    x_wide = x_own.astype(F32)
    input_grad = tokens_out(
        (
            dh + r1 * da - x_wide * (r1**3 * jnp.mean(da * x_wide, 1, keepdims=True))
        ).astype(BF16)
    )

    def halves(*mats):
        return [
            jnp.concatenate([g[:, at : at + wide] for g in mats], 1) for at in (0, wide)
        ]

    ff_part, _ = lax.optimization_barrier((ff_part, dzk))
    ff_total = lax.psum_scatter(ff_part, "row", scatter_dimension=0, tiled=True).astype(F32)
    hidden = w_down.shape[0]
    total_gate, total_up = ff_total[:hidden].T, ff_total[hidden : 2 * hidden].T
    total_ou = reduce_grad(*halves(grad_out, grads[3]), "yx")
    total_qk = reduce_grad(*halves(grads[0], grads[1]), "xy")
    total_v = reduce_grad(*halves(grads[2]), "yx")
    return (
        block_out[:, None],
        input_grad[:, None],
        total_qk[:, :wide],
        total_qk[:, wide:],
        total_v,
        total_ou[:, wide:],
        total_ou[:, :wide].T,
        total_gate,
        total_up,
        ff_total[2 * hidden :],
    )


def solution(mesh):
    rows, cols, copies = [mesh.shape[a] for a in ("row", "col", "dp")]
    split = jax.sharding.Mesh(
        mesh.devices.reshape(rows, cols // 2, 2, copies), ("row", "cx", "cc", "dp")
    )
    placed = (
        P(None, "dp", "row", COL),
        P(None, "dp", "row"),
        P(COL),
        P("row", COL),
        P("row", COL),
        P("row", COL),
        P("row", COL),
        P(COL, "row"),
        P("row", COL),
        P("row", COL),
        P(COL, "row"),
        P(None, "dp", "row", COL),
    )
    return jax.shard_map(
        on_device,
        mesh=split,
        in_specs=placed,
        out_specs=(
            P(None, "dp", "row", COL),
            P(None, "dp", "row", COL),
            P(("row", "dp"), COL),
            P(("row", "dp"), COL),
            P(("row", "dp"), COL),
            P(("row", "dp"), COL),
            P(COL, ("row", "dp")),
            P(("row", "dp"), COL),
            P(("row", "dp"), COL),
            P(COL, ("row", "dp")),
        ),
        check_vma=False,
    )
```

```python
import functools

import jax
import jax.numpy as jnp
from jax import lax
from jax.experimental import pallas as pl
from jax.experimental.pallas import tpu as pltpu
from jax.sharding import PartitionSpec as P

HEAD = 128
TILE = 256
EPS = 1e-06
F32 = jnp.float32
BF16 = jnp.bfloat16


COL = ("cx", "cc")
CHIPS = ("cx", "row", "dp")


def swap(value, axis, bits):
    count = lax.axis_size(axis)
    return lax.ppermute(value, axis, [(i, i ^ bits) for i in range(count)])


def pair(value):
    return swap(value, COL, 1)


def side(value):
    return swap(value, COL, 2)


def bits_of(axis):
    return [1 << b for b in range(lax.axis_size(axis).bit_length() - 1)]


def xor_turn(value, dim, place, count):
    bit = 1
    while bit < count:
        shape = value.shape
        split = value.reshape(shape[:dim] + (count // (2 * bit), 2, bit) + shape[dim + 1 :])
        flipped = jnp.flip(split, dim + 1)
        value = jnp.where((place & bit) != 0, flipped, split).reshape(shape)
        bit *= 2
    return value


def to_order(rows):
    nz, ny = lax.axis_size("row"), lax.axis_size("dp")
    tokens, width = rows.shape
    split = rows.reshape(tokens, nz, ny, width // (nz * ny))
    split = xor_turn(split, 1, lax.axis_index("row"), nz)
    split = xor_turn(split, 2, lax.axis_index("dp"), ny)
    return split.transpose(0, 2, 1, 3).reshape(tokens, width)


def from_order(rows):
    nz, ny = lax.axis_size("row"), lax.axis_size("dp")
    tokens, width = rows.shape
    split = rows.reshape(tokens, ny, nz, width // (nz * ny)).transpose(0, 2, 1, 3)
    split = xor_turn(split, 1, lax.axis_index("row"), nz)
    split = xor_turn(split, 2, lax.axis_index("dp"), ny)
    return split.reshape(tokens, width)


def small_slice():
    return lax.axis_size("row") == 4 and lax.axis_size("dp") == 2


def place_bits():
    turn = lax.axis_index(COL) ^ lax.axis_index("row")
    return jnp.stack([turn & 1, turn >> 1, lax.axis_index("dp"), 0]).astype(jnp.int32)


def pick4(parts, low, high):
    first = [jnp.where(low, parts[k ^ 1], parts[k]) for k in range(4)]
    return [jnp.where(high, first[k ^ 2], first[k]) for k in range(4)]


def assemble_kernel(norm, bits, *refs):
    parts = [r[...].astype(F32) for r in refs[:4]]
    blocks = pick4(parts, bits[0] != 0, bits[1] != 0)
    odd = bits[2] != 0
    halves = [[], []]
    for b in blocks:
        low, high = b[:, :HEAD], b[:, HEAD:]
        halves[0].append(jnp.where(odd, high, low))
        halves[1].append(jnp.where(odd, low, high))
    rows = jnp.concatenate(halves[0] + halves[1], 1)
    refs[4][...] = rows.astype(BF16)
    if norm:
        scale = lax.rsqrt(jnp.mean(rows * rows, 1, keepdims=True) + EPS)
        refs[5][...] = (rows * scale).astype(BF16)
        refs[6][...] = scale


def assemble(parts, norm):
    tokens, width = parts[0].shape
    model = 4 * width
    if not small_slice():
        col = lax.axis_index(COL)
        blocks = pick4(parts, (col & 1) != 0, (col & 2) != 0)
        rows = to_order(jnp.concatenate(blocks, 1))
        if not norm:
            return rows
        wide = rows.astype(F32)
        scale = lax.rsqrt(jnp.mean(wide * wide, 1, keepdims=True) + EPS)
        return rows, (wide * scale).astype(BF16), scale
    step = 128
    row = lambda n: pl.BlockSpec((step, n), lambda i: (i, 0))
    shape = [jax.ShapeDtypeStruct((tokens, model), BF16)]
    specs = [row(model)]
    if norm:
        shape += [shape[0], jax.ShapeDtypeStruct((tokens, 1), F32)]
        specs += [row(model), row(1)]
    out = pl.pallas_call(
        functools.partial(assemble_kernel, norm),
        grid=(tokens // step,),
        in_specs=[pl.BlockSpec(memory_space=pltpu.SMEM)] + [row(width)] * 4,
        out_specs=specs,
        out_shape=shape,
        name="assemble",
    )(place_bits(), *parts)
    return out if norm else out[0]


def divide_kernel(bits, rows_ref, *refs):
    rows = rows_ref[...].astype(F32)
    odd = bits[2] != 0
    blocks = []
    for k in range(4):
        low = rows[:, k * HEAD : (k + 1) * HEAD]
        high = rows[:, (4 + k) * HEAD : (5 + k) * HEAD]
        blocks.append(
            jnp.concatenate([jnp.where(odd, high, low), jnp.where(odd, low, high)], 1)
        )
    for ref, block in zip(refs, pick4(blocks, bits[0] != 0, bits[1] != 0)):
        ref[...] = block.astype(BF16)


def divide(rows):
    tokens, model = rows.shape
    width = model // 4
    if not small_slice():
        col = lax.axis_index(COL)
        whole = from_order(rows)
        blocks = [whole[:, k * width : (k + 1) * width] for k in range(4)]
        return pick4(blocks, (col & 1) != 0, (col & 2) != 0)
    step = 128
    row = lambda n: pl.BlockSpec((step, n), lambda i: (i, 0))
    return pl.pallas_call(
        divide_kernel,
        grid=(tokens // step,),
        in_specs=[pl.BlockSpec(memory_space=pltpu.SMEM), row(model)],
        out_specs=[row(width)] * 4,
        out_shape=[jax.ShapeDtypeStruct((tokens, width), BF16)] * 4,
        name="divide",
    )(place_bits(), rows)


def tokens_in(parts, norm):
    col = lax.axis_index(COL)
    got = []
    for bits in range(4):
        mine = lax.dynamic_index_in_dim(parts, col ^ bits, 0, False)
        got.append(mine if bits == 0 else swap(mine, COL, bits))
    return assemble(got, norm)


def tokens_out(rows):
    col = lax.axis_index(COL)
    parts = divide(rows)
    got = [parts[0]] + [swap(parts[bits], COL, bits) for bits in range(1, 4)]
    return jnp.stack(pick4(got, (col & 1) != 0, (col & 2) != 0))


def gather_weights(first, second):
    ny = lax.axis_size("dp")
    part, width = first.shape[0] // ny, first.shape[1]
    value = jnp.concatenate([first, second], 1)
    value = lax.dynamic_slice_in_dim(value, lax.axis_index("dp") * part, part, 0)
    for bit in bits_of("row"):
        value = jnp.concatenate([value, swap(value, "row", bit)], 0)
    one, two = value[:, :width], value[:, width:]
    one = jnp.concatenate([one, side(one)], 1)
    for bit in bits_of("dp"):
        two = jnp.concatenate([two, swap(two, "dp", bit)], 0)
        one = jnp.concatenate([one, swap(one, "dp", bit)], 0)
    return one, jnp.concatenate([two, side(two)], 1), value


def fold(value, axis):
    for bit in reversed(bits_of(axis)):
        half = value.shape[0] // 2
        got = swap(value[half:].astype(BF16), axis, bit)
        value = value[:half].astype(F32) + got.astype(F32)
    return value


def fold_side(value):
    half = value.shape[1] // 2
    got = side(value[:, half:].astype(BF16))
    return value[:, :half].astype(F32) + got.astype(F32)


def reduce_first(one, two):
    return fold_side(one), fold(two, "dp")


def reduce_rest(one, two):
    return fold(jnp.concatenate([fold(one, "dp"), fold_side(two)], 1), "row")


def dot(left, right, form):
    return jnp.einsum(form, left, right, preferred_element_type=F32)


def nn(a, b):
    return jnp.dot(a, b, preferred_element_type=F32)


def nt(a, b):
    return lax.dot_general(a, b, (((1,), (1,)), ((), ())), preferred_element_type=F32)


def tn(a, b):
    return lax.dot_general(a, b, (((0,), (0,)), ((), ())), preferred_element_type=F32)


def silu_slope(pre):
    logistic = jax.nn.sigmoid(pre)
    return logistic * (1.0 + pre * (1.0 - logistic))


def tile_decay(rate, seg_col, seg_row, at, width):
    rows = seg_col.shape[0]
    shape = (rows, width)
    gap = lax.broadcasted_iota(jnp.int32, shape, 0) + at - lax.broadcasted_iota(jnp.int32, shape, 1)
    visible = (gap >= 0) & (seg_col == seg_row)
    return jnp.where(visible, jnp.exp(-rate * jnp.maximum(gap, 0).astype(F32)), 0.0)


def column(tokens):
    return lax.broadcasted_iota(jnp.int32, (tokens, 1), 0).astype(F32)


def own_weight(rate, seg_col, last):
    tokens = seg_col.shape[0]
    return jnp.where(seg_col == last, jnp.exp(-rate * (tokens - 1.0 - column(tokens))), 0.0)


def entry_weight(rate, seg_col, entry_seg):
    tokens = seg_col.shape[0]
    return jnp.where(seg_col == entry_seg, jnp.exp(-rate * (column(tokens) + 1.0)), 0.0)


def lanes(head):
    return slice(head * HEAD, (head + 1) * HEAD)


def local_kernel(rates, marks, seg_c, zk, zv, k_out, v_out, state):
    last = marks[pl.program_id(0), 0]
    for head in range(state.shape[1]):
        at = lanes(head)
        pre = zk[:, at]
        k, v = (pre * jax.nn.sigmoid(pre)).astype(BF16), zv[:, at].astype(BF16)
        k_out[:, at], v_out[:, at] = k, v
        weight = own_weight(rates[head], seg_c[0], last)
        state[0, head] = tn((k.astype(F32) * weight).astype(BF16), v)


def inner_kernel(rates, marks, seg_c, seg_r, zq, k_ref, v_ref, q_out, o_out):
    seg, tokens = seg_c[0], seg_c.shape[1]
    for head in range(zq.shape[1] // HEAD):
        at = lanes(head)
        pre = zq[:, at]
        q_out[:, at] = (pre * jax.nn.sigmoid(pre)).astype(BF16)
        for top in range(0, tokens, TILE):
            width = top + TILE
            decay = tile_decay(rates[head], seg[top:width], seg_r[0, :, :width], top, width)
            mix = (nt(q_out[top:width, at], k_ref[:width, at]) * decay).astype(BF16)
            o_out[top:width, at] = nn(mix, v_ref[:width, at])


def carry_kernel(rates, marks, seg_c, o_in, q, entry, o_out, squares):
    before = marks[pl.program_id(0), 1]
    total = 0.0
    for head in range(entry.shape[1]):
        at = lanes(head)
        weight = entry_weight(rates[head], seg_c[0], before)
        o = o_in[:, at] + weight * nn(q[:, at], entry[0, head])
        o_out[:, at] = o
        total = total + o * o
    squares[...] = jnp.sum(total, 1, keepdims=True)


def entry_grad_kernel(rates, marks, seg_c, q, do, grad):
    before = marks[pl.program_id(0), 1]
    for head in range(grad.shape[1]):
        at = lanes(head)
        weight = entry_weight(rates[head], seg_c[0], before)
        grad[0, head] = tn(q[:, at], (do[:, at].astype(F32) * weight).astype(BF16))


def inner_grad_kernel(
    rates, marks, seg_c, seg_r, q_ref, k_ref, v_ref, do_ref, entry, zq, dzq, dk, dv
):
    before = marks[pl.program_id(0), 1]
    seg, tokens = seg_c[0], seg_c.shape[1]
    for head in range(entry.shape[1]):
        at = lanes(head)
        weight = entry_weight(rates[head], seg, before)
        for top in range(0, tokens, TILE):
            width = top + TILE
            q, do = q_ref[top:width, at], do_ref[top:width, at]
            k, v = k_ref[:width, at], v_ref[:width, at]
            decay = tile_decay(rates[head], seg[top:width], seg_r[0, :, :width], top, width)
            mix = (nt(q, k) * decay).astype(BF16)
            ds = (nt(do, v) * decay).astype(BF16)
            scaled = (do.astype(F32) * weight[top:width]).astype(BF16)
            dq = nn(ds, k) + nt(scaled, entry[0, head])
            dzq[top:width, at] = (dq * silu_slope(zq[top:width, at])).astype(BF16)
            dk_new, dv_new = tn(ds, q), tn(mix, do)
            if top:
                dk[:top, at] += dk_new[:top]
                dv[:top, at] += dv_new[:top]
            dk[top:width, at] = dk_new[top:]
            dv[top:width, at] = dv_new[top:]


def last_grad_kernel(rates, marks, seg_c, k, v, d_state, zk, dk, dv, dzk, dzv):
    last = marks[pl.program_id(0), 0]
    for head in range(d_state.shape[1]):
        at = lanes(head)
        weight = own_weight(rates[head], seg_c[0], last)
        state = d_state[0, head]
        dk_all = dk[:, at] + weight * nt(v[:, at], state)
        dzk[:, at] = (dk_all * silu_slope(zk[:, at])).astype(BF16)
        scaled = (k[:, at].astype(F32) * weight).astype(BF16)
        dzv[:, at] = (dv[:, at] + nn(scaled, state)).astype(BF16)


def head_call(kernel, tokens, heads, kinds_in, kinds_out, args, flops, name):
    specs = {
        "s": pl.BlockSpec(memory_space=pltpu.SMEM),
        "c": pl.BlockSpec((1, tokens, 1), lambda b: (b, 0, 0)),
        "r": pl.BlockSpec((1, 1, tokens), lambda b: (b, 0, 0)),
        "t": pl.BlockSpec((tokens, heads * HEAD), lambda b: (b, 0)),
        "p": pl.BlockSpec((1, heads, HEAD, HEAD), lambda b: (b, 0, 0, 0)),
        "n": pl.BlockSpec((tokens, 1), lambda b: (b, 0)),
    }
    shapes = {
        "T": jax.ShapeDtypeStruct((2 * tokens, heads * HEAD), F32),
        "t": jax.ShapeDtypeStruct((2 * tokens, heads * HEAD), BF16),
        "p": jax.ShapeDtypeStruct((2, heads, HEAD, HEAD), F32),
        "n": jax.ShapeDtypeStruct((2 * tokens, 1), F32),
    }
    return pl.pallas_call(
        kernel,
        grid=(2,),
        in_specs=[specs[k.lower()] for k in kinds_in],
        out_specs=[specs[k.lower()] for k in kinds_out],
        out_shape=[shapes[k] for k in kinds_out],
        cost_estimate=pl.CostEstimate(flops=flops, bytes_accessed=8 << 20, transcendentals=0),
        name=name,
    )(*args)


def chain(local, factor, reverse):
    count = lax.axis_size("row")
    entry = jnp.zeros(local.shape, BF16)
    for hop in range(count - 1):
        out = (local + factor[:, :, None, None] * entry.astype(F32)).astype(BF16)
        edge = (count - 1 - hop, count - 2 - hop) if reverse else (hop, hop + 1)
        entry = entry + lax.ppermute(out, "row", [edge])
    return entry


def other_first(value):
    return jnp.flip(pair(value), 0)


def ff_gather(w_out, w_gate, w_up, w_down):
    nx, nz, ny = [lax.axis_size(a) for a in CHIPS]
    rows = jnp.concatenate([w_out, w_gate.T, w_up.T, w_down], 0)
    part = rows.shape[1] // ny
    shard = lax.dynamic_slice_in_dim(rows, lax.axis_index("dp") * part, part, 1)
    blocks = lax.all_gather(shard, CHIPS, axis=0, tiled=True)
    hidden = rows.shape[0]
    z, y = lax.axis_index("row"), lax.axis_index("dp")
    if small_slice():
        blocks = blocks.reshape(nx, nz * ny, hidden, part)
        kz, ky = jnp.arange(nz * ny) % nz, jnp.arange(nz * ny) // nz
        tables = jnp.stack([(z ^ kz) * ny + (y ^ ky), (y ^ ky) * nz + (z ^ kz)])
        return blocks, tables.astype(jnp.int32)
    blocks = blocks.reshape(nx, nz, ny, hidden, part)
    blocks = xor_turn(xor_turn(blocks, 1, z, nz), 2, y, ny).transpose(0, 2, 1, 3, 4)
    blocks = blocks.reshape(nx, -1, HEAD // part, hidden, part).transpose(0, 1, 3, 2, 4)
    blocks = blocks.reshape(nx, -1, hidden, HEAD)
    same = jnp.arange(blocks.shape[1], dtype=jnp.int32)
    return blocks, jnp.stack([same, same])


def ff_scatter_xy(grads):
    nx, nz, ny = [lax.axis_size(a) for a in CHIPS]
    hidden = grads.shape[2]
    part = grads.shape[1] * HEAD // (nz * ny)
    if not small_slice():
        z, y = lax.axis_index("row"), lax.axis_index("dp")
        grads = grads.reshape(nx, -1, hidden, HEAD // part, part).transpose(0, 1, 3, 2, 4)
        grads = grads.reshape(nx, ny, nz, hidden, part)
        grads = xor_turn(xor_turn(grads, 1, y, ny), 2, z, nz)
    grads = grads.reshape(-1, part)
    return lax.psum_scatter(grads, ("cx", "dp"), scatter_dimension=0, tiled=True)


def out_kernel(tables, side_of, y_ref, w_ref, own, send, w_all):
    tokens, width = own.shape[0], w_ref.shape[2]
    total = 0.0
    for i in range(w_ref.shape[0]):
        x = jnp.bitwise_xor(side_of[0], i)
        blocks = [w_ref[x, tables[0, p], :, :] for p in range(w_ref.shape[1])]
        w = jnp.concatenate(blocks, 1)
        at = slice(i * width, (i + 1) * width)
        w_all[at, :] = w
        total = total + nn(y_ref[:, at], w)
    own[...] = total[:tokens]
    send[...] = total[tokens:].astype(BF16)


def project_out(y, weights, tables):
    rows, width = y.shape
    nx, blocks, _, lane = weights.shape
    model = blocks * lane
    smem = pl.BlockSpec(memory_space=pltpu.SMEM)
    whole = lambda *shape: pl.BlockSpec(shape, lambda i: (0,) * len(shape))
    return pl.pallas_call(
        out_kernel,
        grid=(1,),
        in_specs=[smem, smem, whole(rows, width), whole(nx, blocks, width // nx, lane)],
        out_specs=[whole(rows // 2, model), whole(rows // 2, model), whole(width, model)],
        out_shape=[
            jax.ShapeDtypeStruct((rows // 2, model), F32),
            jax.ShapeDtypeStruct((rows // 2, model), BF16),
            jax.ShapeDtypeStruct((width, model), BF16),
        ],
        cost_estimate=pl.CostEstimate(
            flops=2 * rows * width * model, bytes_accessed=6 << 20, transcendentals=0
        ),
        name="project_out",
    )(tables, lax.axis_index("cx").reshape(1).astype(jnp.int32), y, weights)


def ff_kernel(tables, b0, b1, g0, g1, w_ref, out, out_send, db, db_send, grads, *scratch):
    m_all, d1_all, d2_all, out_acc, db_acc = scratch
    step = pl.program_id(0)
    blocks, hidden = w_ref.shape[1], grads.shape[2] // 3
    base = w_ref.shape[2] - grads.shape[2]
    tokens = out.shape[0]

    def weight(i):
        at = slice(base + i * hidden, base + (i + 1) * hidden)
        return jnp.concatenate([w_ref[0, tables[0, p], at, :] for p in range(blocks)], 1)

    gate_w, up_w, down_w = weight(0), weight(1), weight(2)
    for half in range(2):
        rows = slice(half * tokens, (half + 1) * tokens)
        b, g = (b1[...], g1[...]) if half else (b0[...], g0[...])
        z1, z2, dm = nt(b, gate_w), nt(b, up_w), nt(g, down_w)
        m, d1, d2 = (z1 * z2).astype(BF16), (dm * z2).astype(BF16), (dm * z1).astype(BF16)
        m_all[rows, :], d1_all[rows, :], d2_all[rows, :] = m, d1, d2
        sums = nn(m, down_w), nn(d1, gate_w) + nn(d2, up_w)
        kept = (out_acc, db_acc) if half else (out, db)

        @pl.when(step == 0)
        def _():
            for ref, value in zip(kept, sums):
                ref[...] = value

        @pl.when(step != 0)
        def _():
            sent = (out_send, db_send) if half else kept
            for to, ref, value in zip(sent, kept, sums):
                to[...] = (ref[...] + value).astype(to.dtype)

    for i, (left, own, other) in enumerate(((d1_all, b0, b1), (d2_all, b0, b1), (m_all, g0, g1))):
        grad = tn(left[:tokens, :], own[...]) + tn(left[tokens:, :], other[...])
        grad = grad.astype(BF16)
        at = slice(i * hidden, (i + 1) * hidden)
        for p in range(blocks):
            grads[0, tables[1, p], at, :] = grad[:, p * HEAD : (p + 1) * HEAD]


def feed_forward(b_own, b_pair, g_own, g_pair, weights, tables, hidden):
    tokens, model = b_own.shape
    rows = 2 * tokens
    nx, blocks, height, width = weights.shape
    once = pl.Buffered(1)
    fixed = lambda n: pl.BlockSpec((n, model), lambda x: (0, 0), pipeline_mode=once)
    turn = lambda n: pl.BlockSpec((1, blocks, n, width), lambda x: (x, 0, 0, 0))
    wide = jax.ShapeDtypeStruct((tokens, model), F32)
    narrow = jax.ShapeDtypeStruct((tokens, model), BF16)
    product = pltpu.VMEM((rows, hidden), BF16)
    total = pltpu.VMEM((tokens, model), F32)
    return pl.pallas_call(
        ff_kernel,
        grid=(nx,),
        in_specs=[pl.BlockSpec(memory_space=pltpu.SMEM)] + [fixed(tokens)] * 4 + [turn(height)],
        out_specs=[fixed(tokens)] * 4 + [turn(3 * hidden)],
        out_shape=[wide, narrow, wide, narrow]
        + [jax.ShapeDtypeStruct((nx, blocks, 3 * hidden, width), BF16)],
        scratch_shapes=[product] * 3 + [total] * 2,
        compiler_params=pltpu.CompilerParams(vmem_limit_bytes=60 << 20),
        cost_estimate=pl.CostEstimate(
            flops=18 * nx * rows * model * hidden, bytes_accessed=36 << 20, transcendentals=0
        ),
        name="feed_forward",
    )(tables, b_own, b_pair, g_own, g_pair, weights)


def on_device(
    block_input,
    segments,
    decay_rate,
    w_query,
    w_key,
    w_value,
    w_output_gate,
    w_out,
    w_gate,
    w_up,
    w_down,
    out_grad,
):
    nz = lax.axis_size("row")
    col = lax.axis_index(COL)
    place = lax.axis_index("row")
    tokens = block_input.shape[2]
    model = block_input.shape[3] * lax.axis_size(COL)
    wide = w_query.shape[1]

    wk, wv, sent = gather_weights(w_key, w_value)
    w_query, w_output_gate, _ = lax.optimization_barrier((w_query, w_output_gate, sent))
    wq, wu, _ = gather_weights(w_query, w_output_gate)
    gathered, tables = ff_gather(w_out, w_gate, w_up, w_down)

    x_own, a_own, r1 = tokens_in(block_input[:, 0], True)
    rates = jnp.concatenate([decay_rate, side(decay_rate)])
    heads = rates.shape[0]
    seg_all = segments[:, 0].astype(F32)
    seg = jnp.stack(
        [
            lax.dynamic_index_in_dim(seg_all, col, 0, False),
            lax.dynamic_index_in_dim(seg_all, col ^ 1, 0, False),
        ]
    )
    last = seg[:, tokens - 1]
    before = lax.ppermute(last, "row", [(i, i + 1) for i in range(nz - 1)])
    entry_seg = jnp.where(place == 0, -1.0, before)
    linked = ((seg[:, 0] == last) & (entry_seg == last)).astype(F32)
    factor = linked[:, None] * jnp.exp(-rates * tokens)[None]
    marks = jnp.stack([last, entry_seg], 1)
    seg_c, seg_r = seg[:, :, None], seg[:, None, :]
    heads_of = functools.partial(head_call, tokens=tokens, heads=heads)
    unit = 2 * heads * 2 * tokens * tokens * HEAD

    def both(own):
        return jnp.concatenate([own, pair(own)], 0)

    def back_sum(lefts, rights, form):
        def total(rows):
            out = dot(lefts[0][rows], rights[0], form)
            for left, right in zip(lefts[1:], rights[1:]):
                out = out + dot(left[rows], right, form)
            return out

        sent = pair(total(slice(tokens, None)).astype(BF16))
        return total(slice(0, tokens)) + sent.astype(F32)

    a = both(a_own)
    zq, zk, zv, zu = [dot(a, w, "td,dc->tc") for w in (wq, wk, wv, wu)]
    zk, g_parts = lax.optimization_barrier((zk, out_grad[:, 0]))
    g_own = tokens_in(g_parts, False)
    g_pair = pair(g_own)
    k, v, local = heads_of(
        local_kernel,
        kinds_in="sscTT",
        kinds_out="ttp",
        args=(rates, marks, seg_c, zk, zv),
        flops=unit // 8,
        name="mixer_local",
    )
    q, o_inner = heads_of(
        inner_kernel,
        kinds_in="sscrTtt",
        kinds_out="tT",
        args=(rates, marks, seg_c, seg_r, zq, k, v),
        flops=unit,
        name="mixer_inner",
    )
    entry = chain(local, factor, False)
    entry, _, _ = lax.optimization_barrier((entry, g_own, g_pair))
    o, squares = heads_of(
        carry_kernel,
        kinds_in="sscTtp",
        kinds_out="Tn",
        args=(rates, marks, seg_c, o_inner, q, entry),
        flops=unit // 8,
        name="mixer_carry",
    )
    gate = jax.nn.sigmoid(zu)
    squares = squares.reshape(2, tokens)
    squares = (squares + other_first(squares)).reshape(2 * tokens, 1)
    r2 = lax.rsqrt(squares / model + EPS)
    y = (o * r2 * gate).astype(BF16)
    attended, attended_send, wo = project_out(y, gathered, tables)
    hres = x_own.astype(F32) + attended + pair(attended_send).astype(F32)
    r3 = lax.rsqrt(jnp.mean(hres * hres, 1, keepdims=True) + EPS)
    b = (hres * r3).astype(BF16)
    out, out_send, db, db_send, ff_grads = feed_forward(
        b, pair(b), g_own, g_pair, gathered, tables, w_down.shape[0]
    )
    db = db + pair(db_send).astype(F32)

    ff_part = ff_scatter_xy(ff_grads)
    dh = (
        g_own.astype(F32)
        + r3 * db
        - hres * (r3**3 * jnp.mean(db * hres, 1, keepdims=True))
    )
    dhr = both(dh.astype(BF16))

    grad_out = dot(dhr, y, "td,tc->dc").astype(BF16)
    dy = dot(dhr, wo, "td,cd->tc")
    dn = dy * gate
    dzu = (dy * o * r2 * gate * (1.0 - gate)).astype(BF16)
    dots = jnp.sum(dn * o, 1).reshape(2, tokens)
    dots = (dots + other_first(dots)).reshape(2 * tokens, 1)
    do = (r2 * dn - o * (r2**3 * dots / model)).astype(BF16)
    out_rows = (hres + out + pair(out_send).astype(F32)).astype(BF16)
    out_rows, do = lax.optimization_barrier((out_rows, do))
    block_out = tokens_out(out_rows)
    (d_entry,) = heads_of(
        entry_grad_kernel,
        kinds_in="ssctt",
        kinds_out="p",
        args=(rates, marks, seg_c, q, do),
        flops=unit // 8,
        name="mixer_entry_grad",
    )
    d_local = chain(d_entry, factor, True)
    dzq, dk, dv = heads_of(
        inner_grad_kernel,
        kinds_in="sscrttttpT",
        kinds_out="tTT",
        args=(rates, marks, seg_c, seg_r, q, k, v, do, entry, zq),
        flops=5 * unit // 2,
        name="mixer_inner_grad",
    )
    grad_u, grad_q = [dot(a, d, "td,tc->dc").astype(BF16) for d in (dzu, dzq)]
    cut = wide // 2
    early = [
        jnp.concatenate(
            [
                piece
                for x in (0, wide)
                for piece in (g[:, x : x + wide], grad_q[:, x + at : x + at + cut])
            ],
            1,
        )
        for g, at in ((grad_out, 0), (grad_u, cut))
    ]
    early = reduce_first(*early)
    *early, _ = lax.optimization_barrier((*early, d_local))
    dzk, dzv = heads_of(
        last_grad_kernel,
        kinds_in="sscttpTTT",
        kinds_out="tt",
        args=(rates, marks, seg_c, k, v, d_local, zk, dk, dv),
        flops=unit // 4,
        name="mixer_last_grad",
    )
    grad_k, grad_v = [dot(a, d, "td,tc->dc").astype(BF16) for d in (dzk, dzv)]
    da = back_sum((dzq, dzk, dzv, dzu), (wq, wk, wv, wu), "tc,dc->td")
    x_wide = x_own.astype(F32)
    input_grad = tokens_out(
        (
            dh + r1 * da - x_wide * (r1**3 * jnp.mean(da * x_wide, 1, keepdims=True))
        ).astype(BF16)
    )

    total = reduce_rest(*early)
    total_kv = reduce_rest(*reduce_first(grad_k, grad_v))
    total_q = jnp.concatenate([total[:, wide : wide + cut], total[:, 2 * wide + cut :]], 1)
    ff_part, _ = lax.optimization_barrier((ff_part, dzk))
    ff_total = lax.psum_scatter(ff_part, "row", scatter_dimension=0, tiled=True).astype(F32)
    hidden = w_down.shape[0]
    total_gate, total_up = ff_total[:hidden].T, ff_total[hidden : 2 * hidden].T
    return (
        block_out[:, None],
        input_grad[:, None],
        total_q,
        total_kv[:, :wide],
        total_kv[:, wide:],
        total[:, wide + cut : 2 * wide + cut],
        total[:, :wide].T,
        total_gate,
        total_up,
        ff_total[2 * hidden :],
    )


def solution(mesh):
    rows, cols, copies = [mesh.shape[a] for a in ("row", "col", "dp")]
    split = jax.sharding.Mesh(
        mesh.devices.reshape(rows, cols // 2, 2, copies), ("row", "cx", "cc", "dp")
    )
    placed = (
        P(None, "dp", "row", COL),
        P(None, "dp", "row"),
        P(COL),
        P("row", COL),
        P("row", COL),
        P("row", COL),
        P("row", COL),
        P(COL, "row"),
        P("row", COL),
        P("row", COL),
        P(COL, "row"),
        P(None, "dp", "row", COL),
    )
    return jax.shard_map(
        on_device,
        mesh=split,
        in_specs=placed,
        out_specs=(
            P(None, "dp", "row", COL),
            P(None, "dp", "row", COL),
            P(("row", "dp"), COL),
            P(("row", "dp"), COL),
            P(("row", "dp"), COL),
            P(("row", "dp"), COL),
            P(COL, ("row", "dp")),
            P(("row", "dp"), COL),
            P(("row", "dp"), COL),
            P(COL, ("row", "dp")),
        ),
        check_vma=False,
    )
```

```python
import functools

import jax
import jax.numpy as jnp
from jax import lax
from jax.experimental import pallas as pl
from jax.experimental.pallas import tpu as pltpu
from jax.sharding import PartitionSpec as P

HEAD = 128
TILE = 256
EPS = 1e-06
F32 = jnp.float32
BF16 = jnp.bfloat16


COL = ("cx", "cc")
CHIPS = ("cx", "row", "dp")


def swap(value, axis, bits):
    count = lax.axis_size(axis)
    return lax.ppermute(value, axis, [(i, i ^ bits) for i in range(count)])


def pair(value):
    return swap(value, COL, 1)


def side(value):
    return swap(value, COL, 2)


def bits_of(axis):
    return [1 << b for b in range(lax.axis_size(axis).bit_length() - 1)]


def xor_turn(value, dim, place, count):
    bit = 1
    while bit < count:
        shape = value.shape
        split = value.reshape(shape[:dim] + (count // (2 * bit), 2, bit) + shape[dim + 1 :])
        flipped = jnp.flip(split, dim + 1)
        value = jnp.where((place & bit) != 0, flipped, split).reshape(shape)
        bit *= 2
    return value


def to_order(rows):
    nz, ny = lax.axis_size("row"), lax.axis_size("dp")
    tokens, width = rows.shape
    split = rows.reshape(tokens, nz, ny, width // (nz * ny))
    split = xor_turn(split, 1, lax.axis_index("row"), nz)
    split = xor_turn(split, 2, lax.axis_index("dp"), ny)
    return split.transpose(0, 2, 1, 3).reshape(tokens, width)


def from_order(rows):
    nz, ny = lax.axis_size("row"), lax.axis_size("dp")
    tokens, width = rows.shape
    split = rows.reshape(tokens, ny, nz, width // (nz * ny)).transpose(0, 2, 1, 3)
    split = xor_turn(split, 1, lax.axis_index("row"), nz)
    split = xor_turn(split, 2, lax.axis_index("dp"), ny)
    return split.reshape(tokens, width)


def small_slice():
    return lax.axis_size("row") == 4 and lax.axis_size("dp") == 2


def place_bits():
    turn = lax.axis_index(COL) ^ lax.axis_index("row")
    return jnp.stack([turn & 1, turn >> 1, lax.axis_index("dp"), 0]).astype(jnp.int32)


def pick4(parts, low, high):
    first = [jnp.where(low, parts[k ^ 1], parts[k]) for k in range(4)]
    return [jnp.where(high, first[k ^ 2], first[k]) for k in range(4)]


def assemble_kernel(norm, bits, *refs):
    parts = [r[...].astype(F32) for r in refs[:4]]
    blocks = pick4(parts, bits[0] != 0, bits[1] != 0)
    odd = bits[2] != 0
    halves = [[], []]
    for b in blocks:
        low, high = b[:, :HEAD], b[:, HEAD:]
        halves[0].append(jnp.where(odd, high, low))
        halves[1].append(jnp.where(odd, low, high))
    rows = jnp.concatenate(halves[0] + halves[1], 1)
    refs[4][...] = rows.astype(BF16)
    if norm:
        scale = lax.rsqrt(jnp.mean(rows * rows, 1, keepdims=True) + EPS)
        refs[5][...] = (rows * scale).astype(BF16)
        refs[6][...] = scale


def assemble(parts, norm):
    tokens, width = parts[0].shape
    model = 4 * width
    if not small_slice():
        col = lax.axis_index(COL)
        blocks = pick4(parts, (col & 1) != 0, (col & 2) != 0)
        rows = to_order(jnp.concatenate(blocks, 1))
        if not norm:
            return rows
        wide = rows.astype(F32)
        scale = lax.rsqrt(jnp.mean(wide * wide, 1, keepdims=True) + EPS)
        return rows, (wide * scale).astype(BF16), scale
    step = 128
    row = lambda n: pl.BlockSpec((step, n), lambda i: (i, 0))
    shape = [jax.ShapeDtypeStruct((tokens, model), BF16)]
    specs = [row(model)]
    if norm:
        shape += [shape[0], jax.ShapeDtypeStruct((tokens, 1), F32)]
        specs += [row(model), row(1)]
    out = pl.pallas_call(
        functools.partial(assemble_kernel, norm),
        grid=(tokens // step,),
        in_specs=[pl.BlockSpec(memory_space=pltpu.SMEM)] + [row(width)] * 4,
        out_specs=specs,
        out_shape=shape,
        name="assemble",
    )(place_bits(), *parts)
    return out if norm else out[0]


def divide_kernel(bits, rows_ref, *refs):
    rows = rows_ref[...].astype(F32)
    odd = bits[2] != 0
    blocks = []
    for k in range(4):
        low = rows[:, k * HEAD : (k + 1) * HEAD]
        high = rows[:, (4 + k) * HEAD : (5 + k) * HEAD]
        blocks.append(
            jnp.concatenate([jnp.where(odd, high, low), jnp.where(odd, low, high)], 1)
        )
    for ref, block in zip(refs, pick4(blocks, bits[0] != 0, bits[1] != 0)):
        ref[...] = block.astype(BF16)


def divide(rows):
    tokens, model = rows.shape
    width = model // 4
    if not small_slice():
        col = lax.axis_index(COL)
        whole = from_order(rows)
        blocks = [whole[:, k * width : (k + 1) * width] for k in range(4)]
        return pick4(blocks, (col & 1) != 0, (col & 2) != 0)
    step = 128
    row = lambda n: pl.BlockSpec((step, n), lambda i: (i, 0))
    return pl.pallas_call(
        divide_kernel,
        grid=(tokens // step,),
        in_specs=[pl.BlockSpec(memory_space=pltpu.SMEM), row(model)],
        out_specs=[row(width)] * 4,
        out_shape=[jax.ShapeDtypeStruct((tokens, width), BF16)] * 4,
        name="divide",
    )(place_bits(), rows)


def tokens_in(parts, norm):
    col = lax.axis_index(COL)
    got = []
    for bits in range(4):
        mine = lax.dynamic_index_in_dim(parts, col ^ bits, 0, False)
        got.append(mine if bits == 0 else swap(mine, COL, bits))
    return assemble(got, norm)


def tokens_out(rows):
    col = lax.axis_index(COL)
    parts = divide(rows)
    got = [parts[0]] + [swap(parts[bits], COL, bits) for bits in range(1, 4)]
    return jnp.stack(pick4(got, (col & 1) != 0, (col & 2) != 0))


def gather_weights(first, second):
    ny = lax.axis_size("dp")
    part, width = first.shape[0] // ny, first.shape[1]
    value = jnp.concatenate([first, second], 1)
    value = lax.dynamic_slice_in_dim(value, lax.axis_index("dp") * part, part, 0)
    for bit in bits_of("row"):
        value = jnp.concatenate([value, swap(value, "row", bit)], 0)
    one, two = value[:, :width], value[:, width:]
    one = jnp.concatenate([one, side(one)], 1)
    for bit in bits_of("dp"):
        two = jnp.concatenate([two, swap(two, "dp", bit)], 0)
        one = jnp.concatenate([one, swap(one, "dp", bit)], 0)
    return one, jnp.concatenate([two, side(two)], 1), value


def fold(value, axis):
    for bit in reversed(bits_of(axis)):
        half = value.shape[0] // 2
        got = swap(value[half:].astype(BF16), axis, bit)
        value = value[:half].astype(F32) + got.astype(F32)
    return value


def fold_side(value):
    half = value.shape[1] // 2
    got = side(value[:, half:].astype(BF16))
    return value[:, :half].astype(F32) + got.astype(F32)


def reduce_first(one, two):
    return fold_side(one), fold(two, "dp")


def reduce_rest(one, two, after=None):
    joined = jnp.concatenate([fold(one, "dp"), fold_side(two)], 1)
    if after is not None:
        joined, _ = lax.optimization_barrier((joined, after))
    return fold(joined, "row")


def dot(left, right, form):
    return jnp.einsum(form, left, right, preferred_element_type=F32)


def nn(a, b):
    return jnp.dot(a, b, preferred_element_type=F32)


def nt(a, b):
    return lax.dot_general(a, b, (((1,), (1,)), ((), ())), preferred_element_type=F32)


def tn(a, b):
    return lax.dot_general(a, b, (((0,), (0,)), ((), ())), preferred_element_type=F32)


def silu_slope(pre):
    logistic = jax.nn.sigmoid(pre)
    return logistic * (1.0 + pre * (1.0 - logistic))


def tile_decay(rate, seg_col, seg_row, at, width):
    rows = seg_col.shape[0]
    shape = (rows, width)
    gap = lax.broadcasted_iota(jnp.int32, shape, 0) + at - lax.broadcasted_iota(jnp.int32, shape, 1)
    visible = (gap >= 0) & (seg_col == seg_row)
    return jnp.where(visible, jnp.exp(-rate * jnp.maximum(gap, 0).astype(F32)), 0.0)


def column(tokens):
    return lax.broadcasted_iota(jnp.int32, (tokens, 1), 0).astype(F32)


def own_weight(rate, seg_col, last):
    tokens = seg_col.shape[0]
    return jnp.where(seg_col == last, jnp.exp(-rate * (tokens - 1.0 - column(tokens))), 0.0)


def entry_weight(rate, seg_col, entry_seg):
    tokens = seg_col.shape[0]
    return jnp.where(seg_col == entry_seg, jnp.exp(-rate * (column(tokens) + 1.0)), 0.0)


def lanes(head):
    return slice(head * HEAD, (head + 1) * HEAD)


def local_kernel(rates, marks, seg_c, zk, zv, k_out, v_out, state):
    last = marks[pl.program_id(0), 0]
    for head in range(state.shape[1]):
        at = lanes(head)
        pre = zk[:, at]
        k, v = (pre * jax.nn.sigmoid(pre)).astype(BF16), zv[:, at].astype(BF16)
        k_out[:, at], v_out[:, at] = k, v
        weight = own_weight(rates[head], seg_c[0], last)
        state[0, head] = tn((k.astype(F32) * weight).astype(BF16), v)


def inner_kernel(rates, marks, seg_c, seg_r, zq, k_ref, v_ref, q_out, o_out):
    seg, tokens = seg_c[0], seg_c.shape[1]
    for head in range(zq.shape[1] // HEAD):
        at = lanes(head)
        pre = zq[:, at]
        q_out[:, at] = (pre * jax.nn.sigmoid(pre)).astype(BF16)
        for top in range(0, tokens, TILE):
            width = top + TILE
            decay = tile_decay(rates[head], seg[top:width], seg_r[0, :, :width], top, width)
            mix = (nt(q_out[top:width, at], k_ref[:width, at]) * decay).astype(BF16)
            o_out[top:width, at] = nn(mix, v_ref[:width, at])


def carry_kernel(rates, marks, seg_c, o_in, q, entry, o_out, squares):
    before = marks[pl.program_id(0), 1]
    total = 0.0
    for head in range(entry.shape[1]):
        at = lanes(head)
        weight = entry_weight(rates[head], seg_c[0], before)
        o = o_in[:, at] + weight * nn(q[:, at], entry[0, head])
        o_out[:, at] = o
        total = total + o * o
    squares[...] = jnp.sum(total, 1, keepdims=True)


def entry_grad_kernel(rates, marks, seg_c, q, do, grad):
    before = marks[pl.program_id(0), 1]
    for head in range(grad.shape[1]):
        at = lanes(head)
        weight = entry_weight(rates[head], seg_c[0], before)
        grad[0, head] = tn(q[:, at], (do[:, at].astype(F32) * weight).astype(BF16))


def inner_grad_kernel(
    rates, marks, seg_c, seg_r, q_ref, k_ref, v_ref, do_ref, entry, zq, dzq, dk, dv
):
    before = marks[pl.program_id(0), 1]
    seg, tokens = seg_c[0], seg_c.shape[1]
    for head in range(entry.shape[1]):
        at = lanes(head)
        weight = entry_weight(rates[head], seg, before)
        for top in range(0, tokens, TILE):
            width = top + TILE
            q, do = q_ref[top:width, at], do_ref[top:width, at]
            k, v = k_ref[:width, at], v_ref[:width, at]
            decay = tile_decay(rates[head], seg[top:width], seg_r[0, :, :width], top, width)
            mix = (nt(q, k) * decay).astype(BF16)
            ds = (nt(do, v) * decay).astype(BF16)
            scaled = (do.astype(F32) * weight[top:width]).astype(BF16)
            dq = nn(ds, k) + nt(scaled, entry[0, head])
            dzq[top:width, at] = (dq * silu_slope(zq[top:width, at])).astype(BF16)
            dk_new, dv_new = tn(ds, q), tn(mix, do)
            if top:
                dk[:top, at] += dk_new[:top]
                dv[:top, at] += dv_new[:top]
            dk[top:width, at] = dk_new[top:]
            dv[top:width, at] = dv_new[top:]


def last_grad_kernel(rates, marks, seg_c, k, v, d_state, zk, dk, dv, dzk, dzv):
    last = marks[pl.program_id(0), 0]
    for head in range(d_state.shape[1]):
        at = lanes(head)
        weight = own_weight(rates[head], seg_c[0], last)
        state = d_state[0, head]
        dk_all = dk[:, at] + weight * nt(v[:, at], state)
        dzk[:, at] = (dk_all * silu_slope(zk[:, at])).astype(BF16)
        scaled = (k[:, at].astype(F32) * weight).astype(BF16)
        dzv[:, at] = (dv[:, at] + nn(scaled, state)).astype(BF16)


def head_call(kernel, tokens, heads, kinds_in, kinds_out, args, flops, name):
    specs = {
        "s": pl.BlockSpec(memory_space=pltpu.SMEM),
        "c": pl.BlockSpec((1, tokens, 1), lambda b: (b, 0, 0)),
        "r": pl.BlockSpec((1, 1, tokens), lambda b: (b, 0, 0)),
        "t": pl.BlockSpec((tokens, heads * HEAD), lambda b: (b, 0)),
        "p": pl.BlockSpec((1, heads, HEAD, HEAD), lambda b: (b, 0, 0, 0)),
        "n": pl.BlockSpec((tokens, 1), lambda b: (b, 0)),
    }
    shapes = {
        "T": jax.ShapeDtypeStruct((2 * tokens, heads * HEAD), F32),
        "t": jax.ShapeDtypeStruct((2 * tokens, heads * HEAD), BF16),
        "p": jax.ShapeDtypeStruct((2, heads, HEAD, HEAD), F32),
        "n": jax.ShapeDtypeStruct((2 * tokens, 1), F32),
    }
    return pl.pallas_call(
        kernel,
        grid=(2,),
        in_specs=[specs[k.lower()] for k in kinds_in],
        out_specs=[specs[k.lower()] for k in kinds_out],
        out_shape=[shapes[k] for k in kinds_out],
        cost_estimate=pl.CostEstimate(flops=flops, bytes_accessed=8 << 20, transcendentals=0),
        name=name,
    )(*args)


def chain(local, factor, reverse):
    count = lax.axis_size("row")
    entry = jnp.zeros(local.shape, BF16)
    for hop in range(count - 1):
        out = (local + factor[:, :, None, None] * entry.astype(F32)).astype(BF16)
        edge = (count - 1 - hop, count - 2 - hop) if reverse else (hop, hop + 1)
        entry = entry + lax.ppermute(out, "row", [edge])
    return entry


def other_first(value):
    return jnp.flip(pair(value), 0)


def ff_gather(w_out, w_gate, w_up, w_down):
    nx, nz, ny = [lax.axis_size(a) for a in CHIPS]
    rows = jnp.concatenate([w_out, w_gate.T, w_up.T, w_down], 0)
    part = rows.shape[1] // ny
    shard = lax.dynamic_slice_in_dim(rows, lax.axis_index("dp") * part, part, 1)
    blocks = lax.all_gather(shard, CHIPS, axis=0, tiled=True)
    hidden = rows.shape[0]
    z, y = lax.axis_index("row"), lax.axis_index("dp")
    if small_slice():
        blocks = blocks.reshape(nx, nz * ny, hidden, part)
        kz, ky = jnp.arange(nz * ny) % nz, jnp.arange(nz * ny) // nz
        tables = jnp.stack([(z ^ kz) * ny + (y ^ ky), (y ^ ky) * nz + (z ^ kz)])
        return blocks, tables.astype(jnp.int32)
    blocks = blocks.reshape(nx, nz, ny, hidden, part)
    blocks = xor_turn(xor_turn(blocks, 1, z, nz), 2, y, ny).transpose(0, 2, 1, 3, 4)
    blocks = blocks.reshape(nx, -1, HEAD // part, hidden, part).transpose(0, 1, 3, 2, 4)
    blocks = blocks.reshape(nx, -1, hidden, HEAD)
    same = jnp.arange(blocks.shape[1], dtype=jnp.int32)
    return blocks, jnp.stack([same, same])


def ff_scatter_xy(grads):
    nx, nz, ny = [lax.axis_size(a) for a in CHIPS]
    hidden = grads.shape[2]
    part = grads.shape[1] * HEAD // (nz * ny)
    if not small_slice():
        z, y = lax.axis_index("row"), lax.axis_index("dp")
        grads = grads.reshape(nx, -1, hidden, HEAD // part, part).transpose(0, 1, 3, 2, 4)
        grads = grads.reshape(nx, ny, nz, hidden, part)
        grads = xor_turn(xor_turn(grads, 1, y, ny), 2, z, nz)
    grads = grads.reshape(-1, part)
    return lax.psum_scatter(grads, ("cx", "dp"), scatter_dimension=0, tiled=True)


def out_kernel(tables, side_of, y_ref, w_ref, own, send, w_all):
    tokens, width = own.shape[0], w_ref.shape[2]
    total = 0.0
    for i in range(w_ref.shape[0]):
        x = jnp.bitwise_xor(side_of[0], i)
        blocks = [w_ref[x, tables[0, p], :, :] for p in range(w_ref.shape[1])]
        w = jnp.concatenate(blocks, 1)
        at = slice(i * width, (i + 1) * width)
        w_all[at, :] = w
        total = total + nn(y_ref[:, at], w)
    own[...] = total[:tokens]
    send[...] = total[tokens:].astype(BF16)


def project_out(y, weights, tables):
    rows, width = y.shape
    nx, blocks, _, lane = weights.shape
    model = blocks * lane
    smem = pl.BlockSpec(memory_space=pltpu.SMEM)
    whole = lambda *shape: pl.BlockSpec(shape, lambda i: (0,) * len(shape))
    return pl.pallas_call(
        out_kernel,
        grid=(1,),
        in_specs=[smem, smem, whole(rows, width), whole(nx, blocks, width // nx, lane)],
        out_specs=[whole(rows // 2, model), whole(rows // 2, model), whole(width, model)],
        out_shape=[
            jax.ShapeDtypeStruct((rows // 2, model), F32),
            jax.ShapeDtypeStruct((rows // 2, model), BF16),
            jax.ShapeDtypeStruct((width, model), BF16),
        ],
        cost_estimate=pl.CostEstimate(
            flops=2 * rows * width * model, bytes_accessed=6 << 20, transcendentals=0
        ),
        name="project_out",
    )(tables, lax.axis_index("cx").reshape(1).astype(jnp.int32), y, weights)


def ff_kernel(tables, b0, b1, g0, g1, w_ref, out, out_send, db, db_send, grads, *scratch):
    m_all, d1_all, d2_all, out_acc, db_acc = scratch
    step = pl.program_id(0)
    blocks, hidden = w_ref.shape[1], grads.shape[2] // 3
    base = w_ref.shape[2] - grads.shape[2]
    tokens = out.shape[0]

    def weight(i):
        at = slice(base + i * hidden, base + (i + 1) * hidden)
        return jnp.concatenate([w_ref[0, tables[0, p], at, :] for p in range(blocks)], 1)

    gate_w, up_w, down_w = weight(0), weight(1), weight(2)
    for half in range(2):
        rows = slice(half * tokens, (half + 1) * tokens)
        b, g = (b1[...], g1[...]) if half else (b0[...], g0[...])
        z1, z2, dm = nt(b, gate_w), nt(b, up_w), nt(g, down_w)
        m, d1, d2 = (z1 * z2).astype(BF16), (dm * z2).astype(BF16), (dm * z1).astype(BF16)
        m_all[rows, :], d1_all[rows, :], d2_all[rows, :] = m, d1, d2
        sums = nn(m, down_w), nn(d1, gate_w) + nn(d2, up_w)
        kept = (out_acc, db_acc) if half else (out, db)

        @pl.when(step == 0)
        def _():
            for ref, value in zip(kept, sums):
                ref[...] = value

        @pl.when(step != 0)
        def _():
            sent = (out_send, db_send) if half else kept
            for to, ref, value in zip(sent, kept, sums):
                to[...] = (ref[...] + value).astype(to.dtype)

    for i, (left, own, other) in enumerate(((d1_all, b0, b1), (d2_all, b0, b1), (m_all, g0, g1))):
        grad = tn(left[:tokens, :], own[...]) + tn(left[tokens:, :], other[...])
        grad = grad.astype(BF16)
        at = slice(i * hidden, (i + 1) * hidden)
        for p in range(blocks):
            grads[0, tables[1, p], at, :] = grad[:, p * HEAD : (p + 1) * HEAD]


def feed_forward(b_own, b_pair, g_own, g_pair, weights, tables, hidden):
    tokens, model = b_own.shape
    rows = 2 * tokens
    nx, blocks, height, width = weights.shape
    once = pl.Buffered(1)
    fixed = lambda n: pl.BlockSpec((n, model), lambda x: (0, 0), pipeline_mode=once)
    turn = lambda n: pl.BlockSpec((1, blocks, n, width), lambda x: (x, 0, 0, 0))
    wide = jax.ShapeDtypeStruct((tokens, model), F32)
    narrow = jax.ShapeDtypeStruct((tokens, model), BF16)
    product = pltpu.VMEM((rows, hidden), BF16)
    total = pltpu.VMEM((tokens, model), F32)
    return pl.pallas_call(
        ff_kernel,
        grid=(nx,),
        in_specs=[pl.BlockSpec(memory_space=pltpu.SMEM)] + [fixed(tokens)] * 4 + [turn(height)],
        out_specs=[fixed(tokens)] * 4 + [turn(3 * hidden)],
        out_shape=[wide, narrow, wide, narrow]
        + [jax.ShapeDtypeStruct((nx, blocks, 3 * hidden, width), BF16)],
        scratch_shapes=[product] * 3 + [total] * 2,
        compiler_params=pltpu.CompilerParams(vmem_limit_bytes=60 << 20),
        cost_estimate=pl.CostEstimate(
            flops=18 * nx * rows * model * hidden, bytes_accessed=36 << 20, transcendentals=0
        ),
        name="feed_forward",
    )(tables, b_own, b_pair, g_own, g_pair, weights)


def on_device(
    block_input,
    segments,
    decay_rate,
    w_query,
    w_key,
    w_value,
    w_output_gate,
    w_out,
    w_gate,
    w_up,
    w_down,
    out_grad,
):
    nz = lax.axis_size("row")
    col = lax.axis_index(COL)
    place = lax.axis_index("row")
    tokens = block_input.shape[2]
    model = block_input.shape[3] * lax.axis_size(COL)
    wide = w_query.shape[1]

    wk, wv, sent = gather_weights(w_key, w_value)
    w_query, w_output_gate, _ = lax.optimization_barrier((w_query, w_output_gate, sent))
    wq, wu, _ = gather_weights(w_query, w_output_gate)
    gathered, tables = ff_gather(w_out, w_gate, w_up, w_down)

    x_own, a_own, r1 = tokens_in(block_input[:, 0], True)
    rates = jnp.concatenate([decay_rate, side(decay_rate)])
    heads = rates.shape[0]
    seg_all = segments[:, 0].astype(F32)
    seg = jnp.stack(
        [
            lax.dynamic_index_in_dim(seg_all, col, 0, False),
            lax.dynamic_index_in_dim(seg_all, col ^ 1, 0, False),
        ]
    )
    last = seg[:, tokens - 1]
    before = lax.ppermute(last, "row", [(i, i + 1) for i in range(nz - 1)])
    entry_seg = jnp.where(place == 0, -1.0, before)
    linked = ((seg[:, 0] == last) & (entry_seg == last)).astype(F32)
    factor = linked[:, None] * jnp.exp(-rates * tokens)[None]
    marks = jnp.stack([last, entry_seg], 1)
    seg_c, seg_r = seg[:, :, None], seg[:, None, :]
    heads_of = functools.partial(head_call, tokens=tokens, heads=heads)
    unit = 2 * heads * 2 * tokens * tokens * HEAD

    def both(own):
        return jnp.concatenate([own, pair(own)], 0)

    def back_sum(lefts, rights, form):
        def total(rows):
            out = dot(lefts[0][rows], rights[0], form)
            for left, right in zip(lefts[1:], rights[1:]):
                out = out + dot(left[rows], right, form)
            return out

        sent = pair(total(slice(tokens, None)).astype(BF16))
        return total(slice(0, tokens)) + sent.astype(F32)

    a = both(a_own)
    zq, zk, zv, zu = [dot(a, w, "td,dc->tc") for w in (wq, wk, wv, wu)]
    zk, g_parts = lax.optimization_barrier((zk, out_grad[:, 0]))
    g_own = tokens_in(g_parts, False)
    g_pair = pair(g_own)
    k, v, local = heads_of(
        local_kernel,
        kinds_in="sscTT",
        kinds_out="ttp",
        args=(rates, marks, seg_c, zk, zv),
        flops=unit // 8,
        name="mixer_local",
    )
    q, o_inner = heads_of(
        inner_kernel,
        kinds_in="sscrTtt",
        kinds_out="tT",
        args=(rates, marks, seg_c, seg_r, zq, k, v),
        flops=unit,
        name="mixer_inner",
    )
    entry = chain(local, factor, False)
    entry, _, _ = lax.optimization_barrier((entry, g_own, g_pair))
    o, squares = heads_of(
        carry_kernel,
        kinds_in="sscTtp",
        kinds_out="Tn",
        args=(rates, marks, seg_c, o_inner, q, entry),
        flops=unit // 8,
        name="mixer_carry",
    )
    gate = jax.nn.sigmoid(zu)
    squares = squares.reshape(2, tokens)
    squares = (squares + other_first(squares)).reshape(2 * tokens, 1)
    r2 = lax.rsqrt(squares / model + EPS)
    y = (o * r2 * gate).astype(BF16)
    attended, attended_send, wo = project_out(y, gathered, tables)
    hres = x_own.astype(F32) + attended + pair(attended_send).astype(F32)
    r3 = lax.rsqrt(jnp.mean(hres * hres, 1, keepdims=True) + EPS)
    b = (hres * r3).astype(BF16)
    out, out_send, db, db_send, ff_grads = feed_forward(
        b, pair(b), g_own, g_pair, gathered, tables, w_down.shape[0]
    )
    db = db + pair(db_send).astype(F32)

    ff_part = ff_scatter_xy(ff_grads)
    dh = (
        g_own.astype(F32)
        + r3 * db
        - hres * (r3**3 * jnp.mean(db * hres, 1, keepdims=True))
    )
    dhr = both(dh.astype(BF16))

    grad_out = dot(dhr, y, "td,tc->dc").astype(BF16)
    dy = dot(dhr, wo, "td,cd->tc")
    dn = dy * gate
    dzu = (dy * o * r2 * gate * (1.0 - gate)).astype(BF16)
    dots = jnp.sum(dn * o, 1).reshape(2, tokens)
    dots = (dots + other_first(dots)).reshape(2 * tokens, 1)
    do = (r2 * dn - o * (r2**3 * dots / model)).astype(BF16)
    out_rows = (hres + out + pair(out_send).astype(F32)).astype(BF16)
    (d_entry,) = heads_of(
        entry_grad_kernel,
        kinds_in="ssctt",
        kinds_out="p",
        args=(rates, marks, seg_c, q, do),
        flops=unit // 8,
        name="mixer_entry_grad",
    )
    d_local = chain(d_entry, factor, True)
    dzq, dk, dv = heads_of(
        inner_grad_kernel,
        kinds_in="sscrttttpT",
        kinds_out="tTT",
        args=(rates, marks, seg_c, seg_r, q, k, v, do, entry, zq),
        flops=5 * unit // 2,
        name="mixer_inner_grad",
    )
    grad_u, grad_q = [dot(a, d, "td,tc->dc").astype(BF16) for d in (dzu, dzq)]
    cut = wide // 2
    early = [
        jnp.concatenate(
            [
                piece
                for x in (0, wide)
                for piece in (g[:, x : x + wide], grad_q[:, x + at : x + at + cut])
            ],
            1,
        )
        for g, at in ((grad_out, 0), (grad_u, cut))
    ]
    early = reduce_first(*early)
    *early, _ = lax.optimization_barrier((*early, d_local))
    dzk, dzv = heads_of(
        last_grad_kernel,
        kinds_in="sscttpTTT",
        kinds_out="tt",
        args=(rates, marks, seg_c, k, v, d_local, zk, dk, dv),
        flops=unit // 4,
        name="mixer_last_grad",
    )
    grad_k, grad_v = [dot(a, d, "td,tc->dc").astype(BF16) for d in (dzk, dzv)]
    da = back_sum((dzq, dzk, dzv, dzu), (wq, wk, wv, wu), "tc,dc->td")
    x_wide = x_own.astype(F32)
    in_rows = (
        dh + r1 * da - x_wide * (r1**3 * jnp.mean(da * x_wide, 1, keepdims=True))
    ).astype(BF16)
    input_grad = tokens_out(in_rows)
    out_rows, _ = lax.optimization_barrier((out_rows, dzk))
    block_out = tokens_out(out_rows)

    total = reduce_rest(*early)
    grad_k, grad_v, ff_part = lax.optimization_barrier((grad_k, grad_v, ff_part))
    total_kv = reduce_rest(*reduce_first(grad_k, grad_v), in_rows)
    total_q = jnp.concatenate([total[:, wide : wide + cut], total[:, 2 * wide + cut :]], 1)
    ff_total = lax.psum_scatter(ff_part, "row", scatter_dimension=0, tiled=True).astype(F32)
    hidden = w_down.shape[0]
    total_gate, total_up = ff_total[:hidden].T, ff_total[hidden : 2 * hidden].T
    return (
        block_out[:, None],
        input_grad[:, None],
        total_q,
        total_kv[:, :wide],
        total_kv[:, wide:],
        total[:, wide + cut : 2 * wide + cut],
        total[:, :wide].T,
        total_gate,
        total_up,
        ff_total[2 * hidden :],
    )


def solution(mesh):
    rows, cols, copies = [mesh.shape[a] for a in ("row", "col", "dp")]
    split = jax.sharding.Mesh(
        mesh.devices.reshape(rows, cols // 2, 2, copies), ("row", "cx", "cc", "dp")
    )
    placed = (
        P(None, "dp", "row", COL),
        P(None, "dp", "row"),
        P(COL),
        P("row", COL),
        P("row", COL),
        P("row", COL),
        P("row", COL),
        P(COL, "row"),
        P("row", COL),
        P("row", COL),
        P(COL, "row"),
        P(None, "dp", "row", COL),
    )
    return jax.shard_map(
        on_device,
        mesh=split,
        in_specs=placed,
        out_specs=(
            P(None, "dp", "row", COL),
            P(None, "dp", "row", COL),
            P(("row", "dp"), COL),
            P(("row", "dp"), COL),
            P(("row", "dp"), COL),
            P(("row", "dp"), COL),
            P(COL, ("row", "dp")),
            P(("row", "dp"), COL),
            P(("row", "dp"), COL),
            P(COL, ("row", "dp")),
        ),
        check_vma=False,
    )
```

```python
import functools

import jax
import jax.numpy as jnp
from jax import lax
from jax.experimental import pallas as pl
from jax.experimental.pallas import tpu as pltpu
from jax.sharding import PartitionSpec as P

HEAD = 128
TILE = 256
EPS = 1e-06
F32 = jnp.float32
BF16 = jnp.bfloat16


COL = ("cx", "cc")
CHIPS = ("cx", "row", "dp")


def swap(value, axis, bits):
    count = lax.axis_size(axis)
    return lax.ppermute(value, axis, [(i, i ^ bits) for i in range(count)])


def pair(value):
    return swap(value, COL, 1)


def side(value):
    return swap(value, COL, 2)


def bits_of(axis):
    return [1 << b for b in range(lax.axis_size(axis).bit_length() - 1)]


def row_places():
    count = lax.axis_size("row")
    places = [0]
    for bit in reversed(bits_of("row")):
        places = places + [p | bit for p in places]
    assert len(places) == count
    return places


def reorder(value, dim):
    take = lambda p: lax.slice_in_dim(value, p, p + 1, axis=dim)
    return jnp.concatenate([take(p) for p in row_places()], dim)


def xor_turn(value, dim, place, count):
    bit = 1
    while bit < count:
        shape = value.shape
        split = value.reshape(shape[:dim] + (count // (2 * bit), 2, bit) + shape[dim + 1 :])
        flipped = jnp.flip(split, dim + 1)
        value = jnp.where((place & bit) != 0, flipped, split).reshape(shape)
        bit *= 2
    return value


def to_order(rows):
    nz, ny = lax.axis_size("row"), lax.axis_size("dp")
    tokens, width = rows.shape
    split = rows.reshape(tokens, nz, ny, width // (nz * ny))
    split = xor_turn(split, 1, lax.axis_index("row"), nz)
    split = reorder(xor_turn(split, 2, lax.axis_index("dp"), ny), 1)
    return split.transpose(0, 2, 1, 3).reshape(tokens, width)


def from_order(rows):
    nz, ny = lax.axis_size("row"), lax.axis_size("dp")
    tokens, width = rows.shape
    split = rows.reshape(tokens, ny, nz, width // (nz * ny)).transpose(0, 2, 1, 3)
    split = reorder(split, 1)
    split = xor_turn(split, 1, lax.axis_index("row"), nz)
    split = xor_turn(split, 2, lax.axis_index("dp"), ny)
    return split.reshape(tokens, width)


def small_slice():
    return lax.axis_size("row") == 4 and lax.axis_size("dp") == 2


def place_bits():
    turn = lax.axis_index(COL) ^ lax.axis_index("row")
    return jnp.stack([turn & 1, turn >> 1, lax.axis_index("dp"), 0]).astype(jnp.int32)


def pick4(parts, low, high):
    first = [jnp.where(low, parts[k ^ 1], parts[k]) for k in range(4)]
    return [jnp.where(high, first[k ^ 2], first[k]) for k in range(4)]


def assemble_kernel(norm, places, bits, *refs):
    parts = [r[...].astype(F32) for r in refs[:4]]
    blocks = pick4(parts, bits[0] != 0, bits[1] != 0)
    odd = bits[2] != 0
    halves = [[], []]
    for b in blocks:
        low, high = b[:, :HEAD], b[:, HEAD:]
        halves[0].append(jnp.where(odd, high, low))
        halves[1].append(jnp.where(odd, low, high))
    rows = jnp.concatenate([half[k] for half in halves for k in places], 1)
    refs[4][...] = rows.astype(BF16)
    if norm:
        scale = lax.rsqrt(jnp.mean(rows * rows, 1, keepdims=True) + EPS)
        refs[5][...] = (rows * scale).astype(BF16)
        refs[6][...] = scale


def assemble(parts, norm):
    tokens, width = parts[0].shape
    model = 4 * width
    if not small_slice():
        col = lax.axis_index(COL)
        blocks = pick4(parts, (col & 1) != 0, (col & 2) != 0)
        rows = to_order(jnp.concatenate(blocks, 1))
        if not norm:
            return rows
        wide = rows.astype(F32)
        scale = lax.rsqrt(jnp.mean(wide * wide, 1, keepdims=True) + EPS)
        return rows, (wide * scale).astype(BF16), scale
    step = 128
    row = lambda n: pl.BlockSpec((step, n), lambda i: (i, 0))
    shape = [jax.ShapeDtypeStruct((tokens, model), BF16)]
    specs = [row(model)]
    if norm:
        shape += [shape[0], jax.ShapeDtypeStruct((tokens, 1), F32)]
        specs += [row(model), row(1)]
    out = pl.pallas_call(
        functools.partial(assemble_kernel, norm, row_places()),
        grid=(tokens // step,),
        in_specs=[pl.BlockSpec(memory_space=pltpu.SMEM)] + [row(width)] * 4,
        out_specs=specs,
        out_shape=shape,
        name="assemble",
    )(place_bits(), *parts)
    return out if norm else out[0]


def divide_kernel(places, bits, rows_ref, *refs):
    rows = rows_ref[...].astype(F32)
    odd = bits[2] != 0
    blocks = []
    for k in places:
        low = rows[:, k * HEAD : (k + 1) * HEAD]
        high = rows[:, (4 + k) * HEAD : (5 + k) * HEAD]
        blocks.append(
            jnp.concatenate([jnp.where(odd, high, low), jnp.where(odd, low, high)], 1)
        )
    parts = pick4(blocks, bits[0] != 0, bits[1] != 0)
    for ref, pieces in zip(refs, (parts[:2], parts[2:])):
        ref[...] = jnp.concatenate(pieces, 1).astype(BF16)


def divide(rows):
    tokens, model = rows.shape
    width = model // 4
    if not small_slice():
        col = lax.axis_index(COL)
        whole = from_order(rows)
        blocks = [whole[:, k * width : (k + 1) * width] for k in range(4)]
        parts = pick4(blocks, (col & 1) != 0, (col & 2) != 0)
        return jnp.concatenate(parts[:2], 1), jnp.concatenate(parts[2:], 1)
    step = 256
    row = lambda n: pl.BlockSpec((step, n), lambda i: (i, 0))
    return pl.pallas_call(
        functools.partial(divide_kernel, row_places()),
        grid=(tokens // step,),
        in_specs=[pl.BlockSpec(memory_space=pltpu.SMEM), row(model)],
        out_specs=[row(2 * width)] * 2,
        out_shape=[jax.ShapeDtypeStruct((tokens, 2 * width), BF16)] * 2,
        name="divide",
    )(place_bits(), rows)


def tokens_in(parts, norm):
    col = lax.axis_index(COL)
    got = []
    for bits in range(4):
        mine = lax.dynamic_index_in_dim(parts, col ^ bits, 0, False)
        got.append(mine if bits == 0 else swap(mine, COL, bits))
    return assemble(got, norm)


def tokens_out(divided):
    col = lax.axis_index(COL)
    near, far = divided
    width = near.shape[1] // 2
    far = side(far)
    mine = near[:, :width]
    near = pair(jnp.concatenate([near[:, width:], far[:, width:]], 1))
    got = [mine, near[:, :width], far[:, :width], near[:, width:]]
    return jnp.stack(pick4(got, (col & 1) != 0, (col & 2) != 0))


def gather_weights(first, second):
    ny = lax.axis_size("dp")
    part, width = first.shape[0] // ny, first.shape[1]
    value = jnp.concatenate([first, second], 1)
    value = lax.dynamic_slice_in_dim(value, lax.axis_index("dp") * part, part, 0)
    for bit in reversed(bits_of("row")):
        value = jnp.concatenate([value, swap(value, "row", bit)], 0)
    one, two = value[:, :width], value[:, width:]
    one = jnp.concatenate([one, side(one)], 1)
    for bit in bits_of("dp"):
        two = jnp.concatenate([two, swap(two, "dp", bit)], 0)
        one = jnp.concatenate([one, swap(one, "dp", bit)], 0)
    return one, jnp.concatenate([two, side(two)], 1), value


def held(value, after):
    return value if after is None else lax.optimization_barrier((value, after))[0]


def fold(value, axis, after=None, bits=None):
    if bits is None:
        bits = bits_of(axis) if axis == "row" else reversed(bits_of(axis))
    for bit in bits:
        half = value.shape[0] // 2
        got = held(swap(value[half:].astype(BF16), axis, bit), after)
        value = value[:half].astype(F32) + got.astype(F32)
    return value


def fold_side(value, after=None):
    half = value.shape[1] // 2
    got = held(side(value[:, half:].astype(BF16)), after)
    return value[:, :half].astype(F32) + got.astype(F32)


def reduce_first(one, two, after):
    return fold_side(one, after), fold(two, "dp", after)


def reduce_second(one, two, after=None):
    return jnp.concatenate([fold(one, "dp", after), fold_side(two, after)], 1)


def dot(left, right, form):
    return jnp.einsum(form, left, right, preferred_element_type=F32)


def nn(a, b):
    return jnp.dot(a, b, preferred_element_type=F32)


def nt(a, b):
    return lax.dot_general(a, b, (((1,), (1,)), ((), ())), preferred_element_type=F32)


def tn(a, b):
    return lax.dot_general(a, b, (((0,), (0,)), ((), ())), preferred_element_type=F32)


def silu_slope(pre):
    logistic = jax.nn.sigmoid(pre)
    return logistic * (1.0 + pre * (1.0 - logistic))


def tile_decay(rate, seg_col, seg_row, at, width):
    rows = seg_col.shape[0]
    shape = (rows, width)
    gap = lax.broadcasted_iota(jnp.int32, shape, 0) + at - lax.broadcasted_iota(jnp.int32, shape, 1)
    visible = (gap >= 0) & (seg_col == seg_row)
    return jnp.where(visible, jnp.exp(-rate * jnp.maximum(gap, 0).astype(F32)), 0.0)


def column(tokens):
    return lax.broadcasted_iota(jnp.int32, (tokens, 1), 0).astype(F32)


def own_weight(rate, seg_col, last):
    tokens = seg_col.shape[0]
    return jnp.where(seg_col == last, jnp.exp(-rate * (tokens - 1.0 - column(tokens))), 0.0)


def entry_weight(rate, seg_col, entry_seg):
    tokens = seg_col.shape[0]
    return jnp.where(seg_col == entry_seg, jnp.exp(-rate * (column(tokens) + 1.0)), 0.0)


def lanes(head):
    return slice(head * HEAD, (head + 1) * HEAD)


def local_kernel(rates, marks, seg_c, zk, zv, k_out, v_out, state):
    last = marks[pl.program_id(0), 0]
    for head in range(state.shape[1]):
        at = lanes(head)
        pre = zk[:, at]
        k, v = (pre * jax.nn.sigmoid(pre)).astype(BF16), zv[:, at].astype(BF16)
        k_out[:, at], v_out[:, at] = k, v
        weight = own_weight(rates[head], seg_c[0], last)
        state[0, head] = tn((k.astype(F32) * weight).astype(BF16), v)


def inner_kernel(rates, marks, seg_c, seg_r, zq, k_ref, v_ref, q_out, o_out):
    seg, tokens = seg_c[0], seg_c.shape[1]
    for head in range(zq.shape[1] // HEAD):
        at = lanes(head)
        pre = zq[:, at]
        q_out[:, at] = (pre * jax.nn.sigmoid(pre)).astype(BF16)
        for top in range(0, tokens, TILE):
            width = top + TILE
            decay = tile_decay(rates[head], seg[top:width], seg_r[0, :, :width], top, width)
            mix = (nt(q_out[top:width, at], k_ref[:width, at]) * decay).astype(BF16)
            o_out[top:width, at] = nn(mix, v_ref[:width, at])


def carry_kernel(rates, marks, seg_c, o_in, q, entry, o_out, squares):
    before = marks[pl.program_id(0), 1]
    total = 0.0
    for head in range(entry.shape[1]):
        at = lanes(head)
        weight = entry_weight(rates[head], seg_c[0], before)
        o = o_in[:, at] + weight * nn(q[:, at], entry[0, head])
        o_out[:, at] = o
        total = total + o * o
    squares[...] = jnp.sum(total, 1, keepdims=True)


def entry_grad_kernel(rates, marks, seg_c, q, do, grad):
    before = marks[pl.program_id(0), 1]
    for head in range(grad.shape[1]):
        at = lanes(head)
        weight = entry_weight(rates[head], seg_c[0], before)
        grad[0, head] = tn(q[:, at], (do[:, at].astype(F32) * weight).astype(BF16))


def inner_grad_kernel(
    rates, marks, seg_c, seg_r, q_ref, k_ref, v_ref, do_ref, entry, zq, dzq, dk, dv
):
    before = marks[pl.program_id(0), 1]
    seg, tokens = seg_c[0], seg_c.shape[1]
    for head in range(entry.shape[1]):
        at = lanes(head)
        weight = entry_weight(rates[head], seg, before)
        for top in range(0, tokens, TILE):
            width = top + TILE
            q, do = q_ref[top:width, at], do_ref[top:width, at]
            k, v = k_ref[:width, at], v_ref[:width, at]
            decay = tile_decay(rates[head], seg[top:width], seg_r[0, :, :width], top, width)
            mix = (nt(q, k) * decay).astype(BF16)
            ds = (nt(do, v) * decay).astype(BF16)
            scaled = (do.astype(F32) * weight[top:width]).astype(BF16)
            dq = nn(ds, k) + nt(scaled, entry[0, head])
            dzq[top:width, at] = (dq * silu_slope(zq[top:width, at])).astype(BF16)
            dk_new, dv_new = tn(ds, q), tn(mix, do)
            if top:
                dk[:top, at] += dk_new[:top]
                dv[:top, at] += dv_new[:top]
            dk[top:width, at] = dk_new[top:]
            dv[top:width, at] = dv_new[top:]


def last_grad_kernel(rates, marks, seg_c, k, v, d_state, zk, dk, dv, dzk, dzv):
    last = marks[pl.program_id(0), 0]
    for head in range(d_state.shape[1]):
        at = lanes(head)
        weight = own_weight(rates[head], seg_c[0], last)
        state = d_state[0, head]
        dk_all = dk[:, at] + weight * nt(v[:, at], state)
        dzk[:, at] = (dk_all * silu_slope(zk[:, at])).astype(BF16)
        scaled = (k[:, at].astype(F32) * weight).astype(BF16)
        dzv[:, at] = (dv[:, at] + nn(scaled, state)).astype(BF16)


def head_call(kernel, tokens, heads, kinds_in, kinds_out, args, flops, name):
    specs = {
        "s": pl.BlockSpec(memory_space=pltpu.SMEM),
        "c": pl.BlockSpec((1, tokens, 1), lambda b: (b, 0, 0)),
        "r": pl.BlockSpec((1, 1, tokens), lambda b: (b, 0, 0)),
        "t": pl.BlockSpec((tokens, heads * HEAD), lambda b: (b, 0)),
        "p": pl.BlockSpec((1, heads, HEAD, HEAD), lambda b: (b, 0, 0, 0)),
        "n": pl.BlockSpec((tokens, 1), lambda b: (b, 0)),
    }
    shapes = {
        "T": jax.ShapeDtypeStruct((2 * tokens, heads * HEAD), F32),
        "t": jax.ShapeDtypeStruct((2 * tokens, heads * HEAD), BF16),
        "p": jax.ShapeDtypeStruct((2, heads, HEAD, HEAD), F32),
        "n": jax.ShapeDtypeStruct((2 * tokens, 1), F32),
    }
    return pl.pallas_call(
        kernel,
        grid=(2,),
        in_specs=[specs[k.lower()] for k in kinds_in],
        out_specs=[specs[k.lower()] for k in kinds_out],
        out_shape=[shapes[k] for k in kinds_out],
        cost_estimate=pl.CostEstimate(flops=flops, bytes_accessed=8 << 20, transcendentals=0),
        name=name,
    )(*args)


def chain(local, factor, reverse):
    count = lax.axis_size("row")
    entry = jnp.zeros(local.shape, BF16)
    for hop in range(count - 1):
        out = (local + factor[:, :, None, None] * entry.astype(F32)).astype(BF16)
        edge = (count - 1 - hop, count - 2 - hop) if reverse else (hop, hop + 1)
        entry = entry + lax.ppermute(out, "row", [edge])
    return entry


def other_first(value):
    return jnp.flip(pair(value), 0)


def ff_gather(w_out, w_gate, w_up, w_down):
    nx, nz, ny = [lax.axis_size(a) for a in CHIPS]
    rows = jnp.concatenate([w_out, w_gate.T, w_up.T, w_down], 0)
    part = rows.shape[1] // ny
    shard = lax.dynamic_slice_in_dim(rows, lax.axis_index("dp") * part, part, 1)
    blocks = lax.all_gather(shard, CHIPS, axis=0, tiled=True)
    hidden = rows.shape[0]
    z, y = lax.axis_index("row"), lax.axis_index("dp")
    if small_slice():
        blocks = blocks.reshape(nx, nz * ny, hidden, part)
        kz, ky = jnp.array(row_places() * ny), jnp.arange(nz * ny) // nz
        tables = jnp.stack([(z ^ kz) * ny + (y ^ ky), (y ^ ky) * nz + (z ^ kz)])
        return blocks, tables.astype(jnp.int32)
    blocks = blocks.reshape(nx, nz, ny, hidden, part)
    blocks = reorder(xor_turn(xor_turn(blocks, 1, z, nz), 2, y, ny), 1)
    blocks = blocks.transpose(0, 2, 1, 3, 4)
    blocks = blocks.reshape(nx, -1, HEAD // part, hidden, part).transpose(0, 1, 3, 2, 4)
    blocks = blocks.reshape(nx, -1, hidden, HEAD)
    same = jnp.arange(blocks.shape[1], dtype=jnp.int32)
    return blocks, jnp.stack([same, same])


def ff_scatter_xy(grads):
    nx, nz, ny = [lax.axis_size(a) for a in CHIPS]
    hidden = grads.shape[2]
    part = grads.shape[1] * HEAD // (nz * ny)
    if not small_slice():
        z, y = lax.axis_index("row"), lax.axis_index("dp")
        grads = grads.reshape(nx, -1, hidden, HEAD // part, part).transpose(0, 1, 3, 2, 4)
        grads = grads.reshape(nx, ny, nz, hidden, part)
        grads = xor_turn(xor_turn(reorder(grads, 2), 1, y, ny), 2, z, nz)
    grads = grads.reshape(-1, part)
    return lax.psum_scatter(grads, ("cx", "dp"), scatter_dimension=0, tiled=True)


def out_kernel(tables, side_of, y_ref, w_ref, own, send, w_all):
    tokens, width = own.shape[0], w_ref.shape[2]
    total = 0.0
    for i in range(w_ref.shape[0]):
        x = jnp.bitwise_xor(side_of[0], i)
        blocks = [w_ref[x, tables[0, p], :, :] for p in range(w_ref.shape[1])]
        w = jnp.concatenate(blocks, 1)
        at = slice(i * width, (i + 1) * width)
        w_all[at, :] = w
        total = total + nn(y_ref[:, at], w)
    own[...] = total[:tokens]
    send[...] = total[tokens:].astype(BF16)


def project_out(y, weights, tables):
    rows, width = y.shape
    nx, blocks, _, lane = weights.shape
    model = blocks * lane
    smem = pl.BlockSpec(memory_space=pltpu.SMEM)
    whole = lambda *shape: pl.BlockSpec(shape, lambda i: (0,) * len(shape))
    return pl.pallas_call(
        out_kernel,
        grid=(1,),
        in_specs=[smem, smem, whole(rows, width), whole(nx, blocks, width // nx, lane)],
        out_specs=[whole(rows // 2, model), whole(rows // 2, model), whole(width, model)],
        out_shape=[
            jax.ShapeDtypeStruct((rows // 2, model), F32),
            jax.ShapeDtypeStruct((rows // 2, model), BF16),
            jax.ShapeDtypeStruct((width, model), BF16),
        ],
        cost_estimate=pl.CostEstimate(
            flops=2 * rows * width * model, bytes_accessed=6 << 20, transcendentals=0
        ),
        name="project_out",
    )(tables, lax.axis_index("cx").reshape(1).astype(jnp.int32), y, weights)


def ff_kernel(tables, b0, b1, g0, g1, w_ref, out, out_send, db, db_send, grads, *scratch):
    m_all, d1_all, d2_all, out_acc, db_acc = scratch
    step = pl.program_id(0)
    blocks, hidden = w_ref.shape[1], grads.shape[2] // 3
    base = w_ref.shape[2] - grads.shape[2]
    tokens = out.shape[0]

    def weight(i):
        at = slice(base + i * hidden, base + (i + 1) * hidden)
        return jnp.concatenate([w_ref[0, tables[0, p], at, :] for p in range(blocks)], 1)

    gate_w, up_w, down_w = weight(0), weight(1), weight(2)
    for half in range(2):
        rows = slice(half * tokens, (half + 1) * tokens)
        b, g = (b1[...], g1[...]) if half else (b0[...], g0[...])
        z1, z2, dm = nt(b, gate_w), nt(b, up_w), nt(g, down_w)
        m, d1, d2 = (z1 * z2).astype(BF16), (dm * z2).astype(BF16), (dm * z1).astype(BF16)
        m_all[rows, :], d1_all[rows, :], d2_all[rows, :] = m, d1, d2
        sums = nn(m, down_w), nn(d1, gate_w) + nn(d2, up_w)
        kept = (out_acc, db_acc) if half else (out, db)

        @pl.when(step == 0)
        def _():
            for ref, value in zip(kept, sums):
                ref[...] = value

        @pl.when(step != 0)
        def _():
            sent = (out_send, db_send) if half else kept
            for to, ref, value in zip(sent, kept, sums):
                to[...] = (ref[...] + value).astype(to.dtype)

    for i, (left, own, other) in enumerate(((d1_all, b0, b1), (d2_all, b0, b1), (m_all, g0, g1))):
        grad = tn(left[:tokens, :], own[...]) + tn(left[tokens:, :], other[...])
        grad = grad.astype(BF16)
        at = slice(i * hidden, (i + 1) * hidden)
        for p in range(blocks):
            grads[0, tables[1, p], at, :] = grad[:, p * HEAD : (p + 1) * HEAD]


def feed_forward(b_own, b_pair, g_own, g_pair, weights, tables, hidden):
    tokens, model = b_own.shape
    rows = 2 * tokens
    nx, blocks, height, width = weights.shape
    once = pl.Buffered(1)
    fixed = lambda n: pl.BlockSpec((n, model), lambda x: (0, 0), pipeline_mode=once)
    turn = lambda n: pl.BlockSpec((1, blocks, n, width), lambda x: (x, 0, 0, 0))
    wide = jax.ShapeDtypeStruct((tokens, model), F32)
    narrow = jax.ShapeDtypeStruct((tokens, model), BF16)
    product = pltpu.VMEM((rows, hidden), BF16)
    total = pltpu.VMEM((tokens, model), F32)
    return pl.pallas_call(
        ff_kernel,
        grid=(nx,),
        in_specs=[pl.BlockSpec(memory_space=pltpu.SMEM)] + [fixed(tokens)] * 4 + [turn(height)],
        out_specs=[fixed(tokens)] * 4 + [turn(3 * hidden)],
        out_shape=[wide, narrow, wide, narrow]
        + [jax.ShapeDtypeStruct((nx, blocks, 3 * hidden, width), BF16)],
        scratch_shapes=[product] * 3 + [total] * 2,
        compiler_params=pltpu.CompilerParams(vmem_limit_bytes=60 << 20),
        cost_estimate=pl.CostEstimate(
            flops=18 * nx * rows * model * hidden, bytes_accessed=36 << 20, transcendentals=0
        ),
        name="feed_forward",
    )(tables, b_own, b_pair, g_own, g_pair, weights)


def on_device(
    block_input,
    segments,
    decay_rate,
    w_query,
    w_key,
    w_value,
    w_output_gate,
    w_out,
    w_gate,
    w_up,
    w_down,
    out_grad,
):
    nz = lax.axis_size("row")
    col = lax.axis_index(COL)
    place = lax.axis_index("row")
    tokens = block_input.shape[2]
    model = block_input.shape[3] * lax.axis_size(COL)
    wide = w_query.shape[1]

    wk, wv, sent = gather_weights(w_key, w_value)
    w_query, w_output_gate, _ = lax.optimization_barrier((w_query, w_output_gate, sent))
    wq, wu, _ = gather_weights(w_query, w_output_gate)
    gathered, tables = ff_gather(w_out, w_gate, w_up, w_down)

    x_own, a_own, r1 = tokens_in(block_input[:, 0], True)
    rates = jnp.concatenate([decay_rate, side(decay_rate)])
    heads = rates.shape[0]
    seg_all = segments[:, 0].astype(F32)
    seg = jnp.stack(
        [
            lax.dynamic_index_in_dim(seg_all, col, 0, False),
            lax.dynamic_index_in_dim(seg_all, col ^ 1, 0, False),
        ]
    )
    last = seg[:, tokens - 1]
    before = lax.ppermute(last, "row", [(i, i + 1) for i in range(nz - 1)])
    entry_seg = jnp.where(place == 0, -1.0, before)
    linked = ((seg[:, 0] == last) & (entry_seg == last)).astype(F32)
    factor = linked[:, None] * jnp.exp(-rates * tokens)[None]
    marks = jnp.stack([last, entry_seg], 1)
    seg_c, seg_r = seg[:, :, None], seg[:, None, :]
    heads_of = functools.partial(head_call, tokens=tokens, heads=heads)
    unit = 2 * heads * 2 * tokens * tokens * HEAD

    def both(own):
        return jnp.concatenate([own, pair(own)], 0)

    def back_sum(lefts, rights, form):
        def total(rows):
            out = dot(lefts[0][rows], rights[0], form)
            for left, right in zip(lefts[1:], rights[1:]):
                out = out + dot(left[rows], right, form)
            return out

        send = total(slice(tokens, None)).astype(BF16)
        return total(slice(0, tokens)) + pair(send).astype(F32), send

    a = both(a_own)
    zq, zk, zv, zu = [dot(a, w, "td,dc->tc") for w in (wq, wk, wv, wu)]
    zk, g_parts = lax.optimization_barrier((zk, out_grad[:, 0]))
    g_own = tokens_in(g_parts, False)
    g_pair = pair(g_own)
    k, v, local = heads_of(
        local_kernel,
        kinds_in="sscTT",
        kinds_out="ttp",
        args=(rates, marks, seg_c, zk, zv),
        flops=unit // 8,
        name="mixer_local",
    )
    q, o_inner = heads_of(
        inner_kernel,
        kinds_in="sscrTtt",
        kinds_out="tT",
        args=(rates, marks, seg_c, seg_r, zq, k, v),
        flops=unit,
        name="mixer_inner",
    )
    entry = chain(local, factor, False)
    entry, _, _ = lax.optimization_barrier((entry, g_own, g_pair))
    o, squares = heads_of(
        carry_kernel,
        kinds_in="sscTtp",
        kinds_out="Tn",
        args=(rates, marks, seg_c, o_inner, q, entry),
        flops=unit // 8,
        name="mixer_carry",
    )
    gate = jax.nn.sigmoid(zu)
    squares = squares.reshape(2, tokens)
    squares = (squares + other_first(squares)).reshape(2 * tokens, 1)
    r2 = lax.rsqrt(squares / model + EPS)
    y = (o * r2 * gate).astype(BF16)
    attended, attended_send, wo = project_out(y, gathered, tables)
    hres = x_own.astype(F32) + attended + pair(attended_send).astype(F32)
    r3 = lax.rsqrt(jnp.mean(hres * hres, 1, keepdims=True) + EPS)
    b = (hres * r3).astype(BF16)
    out, out_send, db, db_send, ff_grads = feed_forward(
        b, pair(b), g_own, g_pair, gathered, tables, w_down.shape[0]
    )
    db = db + pair(db_send).astype(F32)

    ff_part = ff_scatter_xy(ff_grads)
    dh = (
        g_own.astype(F32)
        + r3 * db
        - hres * (r3**3 * jnp.mean(db * hres, 1, keepdims=True))
    )
    dhr = both(dh.astype(BF16))

    grad_out = dot(dhr, y, "td,tc->dc").astype(BF16)
    dy = dot(dhr, wo, "td,cd->tc")
    dn = dy * gate
    dzu = (dy * o * r2 * gate * (1.0 - gate)).astype(BF16)
    dots = jnp.sum(dn * o, 1).reshape(2, tokens)
    dots = (dots + other_first(dots)).reshape(2 * tokens, 1)
    do = (r2 * dn - o * (r2**3 * dots / model)).astype(BF16)
    out_rows = (hres + out + pair(out_send).astype(F32)).astype(BF16)
    (d_entry,) = heads_of(
        entry_grad_kernel,
        kinds_in="ssctt",
        kinds_out="p",
        args=(rates, marks, seg_c, q, do),
        flops=unit // 8,
        name="mixer_entry_grad",
    )
    d_local = chain(d_entry, factor, True)
    dzq, dk, dv = heads_of(
        inner_grad_kernel,
        kinds_in="sscrttttpT",
        kinds_out="tTT",
        args=(rates, marks, seg_c, seg_r, q, k, v, do, entry, zq),
        flops=5 * unit // 2,
        name="mixer_inner_grad",
    )
    grad_u, grad_q = [dot(a, d, "td,tc->dc").astype(BF16) for d in (dzu, dzq)]
    cut = wide // 2
    early = [
        jnp.concatenate(
            [
                piece
                for x in (0, wide)
                for piece in (g[:, x : x + wide], grad_q[:, x + at : x + at + cut])
            ],
            1,
        )
        for g, at in ((grad_out, 0), (grad_u, cut))
    ]
    dzk, dzv = heads_of(
        last_grad_kernel,
        kinds_in="sscttpTTT",
        kinds_out="tt",
        args=(rates, marks, seg_c, k, v, d_local, zk, dk, dv),
        flops=unit // 4,
        name="mixer_last_grad",
    )
    grad_k, grad_v = [dot(a, d, "td,tc->dc").astype(BF16) for d in (dzk, dzv)]
    da, da_send = back_sum((dzq, dzk, dzv, dzu), (wq, wk, wv, wu), "tc,dc->td")
    x_wide = x_own.astype(F32)
    in_rows = (
        dh + r1 * da - x_wide * (r1**3 * jnp.mean(da * x_wide, 1, keepdims=True))
    ).astype(BF16)
    in_rows, ff_part = lax.optimization_barrier((in_rows, ff_part))
    divided = divide(in_rows)
    ready = divided[1]
    input_grad = tokens_out(divided)
    block_out = tokens_out(divide(held(out_rows, ready)))

    early = reduce_second(*reduce_first(*early, d_local), in_rows)
    early = fold(early, "row", ready, bits_of("row")[:1])
    total = fold(early, "row", None, bits_of("row")[1:])
    late = reduce_second(*reduce_first(grad_k, grad_v, ready))
    total_kv = fold(held(late, early), "row")
    total_q = jnp.concatenate([total[:, wide : wide + cut], total[:, 2 * wide + cut :]], 1)
    ff_total = lax.psum_scatter(ff_part, "row", scatter_dimension=0, tiled=True).astype(F32)
    hidden = w_down.shape[0]
    total_gate, total_up = ff_total[:hidden].T, ff_total[hidden : 2 * hidden].T
    return (
        block_out[:, None],
        input_grad[:, None],
        total_q,
        total_kv[:, :wide],
        total_kv[:, wide:],
        total[:, wide + cut : 2 * wide + cut],
        total[:, :wide].T,
        total_gate,
        total_up,
        ff_total[2 * hidden :],
    )


def solution(mesh):
    rows, cols, copies = [mesh.shape[a] for a in ("row", "col", "dp")]
    split = jax.sharding.Mesh(
        mesh.devices.reshape(rows, cols // 2, 2, copies), ("row", "cx", "cc", "dp")
    )
    placed = (
        P(None, "dp", "row", COL),
        P(None, "dp", "row"),
        P(COL),
        P("row", COL),
        P("row", COL),
        P("row", COL),
        P("row", COL),
        P(COL, "row"),
        P("row", COL),
        P("row", COL),
        P(COL, "row"),
        P(None, "dp", "row", COL),
    )
    return jax.shard_map(
        on_device,
        mesh=split,
        in_specs=placed,
        out_specs=(
            P(None, "dp", "row", COL),
            P(None, "dp", "row", COL),
            P(("row", "dp"), COL),
            P(("row", "dp"), COL),
            P(("row", "dp"), COL),
            P(("row", "dp"), COL),
            P(COL, ("row", "dp")),
            P(("row", "dp"), COL),
            P(("row", "dp"), COL),
            P(COL, ("row", "dp")),
        ),
        check_vma=False,
    )
```

```python
import functools

import jax
import jax.numpy as jnp
from jax import lax
from jax.experimental import pallas as pl
from jax.experimental.pallas import tpu as pltpu
from jax.sharding import PartitionSpec as P

HEAD = 128
TILE = 256
EPS = 1e-06
F32 = jnp.float32
BF16 = jnp.bfloat16


COL = ("cx", "cc")
CHIPS = ("cx", "row", "dp")


def swap(value, axis, bits):
    count = lax.axis_size(axis)
    return lax.ppermute(value, axis, [(i, i ^ bits) for i in range(count)])


def pair(value):
    return swap(value, COL, 1)


def side(value):
    return swap(value, COL, 2)


def bits_of(axis):
    return [1 << b for b in range(lax.axis_size(axis).bit_length() - 1)]


def row_places():
    count = lax.axis_size("row")
    places = [0]
    for bit in reversed(bits_of("row")):
        places = places + [p | bit for p in places]
    assert len(places) == count
    return places


def reorder(value, dim):
    take = lambda p: lax.slice_in_dim(value, p, p + 1, axis=dim)
    return jnp.concatenate([take(p) for p in row_places()], dim)


def xor_turn(value, dim, place, count):
    bit = 1
    while bit < count:
        shape = value.shape
        split = value.reshape(shape[:dim] + (count // (2 * bit), 2, bit) + shape[dim + 1 :])
        flipped = jnp.flip(split, dim + 1)
        value = jnp.where((place & bit) != 0, flipped, split).reshape(shape)
        bit *= 2
    return value


def to_order(rows):
    nz, ny = lax.axis_size("row"), lax.axis_size("dp")
    tokens, width = rows.shape
    split = rows.reshape(tokens, nz, ny, width // (nz * ny))
    split = xor_turn(split, 1, lax.axis_index("row"), nz)
    split = reorder(xor_turn(split, 2, lax.axis_index("dp"), ny), 1)
    return split.transpose(0, 2, 1, 3).reshape(tokens, width)


def from_order(rows):
    nz, ny = lax.axis_size("row"), lax.axis_size("dp")
    tokens, width = rows.shape
    split = rows.reshape(tokens, ny, nz, width // (nz * ny)).transpose(0, 2, 1, 3)
    split = reorder(split, 1)
    split = xor_turn(split, 1, lax.axis_index("row"), nz)
    split = xor_turn(split, 2, lax.axis_index("dp"), ny)
    return split.reshape(tokens, width)


def small_slice():
    return lax.axis_size("row") == 4 and lax.axis_size("dp") == 2


def place_bits():
    turn = lax.axis_index(COL) ^ lax.axis_index("row")
    return jnp.stack([turn & 1, turn >> 1, lax.axis_index("dp"), 0]).astype(jnp.int32)


def pick4(parts, low, high):
    first = [jnp.where(low, parts[k ^ 1], parts[k]) for k in range(4)]
    return [jnp.where(high, first[k ^ 2], first[k]) for k in range(4)]


def assemble_kernel(norm, places, bits, *refs):
    parts = [r[...].astype(F32) for r in refs[:4]]
    blocks = pick4(parts, bits[0] != 0, bits[1] != 0)
    odd = bits[2] != 0
    halves = [[], []]
    for b in blocks:
        low, high = b[:, :HEAD], b[:, HEAD:]
        halves[0].append(jnp.where(odd, high, low))
        halves[1].append(jnp.where(odd, low, high))
    rows = jnp.concatenate([half[k] for half in halves for k in places], 1)
    refs[4][...] = rows.astype(BF16)
    if norm:
        scale = lax.rsqrt(jnp.mean(rows * rows, 1, keepdims=True) + EPS)
        refs[5][...] = (rows * scale).astype(BF16)
        refs[6][...] = scale


def assemble(parts, norm):
    tokens, width = parts[0].shape
    model = 4 * width
    if not small_slice():
        col = lax.axis_index(COL)
        blocks = pick4(parts, (col & 1) != 0, (col & 2) != 0)
        rows = to_order(jnp.concatenate(blocks, 1))
        if not norm:
            return rows
        wide = rows.astype(F32)
        scale = lax.rsqrt(jnp.mean(wide * wide, 1, keepdims=True) + EPS)
        return rows, (wide * scale).astype(BF16), scale
    step = 128
    row = lambda n: pl.BlockSpec((step, n), lambda i: (i, 0))
    shape = [jax.ShapeDtypeStruct((tokens, model), BF16)]
    specs = [row(model)]
    if norm:
        shape += [shape[0], jax.ShapeDtypeStruct((tokens, 1), F32)]
        specs += [row(model), row(1)]
    out = pl.pallas_call(
        functools.partial(assemble_kernel, norm, row_places()),
        grid=(tokens // step,),
        in_specs=[pl.BlockSpec(memory_space=pltpu.SMEM)] + [row(width)] * 4,
        out_specs=specs,
        out_shape=shape,
        name="assemble",
    )(place_bits(), *parts)
    return out if norm else out[0]


def divide_kernel(places, bits, rows_ref, *refs):
    rows = rows_ref[...].astype(F32)
    odd = bits[2] != 0
    blocks = []
    for k in places:
        low = rows[:, k * HEAD : (k + 1) * HEAD]
        high = rows[:, (4 + k) * HEAD : (5 + k) * HEAD]
        blocks.append(
            jnp.concatenate([jnp.where(odd, high, low), jnp.where(odd, low, high)], 1)
        )
    parts = pick4(blocks, bits[0] != 0, bits[1] != 0)
    for ref, pieces in zip(refs, (parts[:2], parts[2:])):
        ref[...] = jnp.concatenate(pieces, 1).astype(BF16)


def divide(rows):
    tokens, model = rows.shape
    width = model // 4
    if not small_slice():
        col = lax.axis_index(COL)
        whole = from_order(rows)
        blocks = [whole[:, k * width : (k + 1) * width] for k in range(4)]
        parts = pick4(blocks, (col & 1) != 0, (col & 2) != 0)
        return jnp.concatenate(parts[:2], 1), jnp.concatenate(parts[2:], 1)
    step = 256
    row = lambda n: pl.BlockSpec((step, n), lambda i: (i, 0))
    return pl.pallas_call(
        functools.partial(divide_kernel, row_places()),
        grid=(tokens // step,),
        in_specs=[pl.BlockSpec(memory_space=pltpu.SMEM), row(model)],
        out_specs=[row(2 * width)] * 2,
        out_shape=[jax.ShapeDtypeStruct((tokens, 2 * width), BF16)] * 2,
        name="divide",
    )(place_bits(), rows)


def tokens_in(parts, norm):
    col = lax.axis_index(COL)
    got = []
    for bits in range(4):
        mine = lax.dynamic_index_in_dim(parts, col ^ bits, 0, False)
        got.append(mine if bits == 0 else swap(mine, COL, bits))
    return assemble(got, norm)


def tokens_out(divided):
    col = lax.axis_index(COL)
    near, far = divided
    width = near.shape[1] // 2
    far = side(far)
    mine = near[:, :width]
    near = pair(jnp.concatenate([near[:, width:], far[:, width:]], 1))
    got = [mine, near[:, :width], far[:, :width], near[:, width:]]
    return jnp.stack(pick4(got, (col & 1) != 0, (col & 2) != 0))


def gather_weights(first, second):
    ny = lax.axis_size("dp")
    part, width = first.shape[0] // ny, first.shape[1]
    value = jnp.concatenate([first, second], 1)
    value = lax.dynamic_slice_in_dim(value, lax.axis_index("dp") * part, part, 0)
    for bit in reversed(bits_of("row")):
        value = jnp.concatenate([value, swap(value, "row", bit)], 0)
    one, two = value[:, :width], value[:, width:]
    one = jnp.concatenate([one, side(one)], 1)
    for bit in bits_of("dp"):
        two = jnp.concatenate([two, swap(two, "dp", bit)], 0)
        one = jnp.concatenate([one, swap(one, "dp", bit)], 0)
    return one, jnp.concatenate([two, side(two)], 1), value


def held(value, after):
    return value if after is None else lax.optimization_barrier((value, after))[0]


def fold(value, axis, after=None, bits=None):
    if bits is None:
        bits = bits_of(axis) if axis == "row" else reversed(bits_of(axis))
    for bit in bits:
        half = value.shape[0] // 2
        got = held(swap(value[half:].astype(BF16), axis, bit), after)
        value = value[:half].astype(F32) + got.astype(F32)
    return value


def fold_side(value, after=None):
    half = value.shape[1] // 2
    got = held(side(value[:, half:].astype(BF16)), after)
    return value[:, :half].astype(F32) + got.astype(F32)


def reduce_first(one, two, after):
    return fold_side(one, after), fold(two, "dp", after)


def reduce_second(one, two, after=None):
    return jnp.concatenate([fold(one, "dp", after), fold_side(two, after)], 1)


def dot(left, right, form):
    return jnp.einsum(form, left, right, preferred_element_type=F32)


def nn(a, b):
    return jnp.dot(a, b, preferred_element_type=F32)


def nt(a, b):
    return lax.dot_general(a, b, (((1,), (1,)), ((), ())), preferred_element_type=F32)


def tn(a, b):
    return lax.dot_general(a, b, (((0,), (0,)), ((), ())), preferred_element_type=F32)


def silu_slope(pre):
    logistic = jax.nn.sigmoid(pre)
    return logistic * (1.0 + pre * (1.0 - logistic))


def tile_decay(rate, seg_col, seg_row, at, width):
    rows = seg_col.shape[0]
    shape = (rows, width)
    gap = lax.broadcasted_iota(jnp.int32, shape, 0) + at - lax.broadcasted_iota(jnp.int32, shape, 1)
    visible = (gap >= 0) & (seg_col == seg_row)
    return jnp.where(visible, jnp.exp(-rate * jnp.maximum(gap, 0).astype(F32)), 0.0)


def column(tokens):
    return lax.broadcasted_iota(jnp.int32, (tokens, 1), 0).astype(F32)


def own_weight(rate, seg_col, last):
    tokens = seg_col.shape[0]
    return jnp.where(seg_col == last, jnp.exp(-rate * (tokens - 1.0 - column(tokens))), 0.0)


def entry_weight(rate, seg_col, entry_seg):
    tokens = seg_col.shape[0]
    return jnp.where(seg_col == entry_seg, jnp.exp(-rate * (column(tokens) + 1.0)), 0.0)


def lanes(head):
    return slice(head * HEAD, (head + 1) * HEAD)


def local_kernel(rates, marks, seg_c, zk, zv, k_out, v_out, state):
    last = marks[pl.program_id(0), 0]
    for head in range(state.shape[1]):
        at = lanes(head)
        pre = zk[:, at]
        k, v = (pre * jax.nn.sigmoid(pre)).astype(BF16), zv[:, at].astype(BF16)
        k_out[:, at], v_out[:, at] = k, v
        weight = own_weight(rates[head], seg_c[0], last)
        state[0, head] = tn((k.astype(F32) * weight).astype(BF16), v)


def inner_kernel(rates, marks, seg_c, seg_r, zq, k_ref, v_ref, q_out, o_out):
    seg, tokens = seg_c[0], seg_c.shape[1]
    for head in range(zq.shape[1] // HEAD):
        at = lanes(head)
        pre = zq[:, at]
        q_out[:, at] = (pre * jax.nn.sigmoid(pre)).astype(BF16)
        for top in range(0, tokens, TILE):
            width = top + TILE
            decay = tile_decay(rates[head], seg[top:width], seg_r[0, :, :width], top, width)
            mix = (nt(q_out[top:width, at], k_ref[:width, at]) * decay).astype(BF16)
            o_out[top:width, at] = nn(mix, v_ref[:width, at])


def carry_kernel(rates, marks, seg_c, o_in, q, entry, o_out, squares):
    before = marks[pl.program_id(0), 1]
    total = 0.0
    for head in range(entry.shape[1]):
        at = lanes(head)
        weight = entry_weight(rates[head], seg_c[0], before)
        o = o_in[:, at] + weight * nn(q[:, at], entry[0, head])
        o_out[:, at] = o
        total = total + o * o
    squares[...] = jnp.sum(total, 1, keepdims=True)


def entry_grad_kernel(rates, marks, seg_c, q, do, grad):
    before = marks[pl.program_id(0), 1]
    for head in range(grad.shape[1]):
        at = lanes(head)
        weight = entry_weight(rates[head], seg_c[0], before)
        grad[0, head] = tn(q[:, at], (do[:, at].astype(F32) * weight).astype(BF16))


def inner_grad_kernel(
    rates, marks, seg_c, seg_r, q_ref, k_ref, v_ref, do_ref, entry, zq, dzq, dk, dv
):
    before = marks[pl.program_id(0), 1]
    seg, tokens = seg_c[0], seg_c.shape[1]
    for head in range(entry.shape[1]):
        at = lanes(head)
        weight = entry_weight(rates[head], seg, before)
        for top in range(0, tokens, TILE):
            width = top + TILE
            q, do = q_ref[top:width, at], do_ref[top:width, at]
            k, v = k_ref[:width, at], v_ref[:width, at]
            decay = tile_decay(rates[head], seg[top:width], seg_r[0, :, :width], top, width)
            mix = (nt(q, k) * decay).astype(BF16)
            ds = (nt(do, v) * decay).astype(BF16)
            scaled = (do.astype(F32) * weight[top:width]).astype(BF16)
            dq = nn(ds, k) + nt(scaled, entry[0, head])
            dzq[top:width, at] = (dq * silu_slope(zq[top:width, at])).astype(BF16)
            dk_new, dv_new = tn(ds, q), tn(mix, do)
            if top:
                dk[:top, at] += dk_new[:top]
                dv[:top, at] += dv_new[:top]
            dk[top:width, at] = dk_new[top:]
            dv[top:width, at] = dv_new[top:]


def last_grad_kernel(rates, marks, seg_c, k, v, d_state, zk, dk, dv, dzk, dzv):
    last = marks[pl.program_id(0), 0]
    for head in range(d_state.shape[1]):
        at = lanes(head)
        weight = own_weight(rates[head], seg_c[0], last)
        state = d_state[0, head]
        dk_all = dk[:, at] + weight * nt(v[:, at], state)
        dzk[:, at] = (dk_all * silu_slope(zk[:, at])).astype(BF16)
        scaled = (k[:, at].astype(F32) * weight).astype(BF16)
        dzv[:, at] = (dv[:, at] + nn(scaled, state)).astype(BF16)


def head_call(kernel, tokens, heads, kinds_in, kinds_out, args, flops, name):
    specs = {
        "s": pl.BlockSpec(memory_space=pltpu.SMEM),
        "c": pl.BlockSpec((1, tokens, 1), lambda b: (b, 0, 0)),
        "r": pl.BlockSpec((1, 1, tokens), lambda b: (b, 0, 0)),
        "t": pl.BlockSpec((tokens, heads * HEAD), lambda b: (b, 0)),
        "p": pl.BlockSpec((1, heads, HEAD, HEAD), lambda b: (b, 0, 0, 0)),
        "n": pl.BlockSpec((tokens, 1), lambda b: (b, 0)),
    }
    shapes = {
        "T": jax.ShapeDtypeStruct((2 * tokens, heads * HEAD), F32),
        "t": jax.ShapeDtypeStruct((2 * tokens, heads * HEAD), BF16),
        "p": jax.ShapeDtypeStruct((2, heads, HEAD, HEAD), F32),
        "n": jax.ShapeDtypeStruct((2 * tokens, 1), F32),
    }
    return pl.pallas_call(
        kernel,
        grid=(2,),
        in_specs=[specs[k.lower()] for k in kinds_in],
        out_specs=[specs[k.lower()] for k in kinds_out],
        out_shape=[shapes[k] for k in kinds_out],
        cost_estimate=pl.CostEstimate(flops=flops, bytes_accessed=8 << 20, transcendentals=0),
        name=name,
    )(*args)


def chain(local, factor, reverse):
    count = lax.axis_size("row")
    entry, sent = jnp.zeros(local.shape, BF16), []
    for hop in range(count - 1):
        out = (local + factor[:, :, None, None] * entry.astype(F32)).astype(BF16)
        sent.append(out)
        edge = (count - 1 - hop, count - 2 - hop) if reverse else (hop, hop + 1)
        entry = entry + lax.ppermute(out, "row", [edge])
    return entry, sent


def other_first(value):
    return jnp.flip(pair(value), 0)


def ff_gather(w_out, w_gate, w_up, w_down):
    nx, nz, ny = [lax.axis_size(a) for a in CHIPS]
    rows = jnp.concatenate([w_out, w_gate.T, w_up.T, w_down], 0)
    part = rows.shape[1] // ny
    shard = lax.dynamic_slice_in_dim(rows, lax.axis_index("dp") * part, part, 1)
    blocks = lax.all_gather(shard, CHIPS, axis=0, tiled=True)
    hidden = rows.shape[0]
    z, y = lax.axis_index("row"), lax.axis_index("dp")
    if small_slice():
        blocks = blocks.reshape(nx, nz * ny, hidden, part)
        kz, ky = jnp.array(row_places() * ny), jnp.arange(nz * ny) // nz
        tables = jnp.stack([(z ^ kz) * ny + (y ^ ky), (y ^ ky) * nz + (z ^ kz)])
        return blocks, tables.astype(jnp.int32)
    blocks = blocks.reshape(nx, nz, ny, hidden, part)
    blocks = reorder(xor_turn(xor_turn(blocks, 1, z, nz), 2, y, ny), 1)
    blocks = blocks.transpose(0, 2, 1, 3, 4)
    blocks = blocks.reshape(nx, -1, HEAD // part, hidden, part).transpose(0, 1, 3, 2, 4)
    blocks = blocks.reshape(nx, -1, hidden, HEAD)
    same = jnp.arange(blocks.shape[1], dtype=jnp.int32)
    return blocks, jnp.stack([same, same])


def ff_scatter_xy(grads):
    nx, nz, ny = [lax.axis_size(a) for a in CHIPS]
    hidden = grads.shape[2]
    part = grads.shape[1] * HEAD // (nz * ny)
    if not small_slice():
        z, y = lax.axis_index("row"), lax.axis_index("dp")
        grads = grads.reshape(nx, -1, hidden, HEAD // part, part).transpose(0, 1, 3, 2, 4)
        grads = grads.reshape(nx, ny, nz, hidden, part)
        grads = xor_turn(xor_turn(reorder(grads, 2), 1, y, ny), 2, z, nz)
    grads = grads.reshape(-1, part)
    return lax.psum_scatter(grads, ("cx", "dp"), scatter_dimension=0, tiled=True)


def out_kernel(tables, side_of, y_ref, w_ref, own, send, w_all):
    tokens, width = own.shape[0], w_ref.shape[2]
    total = 0.0
    for i in range(w_ref.shape[0]):
        x = jnp.bitwise_xor(side_of[0], i)
        blocks = [w_ref[x, tables[0, p], :, :] for p in range(w_ref.shape[1])]
        w = jnp.concatenate(blocks, 1)
        at = slice(i * width, (i + 1) * width)
        w_all[at, :] = w
        total = total + nn(y_ref[:, at], w)
    own[...] = total[:tokens]
    send[...] = total[tokens:].astype(BF16)


def project_out(y, weights, tables):
    rows, width = y.shape
    nx, blocks, _, lane = weights.shape
    model = blocks * lane
    smem = pl.BlockSpec(memory_space=pltpu.SMEM)
    whole = lambda *shape: pl.BlockSpec(shape, lambda i: (0,) * len(shape))
    return pl.pallas_call(
        out_kernel,
        grid=(1,),
        in_specs=[smem, smem, whole(rows, width), whole(nx, blocks, width // nx, lane)],
        out_specs=[whole(rows // 2, model), whole(rows // 2, model), whole(width, model)],
        out_shape=[
            jax.ShapeDtypeStruct((rows // 2, model), F32),
            jax.ShapeDtypeStruct((rows // 2, model), BF16),
            jax.ShapeDtypeStruct((width, model), BF16),
        ],
        cost_estimate=pl.CostEstimate(
            flops=2 * rows * width * model, bytes_accessed=6 << 20, transcendentals=0
        ),
        name="project_out",
    )(tables, lax.axis_index("cx").reshape(1).astype(jnp.int32), y, weights)


def ff_kernel(tables, b0, b1, g0, g1, w_ref, out, out_send, db, db_send, grads, *scratch):
    m_all, d1_all, d2_all, out_acc, db_acc = scratch
    step = pl.program_id(0)
    blocks, hidden = w_ref.shape[1], grads.shape[2] // 3
    base = w_ref.shape[2] - grads.shape[2]
    tokens = out.shape[0]

    def weight(i):
        at = slice(base + i * hidden, base + (i + 1) * hidden)
        return jnp.concatenate([w_ref[0, tables[0, p], at, :] for p in range(blocks)], 1)

    gate_w, up_w, down_w = weight(0), weight(1), weight(2)
    for half in range(2):
        rows = slice(half * tokens, (half + 1) * tokens)
        b, g = (b1[...], g1[...]) if half else (b0[...], g0[...])
        z1, z2, dm = nt(b, gate_w), nt(b, up_w), nt(g, down_w)
        m, d1, d2 = (z1 * z2).astype(BF16), (dm * z2).astype(BF16), (dm * z1).astype(BF16)
        m_all[rows, :], d1_all[rows, :], d2_all[rows, :] = m, d1, d2
        sums = nn(m, down_w), nn(d1, gate_w) + nn(d2, up_w)
        kept = (out_acc, db_acc) if half else (out, db)

        @pl.when(step == 0)
        def _():
            for ref, value in zip(kept, sums):
                ref[...] = value

        @pl.when(step != 0)
        def _():
            sent = (out_send, db_send) if half else kept
            for to, ref, value in zip(sent, kept, sums):
                to[...] = (ref[...] + value).astype(to.dtype)

    for i, (left, own, other) in enumerate(((d1_all, b0, b1), (d2_all, b0, b1), (m_all, g0, g1))):
        grad = tn(left[:tokens, :], own[...]) + tn(left[tokens:, :], other[...])
        grad = grad.astype(BF16)
        at = slice(i * hidden, (i + 1) * hidden)
        for p in range(blocks):
            grads[0, tables[1, p], at, :] = grad[:, p * HEAD : (p + 1) * HEAD]


def feed_forward(b_own, b_pair, g_own, g_pair, weights, tables, hidden):
    tokens, model = b_own.shape
    rows = 2 * tokens
    nx, blocks, height, width = weights.shape
    once = pl.Buffered(1)
    fixed = lambda n: pl.BlockSpec((n, model), lambda x: (0, 0), pipeline_mode=once)
    turn = lambda n: pl.BlockSpec((1, blocks, n, width), lambda x: (x, 0, 0, 0))
    wide = jax.ShapeDtypeStruct((tokens, model), F32)
    narrow = jax.ShapeDtypeStruct((tokens, model), BF16)
    product = pltpu.VMEM((rows, hidden), BF16)
    total = pltpu.VMEM((tokens, model), F32)
    return pl.pallas_call(
        ff_kernel,
        grid=(nx,),
        in_specs=[pl.BlockSpec(memory_space=pltpu.SMEM)] + [fixed(tokens)] * 4 + [turn(height)],
        out_specs=[fixed(tokens)] * 4 + [turn(3 * hidden)],
        out_shape=[wide, narrow, wide, narrow]
        + [jax.ShapeDtypeStruct((nx, blocks, 3 * hidden, width), BF16)],
        scratch_shapes=[product] * 3 + [total] * 2,
        compiler_params=pltpu.CompilerParams(vmem_limit_bytes=60 << 20),
        cost_estimate=pl.CostEstimate(
            flops=18 * nx * rows * model * hidden, bytes_accessed=36 << 20, transcendentals=0
        ),
        name="feed_forward",
    )(tables, b_own, b_pair, g_own, g_pair, weights)


def on_device(
    block_input,
    segments,
    decay_rate,
    w_query,
    w_key,
    w_value,
    w_output_gate,
    w_out,
    w_gate,
    w_up,
    w_down,
    out_grad,
):
    nz = lax.axis_size("row")
    col = lax.axis_index(COL)
    place = lax.axis_index("row")
    tokens = block_input.shape[2]
    model = block_input.shape[3] * lax.axis_size(COL)
    wide = w_query.shape[1]

    wk, wv, sent = gather_weights(w_key, w_value)
    w_query, w_output_gate, _ = lax.optimization_barrier((w_query, w_output_gate, sent))
    wq, wu, _ = gather_weights(w_query, w_output_gate)
    gathered, tables = ff_gather(w_out, w_gate, w_up, w_down)

    x_own, a_own, r1 = tokens_in(block_input[:, 0], True)
    rates = jnp.concatenate([decay_rate, side(decay_rate)])
    heads = rates.shape[0]
    seg_all = segments[:, 0].astype(F32)
    seg = jnp.stack(
        [
            lax.dynamic_index_in_dim(seg_all, col, 0, False),
            lax.dynamic_index_in_dim(seg_all, col ^ 1, 0, False),
        ]
    )
    last = seg[:, tokens - 1]
    before = lax.ppermute(last, "row", [(i, i + 1) for i in range(nz - 1)])
    entry_seg = jnp.where(place == 0, -1.0, before)
    linked = ((seg[:, 0] == last) & (entry_seg == last)).astype(F32)
    factor = linked[:, None] * jnp.exp(-rates * tokens)[None]
    marks = jnp.stack([last, entry_seg], 1)
    seg_c, seg_r = seg[:, :, None], seg[:, None, :]
    heads_of = functools.partial(head_call, tokens=tokens, heads=heads)
    unit = 2 * heads * 2 * tokens * tokens * HEAD

    def both(own):
        return jnp.concatenate([own, pair(own)], 0)

    def back_sum(lefts, rights, form):
        def total(rows):
            out = dot(lefts[0][rows], rights[0], form)
            for left, right in zip(lefts[1:], rights[1:]):
                out = out + dot(left[rows], right, form)
            return out

        send = total(slice(tokens, None)).astype(BF16)
        return total(slice(0, tokens)) + pair(send).astype(F32), send

    a = both(a_own)
    zq, zk, zv, zu = [dot(a, w, "td,dc->tc") for w in (wq, wk, wv, wu)]
    zk, g_parts = lax.optimization_barrier((zk, out_grad[:, 0]))
    g_own = tokens_in(g_parts, False)
    g_pair = pair(g_own)
    k, v, local = heads_of(
        local_kernel,
        kinds_in="sscTT",
        kinds_out="ttp",
        args=(rates, marks, seg_c, zk, zv),
        flops=unit // 8,
        name="mixer_local",
    )
    q, o_inner = heads_of(
        inner_kernel,
        kinds_in="sscrTtt",
        kinds_out="tT",
        args=(rates, marks, seg_c, seg_r, zq, k, v),
        flops=unit,
        name="mixer_inner",
    )
    entry, _ = chain(local, factor, False)
    entry, _, _ = lax.optimization_barrier((entry, g_own, g_pair))
    o, squares = heads_of(
        carry_kernel,
        kinds_in="sscTtp",
        kinds_out="Tn",
        args=(rates, marks, seg_c, o_inner, q, entry),
        flops=unit // 8,
        name="mixer_carry",
    )
    gate = jax.nn.sigmoid(zu)
    squares = squares.reshape(2, tokens)
    squares = (squares + other_first(squares)).reshape(2 * tokens, 1)
    r2 = lax.rsqrt(squares / model + EPS)
    y = (o * r2 * gate).astype(BF16)
    attended, attended_send, wo = project_out(y, gathered, tables)
    hres = x_own.astype(F32) + attended + pair(attended_send).astype(F32)
    r3 = lax.rsqrt(jnp.mean(hres * hres, 1, keepdims=True) + EPS)
    b = (hres * r3).astype(BF16)
    out, out_send, db, db_send, ff_grads = feed_forward(
        b, pair(b), g_own, g_pair, gathered, tables, w_down.shape[0]
    )
    db = db + pair(db_send).astype(F32)

    ff_part = ff_scatter_xy(ff_grads)
    dh = (
        g_own.astype(F32)
        + r3 * db
        - hres * (r3**3 * jnp.mean(db * hres, 1, keepdims=True))
    )
    dhr = both(dh.astype(BF16))

    dy = dot(dhr, wo, "td,cd->tc")
    dn = dy * gate
    dzu = (dy * o * r2 * gate * (1.0 - gate)).astype(BF16)
    dots = jnp.sum(dn * o, 1).reshape(2, tokens)
    dots = (dots + other_first(dots)).reshape(2 * tokens, 1)
    do = (r2 * dn - o * (r2**3 * dots / model)).astype(BF16)
    out_rows = (hres + out + pair(out_send).astype(F32)).astype(BF16)
    (d_entry,) = heads_of(
        entry_grad_kernel,
        kinds_in="ssctt",
        kinds_out="p",
        args=(rates, marks, seg_c, q, do),
        flops=unit // 8,
        name="mixer_entry_grad",
    )
    d_local, sent = chain(d_entry, factor, True)
    dzq, dk, dv = heads_of(
        inner_grad_kernel,
        kinds_in="sscrttttpT",
        kinds_out="tTT",
        args=(rates, marks, seg_c, seg_r, q, k, v, do, entry, zq),
        flops=5 * unit // 2,
        name="mixer_inner_grad",
    )
    dzq, dhr, dzu_first, _ = lax.optimization_barrier((dzq, dhr, dzu, sent[1]))
    grad_out = dot(dhr, y, "td,tc->dc").astype(BF16)
    grad_u, grad_q = [dot(a, d, "td,tc->dc").astype(BF16) for d in (dzu_first, dzq)]
    dzq, dzu, _ = lax.optimization_barrier((dzq, dzu, sent[2]))
    cut = wide // 2
    early = [
        jnp.concatenate(
            [
                piece
                for x in (0, wide)
                for piece in (g[:, x : x + wide], grad_q[:, x + at : x + at + cut])
            ],
            1,
        )
        for g, at in ((grad_out, 0), (grad_u, cut))
    ]
    dzk, dzv = heads_of(
        last_grad_kernel,
        kinds_in="sscttpTTT",
        kinds_out="tt",
        args=(rates, marks, seg_c, k, v, d_local, zk, dk, dv),
        flops=unit // 4,
        name="mixer_last_grad",
    )
    grad_k, grad_v = [dot(a, d, "td,tc->dc").astype(BF16) for d in (dzk, dzv)]
    da, da_send = back_sum((dzq, dzk, dzv, dzu), (wq, wk, wv, wu), "tc,dc->td")
    x_wide = x_own.astype(F32)
    in_rows = (
        dh + r1 * da - x_wide * (r1**3 * jnp.mean(da * x_wide, 1, keepdims=True))
    ).astype(BF16)
    in_rows, ff_part = lax.optimization_barrier((in_rows, ff_part))
    divided = divide(in_rows)
    ready = divided[1]
    input_grad = tokens_out(divided)
    block_out = tokens_out(divide(held(out_rows, ready)))

    early = reduce_second(*reduce_first(*early, d_local), in_rows)
    early = fold(early, "row", ready, bits_of("row")[:1])
    total = fold(early, "row", None, bits_of("row")[1:])
    late = reduce_second(*reduce_first(grad_k, grad_v, ready))
    total_kv = fold(held(late, early), "row")
    total_q = jnp.concatenate([total[:, wide : wide + cut], total[:, 2 * wide + cut :]], 1)
    ff_total = lax.psum_scatter(ff_part, "row", scatter_dimension=0, tiled=True).astype(F32)
    hidden = w_down.shape[0]
    total_gate, total_up = ff_total[:hidden].T, ff_total[hidden : 2 * hidden].T
    return (
        block_out[:, None],
        input_grad[:, None],
        total_q,
        total_kv[:, :wide],
        total_kv[:, wide:],
        total[:, wide + cut : 2 * wide + cut],
        total[:, :wide].T,
        total_gate,
        total_up,
        ff_total[2 * hidden :],
    )


def solution(mesh):
    rows, cols, copies = [mesh.shape[a] for a in ("row", "col", "dp")]
    split = jax.sharding.Mesh(
        mesh.devices.reshape(rows, cols // 2, 2, copies), ("row", "cx", "cc", "dp")
    )
    placed = (
        P(None, "dp", "row", COL),
        P(None, "dp", "row"),
        P(COL),
        P("row", COL),
        P("row", COL),
        P("row", COL),
        P("row", COL),
        P(COL, "row"),
        P("row", COL),
        P("row", COL),
        P(COL, "row"),
        P(None, "dp", "row", COL),
    )
    return jax.shard_map(
        on_device,
        mesh=split,
        in_specs=placed,
        out_specs=(
            P(None, "dp", "row", COL),
            P(None, "dp", "row", COL),
            P(("row", "dp"), COL),
            P(("row", "dp"), COL),
            P(("row", "dp"), COL),
            P(("row", "dp"), COL),
            P(COL, ("row", "dp")),
            P(("row", "dp"), COL),
            P(("row", "dp"), COL),
            P(COL, ("row", "dp")),
        ),
        check_vma=False,
    )
```
